256 devices in a mesh: seq: 32 (over y, z), head: 8 (over x, core).
Axes of the slice: x: 4, y: 4, z: 8, core: 2. Of those that a mesh axis runs over, the one named last changes fastest.
Arguments:
- new_query: bfloat16 [96, 4, 4096], P(None, None, 'head'), may hold values from -40 to 40
- fresh_key_value: bfloat16 [96, 4, 8, 128], P('seq', None, 'head'), may hold values from -24 to 24
- prompt_cache: bfloat16 [8, 32768, 8, 128], P(None, 'seq', 'head'), may hold values from -30 to 30
- decoded_tail_cache: bfloat16 [96, 1024, 8, 128], P(None, 'seq', 'head'), may hold values from -6 to 6
- sinks: float32 [64], P('head'), may hold values from 2 to 14
- prompt_group: int32 [96], replicated, may hold values from 0 to 7, as said below
- prompt_lens: int32 [8], replicated, may hold values from 1 to 32768
- tail_lens: int32 [96], replicated, may hold values from 0 to 1024
- o_weight: bfloat16 [4096, 2880], P('head'), may hold values from -0.09375 to 0.09375
- resid: bfloat16 [96, 4, 2880], P('seq'), may hold values from -1.796875 to 1.796875
- norm_gain: float32 [2880], replicated, may hold values from 0.3 to 3
- expert_ids: int32 [96, 4, 4], replicated, may hold values from 0 to 31, all different within a row; in each aligned block of 12 rows (0 to 11, 12 to 23, ..., all dimensions but the last counted through in order) at most 3 rows name the same one
- route_weights: float32 [96, 4, 4], P('seq'), may hold values from 0.05 to 0.6
- gate_up: bfloat16 [32, 2880, 2, 2880], P('seq', None, None, 'head'), may hold values from -0.3125 to 0.3125
- down_weight: bfloat16 [32, 2880, 2880], P('seq', 'head'), may hold values from -0.0390625 to 0.0390625
Outputs:
- output: bfloat16 [96, 4, 2880], P('seq')
The draws below stay inside these ranges and needn't reach their ends.
Inputs may be any that keep to these rules, and one draw needn't show every extreme that they name: `prompt_group`: each of the 8 groups holds exactly 12 requests. `expert_ids`: a token's 4 picks are distinct; among the 12 tokens of the requests s * 3 to (s + 1) * 3 - 1 no expert is picked more than 3 times.
All inputs are finite; a program needn't handle non-finite values.
Results may differ from the reference program's by a relative error of at most 0.025.
Values may be sent and summed in bfloat16 or wider, within the bound.
A program may use at most 128 MiB of HBM per device.

```python
import math
import jax
import jax.numpy as jnp
import numpy as np
from jax import lax

D = 2880
QUERY_HEADS = 64
KEY_VALUE_HEADS = 8
HEAD_SIZE = 64
FF = 2880
TOP = 4
PROMPT_GROUPS = 8
GREQ = 12
DECODE_STEPS = 4
EXPERTS = 32
REQUEST_COUNT = 96
TOK_DEV = 12
PROMPT_LENGTH = 32768
TAIL_LENGTH = 1024
MOST = 3
N_SEQ = 32


def draw_prompt_group(key, part):
    shuffled = jax.random.permutation(key, REQUEST_COUNT)
    return (shuffled // GREQ).astype(jnp.int32)


def bounded_lengths(key, count, lowest, highest):
    first_key, second_key = jax.random.split(key)
    lengths = jax.random.randint(first_key, (count,), lowest, highest + 1)
    chosen = jax.random.randint(second_key, (), 0, count)
    return jnp.where(jnp.arange(count) == chosen, highest, lengths).astype(jnp.int32)


def draw_prompt_lens(key, part):
    return bounded_lengths(key, PROMPT_GROUPS, 1, PROMPT_LENGTH)


def draw_tail_lens(key, part):
    return bounded_lengths(key, REQUEST_COUNT, 0, TAIL_LENGTH)


def draw_prompt_cache(key, part):
    subkeys = jax.random.split(key, 1)
    complete_shape = (PROMPT_GROUPS, PROMPT_LENGTH, KEY_VALUE_HEADS, 2 * HEAD_SIZE)
    result = jnp.clip(jax.random.normal(subkeys[0], complete_shape, jnp.float32), -6.0, 6.0)
    return result.astype(jnp.bfloat16)


def query_field(key):
    subkeys = jax.random.split(key, 1)
    complete_shape = (REQUEST_COUNT, DECODE_STEPS, QUERY_HEADS, HEAD_SIZE)
    result = 2.5 * jnp.clip(jax.random.normal(subkeys[0], complete_shape, jnp.float32), -6.0, 6.0)
    return result


def draw_new_query(key, part):
    result = query_field(key)
    return result.reshape(REQUEST_COUNT, DECODE_STEPS, QUERY_HEADS * HEAD_SIZE).astype(jnp.bfloat16)


def draw_fresh_key_value(key, part):
    group_width = QUERY_HEADS // KEY_VALUE_HEADS
    queries = query_field(key).astype(jnp.bfloat16).astype(jnp.float32)
    queries = queries.reshape(REQUEST_COUNT, DECODE_STEPS, KEY_VALUE_HEADS, group_width, HEAD_SIZE)
    mean_query = jnp.mean(queries, axis=3)
    strength = (math.log(PROMPT_LENGTH) + 1.0) / 6.25
    lead = strength * group_width / math.sqrt(HEAD_SIZE)
    own_keys = jax.random.fold_in(key, 811)
    noise_key, value_key = jax.random.split(own_keys)
    half_shape = (REQUEST_COUNT, DECODE_STEPS, KEY_VALUE_HEADS, HEAD_SIZE)
    noise = 0.5 * jnp.clip(jax.random.normal(noise_key, half_shape, jnp.float32), -6.0, 6.0)
    values = jnp.clip(jax.random.normal(value_key, half_shape, jnp.float32), -6.0, 6.0)
    keys = jnp.clip(lead * mean_query + noise, -24.0, 24.0)
    return jnp.concatenate([keys, values], axis=-1).astype(jnp.bfloat16)


def shard_levels(rng, shape, pieces, least, top_value):
    def one(axis_at, blocks):
        steps = jax.random.uniform(jax.random.fold_in(jax.random.fold_in(rng, 6), axis_at), (blocks,), jnp.float32, least / len(pieces), top_value / len(pieces))
        return jnp.repeat(jnp.exp(steps), shape[axis_at] // blocks).reshape((-1,) + (1,) * (len(shape) - axis_at - 1))

    loudness = one(*pieces[0])
    for cut in pieces[1:]:
        loudness = loudness * one(*cut)
    return loudness


def shared_out(key, own, number, rows, amount, top, limit, lean):
    ranking = jax.random.permutation(key, amount)
    heavy_load, usual = shares(amount, rows * top, limit, lean, True), shares(amount, rows * top, limit, lean, False)
    places = jnp.arange(amount)

    def named(sizes, offset_by):
        used = int((sizes > 0).sum())
        fixed = max(1, used // 4)
        passed = fixed + (places - fixed + offset_by * (used - fixed)) % max(1, amount - fixed)
        return jnp.zeros((amount,), jnp.int32).at[ranking[jnp.where(places < fixed, places, passed)]].set(jnp.asarray(sizes, jnp.int32))

    sizes = jnp.where(number % 4 == 0, named(heavy_load, number // 4), named(usual, number - number // 4 - 1))
    mixed = jax.random.permutation(jax.random.fold_in(own, 3), amount)
    source_of, taker = mixed[0:amount // 2 * 2:2], mixed[1:amount // 2 * 2:2]
    room = jnp.minimum(sizes[source_of] - 1, limit - sizes[taker]) // 2
    room = jnp.where((source_of == ranking[0]) | (taker == ranking[0]) | (sizes[taker] == 0), 0, jnp.maximum(room, 0))
    passed = jax.random.randint(jax.random.fold_in(own, 4), (amount // 2,), 0, 1 << 20) % (room + 1)
    sizes = sizes.at[source_of].add(-passed).at[taker].add(passed)
    items = jnp.searchsorted(jnp.cumsum(sizes), jnp.arange(rows * top), side="right").astype(jnp.int32)
    listing = items.reshape(top, rows).T
    listing = listing[jax.random.permutation(jax.random.fold_in(own, 1), rows)]
    offset_by = jax.random.randint(jax.random.fold_in(own, 2), (rows, 1), 0, top)
    return jnp.take_along_axis(listing, (jnp.arange(top)[None, :] + offset_by) % top, axis=1)


def shares(count, total, limit, lean, full):
    loads = [(1 << 20) // math.isqrt(rank ** lean) + 1 for rank in range(1, count + 1)]
    largest = limit if full else min(limit, max(-(-total // count), total * loads[0] // sum(loads)))
    least = 1 if total - largest >= count - 1 else 0
    counts, spare = [largest] + [least] * (count - 1), total - largest - least * (count - 1)
    while spare > 0:
        movable = [i for i in range(1, count) if counts[i] < largest] or [i for i in range(1, count) if counts[i] < limit]
        whole, budget = sum([loads[i] for i in movable]), spare
        for i in movable:
            extra = min(limit - counts[i], max(1, budget * loads[i] // whole), spare)
            counts[i] = counts[i] + extra
            spare = spare - extra
    return np.array(counts)


def gaussian(rng, extent, scale, reach, shards=(), kind=jnp.bfloat16):
    entries = jax.random.normal(rng, extent, jnp.float32) * scale
    if len(shards) > 0:
        entries = shard_levels(rng, extent, shards, -0.22, 0.18) * entries
    return jnp.clip(entries, min=-reach, max=reach).astype(kind)


def setup_inputs(seed: int = 0) -> dict:
    arg_keys = jax.random.split(jax.random.key(seed), 16)
    new_query = draw_new_query(jax.random.fold_in(arg_keys[15], 71), 0)
    fresh_key_value = draw_fresh_key_value(jax.random.fold_in(arg_keys[15], 71), 0)
    prompt_cache = draw_prompt_cache(jax.random.fold_in(arg_keys[15], 71), 0)
    decoded_tail_cache = gaussian(arg_keys[3], (REQUEST_COUNT, TAIL_LENGTH, KEY_VALUE_HEADS, 2 * HEAD_SIZE), 1.0, 6.0, ((1, 32), (2, 8)))
    sinks = jnp.clip(2.0 + 12.0 * jax.random.uniform(arg_keys[4], (QUERY_HEADS,), jnp.float32) ** shard_levels(arg_keys[4], (QUERY_HEADS,), ((0, 8),), -0.2, 0.2), 2.0, 14.0)
    prompt_group = draw_prompt_group(jax.random.fold_in(arg_keys[15], 71), 0)
    prompt_lens = draw_prompt_lens(jax.random.fold_in(arg_keys[15], 71), 0)
    tail_lens = draw_tail_lens(jax.random.fold_in(arg_keys[15], 71), 0)
    o_weight = gaussian(arg_keys[8], (QUERY_HEADS * HEAD_SIZE, D), (QUERY_HEADS * HEAD_SIZE) ** -0.5, 0.09375, ((0, 8),))
    resid = gaussian(arg_keys[9], (REQUEST_COUNT, DECODE_STEPS, D), 0.3, 1.796875, ((0, 32),))
    norm_gain = jnp.clip(jnp.exp(jax.random.uniform(arg_keys[10], (D,), jnp.float32, math.log(0.3), math.log(3.0))), 0.3, 3.0)
    expert_ids_keys = jax.random.split(jax.random.fold_in(arg_keys[11], 1), REQUEST_COUNT * DECODE_STEPS // TOK_DEV)
    expert_ids_turns = jax.random.permutation(jax.random.fold_in(arg_keys[11], 3), REQUEST_COUNT * DECODE_STEPS // TOK_DEV)
    expert_ids = jax.vmap(lambda own, number: shared_out(jax.random.fold_in(arg_keys[11], 2), own, number, TOK_DEV, EXPERTS, TOP, MOST, 2))(expert_ids_keys, expert_ids_turns).reshape((REQUEST_COUNT, DECODE_STEPS, TOP))
    route_weights = jnp.clip(jnp.exp(math.log(0.6) - 2.4849067 * jax.random.uniform(arg_keys[12], (REQUEST_COUNT, DECODE_STEPS, TOP), jnp.float32) ** shard_levels(arg_keys[12], (REQUEST_COUNT, DECODE_STEPS, TOP), ((0, 32),), -0.2, 0.2)), 0.05, 0.6)
    gate_up = gaussian(arg_keys[13], (EXPERTS, D, 2, FF), (D // 9) ** -0.5, 0.3125, ((0, 32), (3, 8)))
    down_weight = gaussian(arg_keys[14], (EXPERTS, FF, D), (FF * 9) ** -0.5, 0.0390625, ((0, 32), (1, 8)))
    return dict(new_query=new_query, fresh_key_value=fresh_key_value, prompt_cache=prompt_cache, decoded_tail_cache=decoded_tail_cache, sinks=sinks, prompt_group=prompt_group, prompt_lens=prompt_lens, tail_lens=tail_lens, o_weight=o_weight, resid=resid, norm_gain=norm_gain, expert_ids=expert_ids, route_weights=route_weights, gate_up=gate_up, down_weight=down_weight)


def rotate(vector, position):
    half_width = vector.shape[-1] // 2
    frequency = jnp.exp(jnp.arange(half_width, dtype=jnp.float32) * (-2.0 * math.log(150000.0) / vector.shape[-1]))
    angle = position[..., None] * frequency
    cosine = jnp.cos(angle)
    sine_part = jnp.sin(angle)
    leading = vector[..., :half_width]
    trailing = vector[..., half_width:]
    return jnp.concatenate([leading * cosine - trailing * sine_part, trailing * cosine + leading * sine_part], axis=-1)

def expert_rows(row_block, joined_weight, down_rows):
    projected = jnp.dot(row_block, joined_weight.reshape(D, 2 * FF), preferred_element_type=jnp.float32)
    gate_part = jnp.minimum(projected[:, :FF], 7.0)
    up_part = jnp.clip(projected[:, FF:], -7.0, 7.0)
    activation = ((up_part + 1.0) * gate_part * jax.nn.sigmoid(1.702 * gate_part)).astype(jnp.bfloat16)
    return jnp.dot(activation, down_rows, preferred_element_type=jnp.float32)

def reference(new_query, fresh_key_value, prompt_cache, decoded_tail_cache, sinks, prompt_group, prompt_lens, tail_lens, o_weight, resid, norm_gain, expert_ids, route_weights, gate_up, down_weight):
    requests_per_group = QUERY_HEADS // KEY_VALUE_HEADS
    factor_scale = 1.0 / math.sqrt(HEAD_SIZE)
    attention_sink_rows = sinks.reshape(KEY_VALUE_HEADS, requests_per_group)

    def one_request(request):
        group_id = prompt_group[request]
        prompt_length = prompt_lens[group_id]
        tail_length = tail_lens[request]
        position = (prompt_length + tail_length + jnp.arange(DECODE_STEPS, dtype=jnp.int32)).astype(jnp.float32)
        query_matrix = rotate(new_query[request].reshape(DECODE_STEPS, QUERY_HEADS, HEAD_SIZE).astype(jnp.float32), position[:, None]).astype(jnp.bfloat16)
        query_matrix = query_matrix.reshape(DECODE_STEPS, KEY_VALUE_HEADS, requests_per_group, HEAD_SIZE)
        fresh = fresh_key_value[request]
        fresh_keys = rotate(fresh[:, :, :HEAD_SIZE].astype(jnp.float32), position[:, None]).astype(jnp.bfloat16)
        prompt_rows = prompt_cache[group_id]
        tail_rows = decoded_tail_cache[request]
        key_rows = jnp.concatenate([prompt_rows[:, :, :HEAD_SIZE], tail_rows[:, :, :HEAD_SIZE], fresh_keys], axis=0)
        value_rows = jnp.concatenate([prompt_rows[:, :, HEAD_SIZE:], tail_rows[:, :, HEAD_SIZE:], fresh[:, :, HEAD_SIZE:]], axis=0)
        cache_valid = jnp.concatenate([jnp.arange(PROMPT_LENGTH) < prompt_length, jnp.arange(TAIL_LENGTH) < tail_length])
        cache_valid = jnp.broadcast_to(cache_valid[None, :], (DECODE_STEPS, PROMPT_LENGTH + TAIL_LENGTH))
        fresh_valid = jnp.arange(DECODE_STEPS)[None, :] <= jnp.arange(DECODE_STEPS)[:, None]
        valid = jnp.concatenate([cache_valid, fresh_valid], axis=1)
        scores = jnp.einsum('tcgd,lcd->tcgl', query_matrix.astype(jnp.float32), key_rows.astype(jnp.float32)) * factor_scale
        scores = jnp.where(valid[:, None, None, :], scores, -jnp.inf)
        highest = jnp.maximum(lax.optimization_barrier(jnp.max(scores, axis=-1)), attention_sink_rows[None])
        weights = jnp.exp(scores - highest[..., None])
        denom = lax.optimization_barrier(jnp.sum(weights, axis=-1)) + jnp.exp(attention_sink_rows[None] - highest)
        rounded = weights.astype(jnp.bfloat16)
        attended = jnp.einsum('tcgl,lcd->tcgd', rounded.astype(jnp.float32), value_rows.astype(jnp.float32)) / denom[..., None]
        return attended.reshape(DECODE_STEPS, QUERY_HEADS * HEAD_SIZE).astype(jnp.bfloat16)
    attended = lax.map(one_request, jnp.arange(REQUEST_COUNT, dtype=jnp.int32))
    flat_rows = attended.reshape(REQUEST_COUNT * DECODE_STEPS, QUERY_HEADS * HEAD_SIZE)
    projected = jnp.dot(flat_rows, o_weight, preferred_element_type=jnp.float32)
    hidden = (resid.reshape(REQUEST_COUNT * DECODE_STEPS, D).astype(jnp.float32) + projected).astype(jnp.bfloat16)
    wide = hidden.astype(jnp.float32)
    normed = (wide * lax.rsqrt(lax.optimization_barrier(jnp.mean(wide * wide, axis=-1, keepdims=True)) + 1e-05) * norm_gain).astype(jnp.bfloat16)
    picks = expert_ids.reshape(-1)
    pick_weights = route_weights.reshape(-1)
    capacity = N_SEQ * MOST

    def one_expert(running, expert):
        matches = picks == expert
        chosen = jnp.nonzero(matches, size=capacity, fill_value=0)[0].astype(jnp.int32)
        live_rows = (jnp.arange(capacity) < jnp.sum(matches.astype(jnp.int32))).astype(jnp.float32)
        token_rows = chosen // TOP
        result = expert_rows(normed[token_rows], gate_up[expert], down_weight[expert])
        scaled = result * (pick_weights[chosen] * live_rows)[:, None]
        return (running.at[token_rows].add(scaled), None)
    expert_total, unused = lax.scan(one_expert, jnp.zeros((REQUEST_COUNT * DECODE_STEPS, D), jnp.float32), jnp.arange(EXPERTS, dtype=jnp.int32))
    return (wide + expert_total).astype(jnp.bfloat16).reshape(REQUEST_COUNT, DECODE_STEPS, D)
```

```python
import math

import jax
import jax.numpy as jnp
import numpy as np
from jax import lax
from jax.experimental import pallas as pl
from jax.experimental.pallas import tpu as pltpu
from jax.sharding import PartitionSpec as P

MESH = pl.DeviceIdType.MESH
LOW = -1e30
FLOOR = -1e29
F32 = jnp.float32
BF16 = jnp.bfloat16

N_SEQ = 32
N_HEAD = 8
REQ = 96
GROUPS = 8
MEMBERS = 12
PBLOCK = 1024
TBLOCK = 32
D = 2880
CH = 384
LASTC = 192
FFL = 360
ROWS = 96
NT = (((1,), (1,)), ((), ()))
NN = (((1,), (0,)), ((), ()))
TN = (((0,), (0,)), ((), ()))


def dot(a, b, dims):
    return lax.dot_general(a, b, dims, preferred_element_type=F32)


def iota(shape, axis):
    return lax.broadcasted_iota(jnp.int32, shape, axis)


def turned(x, cosine, sine, lane):
    ahead = pltpu.roll(x, 96, 1)
    behind = pltpu.roll(x, 32, 1)
    partner = jnp.where((lane & 63) < 32, -ahead, behind)
    return x * cosine + partner * sine


def tiles_of(out, peak, lane):
    first, second = out[:16], out[16:]
    values = jnp.where(lane < 64, pltpu.roll(first, 64, 1), second).astype(BF16)
    hi0 = first.astype(BF16).astype(F32)
    hi1 = second.astype(BF16).astype(F32)
    lo0 = first - hi0
    lo1 = second - hi1
    stats = jnp.where(
        lane < 4,
        jnp.where(lane == 0, peak[:16], jnp.where(lane == 1, hi0, jnp.where(lane == 2, lo0, 0.0))),
        jnp.where(
            lane == 4, peak[16:], jnp.where(lane == 5, hi1, jnp.where(lane == 6, lo1, 0.0))
        ),
    )
    return values, jnp.where(lane < 8, stats, 0.0)


def layer_kernel(
    order,
    rank,
    tail_lens,
    prompt_lens,
    sinks,
    cosb,
    sinb,
    steps_cos,
    steps_sin,
    fresh,
    ids,
    routes,
    resid,
    gain,
    q_hbm,
    prompt_hbm,
    tail_hbm,
    ow_hbm,
    gu_hbm,
    dn_hbm,
    out_ref,
    q_v,
    prompt_v,
    tail_v,
    ow_v,
    gu_v,
    dn_v,
    dn_last,
    q_all,
    acc_s,
    stat_s,
    msg1,
    rcv1,
    msg2,
    rcv2,
    msg3,
    rcv3,
    msg4,
    rcv4,
    msg5,
    rcv5,
    msg6,
    rcv6,
    msg7,
    rcv7,
    load_sem,
    prompt_sem,
    send1,
    recv1,
    send2,
    recv2,
    send3,
    recv3,
    send4,
    recv4,
    send5,
    recv5,
    send6,
    recv6,
    send7,
    recv7,
):
    me = lax.axis_index("seq")
    head = lax.axis_index("head")
    barrier = pltpu.get_barrier_semaphore()

    def greet_seq(d, carry):
        pl.semaphore_signal(
            barrier, inc=1, device_id=(lax.rem(me + d, N_SEQ), head), device_id_type=MESH
        )
        return carry

    def greet_head(d, carry):
        pl.semaphore_signal(
            barrier, inc=1, device_id=(me, lax.rem(head + d, N_HEAD)), device_id_type=MESH
        )
        return carry

    load_q = pltpu.make_async_copy(q_hbm, q_v, load_sem.at[0])
    load_tail = pltpu.make_async_copy(tail_hbm, tail_v, load_sem.at[1])
    load_ow = pltpu.make_async_copy(ow_hbm, ow_v.at[pl.ds(0, D)], load_sem.at[2])
    load_gu = pltpu.make_async_copy(gu_hbm, gu_v, load_sem.at[3])
    load_dn = pltpu.make_async_copy(dn_hbm, dn_v, load_sem.at[4])
    load_q.start()
    load_tail.start()

    def load_prompt(g):
        return pltpu.make_async_copy(prompt_hbm.at[g], prompt_v.at[g], prompt_sem.at[g])

    for g in range(GROUPS):
        load_prompt(g).start()
    load_ow.start()
    load_gu.start()
    load_dn.start()
    lax.fori_loop(1, N_SEQ, greet_seq, 0)
    lax.fori_loop(1, N_HEAD, greet_head, 0)

    lane = iota((16, 128), 1)
    row = iota((16, 128), 0)

    load_q.wait()
    ct = steps_cos[...]
    st = steps_sin[...]

    def rotate_one(i, carry):
        r = order[i]
        x = q_v[r].astype(F32)
        c0 = cosb[r]
        s0 = sinb[r]
        y = turned(x, c0 * ct - s0 * st, s0 * ct + c0 * st, lane)
        y = y.astype(BF16).astype(F32) * 0.125
        q_all[i, 0:16, :] = jnp.where(lane < 64, y, 0.0).astype(BF16)
        q_all[i, 16:32, :] = jnp.where(lane < 64, pltpu.roll(y, 64, 1), 0.0).astype(
            BF16
        )
        return carry

    lax.fori_loop(0, REQ, rotate_one, 0, unroll=4)
    load_tail.wait()

    pos_row = iota((1, PBLOCK), 1) + me * PBLOCK
    col128 = iota((1, 128), 1)
    big_lane = iota((PBLOCK, 128), 1)
    tail_lane = iota((128, 128), 1)
    same_req = (iota((128, 128), 0) >> 5) == (iota((128, 128), 1) >> 5)

    def one_group(g, carry):
        load_prompt(g).wait()
        kv = prompt_v[g]
        vx = jnp.where(big_lane < 64, jnp.ones_like(kv), kv)
        bias = jnp.where(pos_row < prompt_lens[g], 0.0, LOW)
        for b in range(3):
            base = g * MEMBERS + b * 4
            q = q_all[pl.ds(base, 4)].reshape(128, 128)
            members = [order[base + i] for i in range(4)]
            kt = jnp.concatenate([tail_v[r] for r in members], axis=0)
            vt = jnp.where(tail_lane < 64, jnp.ones_like(kt), kt)
            limit = jnp.zeros((1, 128), jnp.int32)
            for i in range(4):
                limit = jnp.where((col128 >> 5) == i, tail_lens[members[i]], limit)
            ok = ((col128 & 31) + me * TBLOCK) < limit
            tail_bias = jnp.where(ok, 0.0, LOW)
            s = dot(q, kv, NT) + bias
            s2 = jnp.where(same_req, dot(q, kt, NT) + tail_bias, LOW)
            peak = jnp.maximum(
                jnp.max(s, axis=1, keepdims=True), jnp.max(s2, axis=1, keepdims=True)
            )
            peak = jnp.maximum(peak, FLOOR).astype(BF16).astype(F32)
            w = jnp.exp(s - peak).astype(BF16)
            w2 = jnp.exp(s2 - peak).astype(BF16)
            o = dot(w, vx, NN) + dot(w2, vt, NN)
            for i in range(4):
                values, stats = tiles_of(
                    o[32 * i : 32 * i + 32], peak[32 * i : 32 * i + 32], lane
                )
                acc_s[base + i] = values
                stat_s[base + i] = stats
        return carry

    lax.fori_loop(0, GROUPS, one_group, 0)

    pl.semaphore_wait(barrier, N_SEQ - 1 + N_HEAD - 1)

    def pack(dst, slot, o):
        total = jnp.zeros((16, 128), F32)
        for i in range(3):
            k = rank[3 * o + i]
            dst[slot, 16 * i : 16 * i + 16, :] = acc_s[k]
            piece = stat_s[k]
            total = total + (piece if i == 0 else pltpu.roll(piece, 8 * i, 1))
        dst[slot, 48:64, :] = total.astype(BF16)

    def seq_copy(msg, rcv, send, recv, to):
        return pltpu.make_async_remote_copy(
            src_ref=msg.at[to],
            dst_ref=rcv.at[me],
            send_sem=send.at[to],
            recv_sem=recv.at[me],
            device_id=(to, head),
            device_id_type=MESH,
        )

    def seq_arrival(msg, rcv, send, recv, source):
        return pltpu.make_async_remote_copy(
            src_ref=msg.at[source],
            dst_ref=rcv.at[source],
            send_sem=send.at[source],
            recv_sem=recv.at[source],
            device_id=(source, head),
            device_id_type=MESH,
        )

    def head_copy(msg, slot, rcv, send, recv, to):
        return pltpu.make_async_remote_copy(
            src_ref=msg if slot is None else msg.at[slot],
            dst_ref=rcv.at[head],
            send_sem=send.at[to],
            recv_sem=recv.at[head],
            device_id=(me, to),
            device_id_type=MESH,
        )

    def head_arrival(msg, slot, rcv, send, recv, source):
        return pltpu.make_async_remote_copy(
            src_ref=msg if slot is None else msg.at[slot],
            dst_ref=rcv.at[source],
            send_sem=send.at[source],
            recv_sem=recv.at[source],
            device_id=(me, source),
            device_id_type=MESH,
        )

    def others(count, mine, body):
        def step(d, carry):
            body(lax.rem(mine + d, count))
            return carry

        lax.fori_loop(1, count, step, 0)

    def send_partials(o):
        pack(msg1, o, o)
        seq_copy(msg1, rcv1, send1, recv1, o).start()

    others(N_SEQ, me, send_partials)
    pack(rcv1, me, me)

    base_c = jnp.zeros((16, 128), F32)
    base_s = jnp.zeros((16, 128), F32)
    for i in range(3):
        base_c = jnp.where((row >> 2) == i, cosb[me * 3 + i], base_c)
        base_s = jnp.where((row >> 2) == i, sinb[me * 3 + i], base_s)
    kv_new = fresh[...].astype(F32)
    key_new = turned(kv_new, base_c * ct - base_s * st, base_s * ct + base_c * st, lane)
    kn = jnp.where(lane < 64, key_new, kv_new).astype(BF16)
    vn = jnp.where(lane < 64, 1.0, kv_new).astype(BF16)
    fresh_stats = jnp.zeros((16, 128), F32)
    srow = iota((32, 16), 0)
    scol = iota((32, 16), 1)
    for i in range(3):
        k = rank[3 * me + i]
        q = q_all[k]
        seen = ((scol >> 2) == i) & ((scol & 3) <= (srow & 3))
        s = jnp.where(seen, dot(q, kn, NT), LOW)
        peak = jnp.max(s, axis=1, keepdims=True).astype(BF16).astype(F32)
        w = jnp.exp(s - peak).astype(BF16)
        values, stats = tiles_of(dot(w, vn, NN), peak, lane)
        rcv1[N_SEQ, 16 * i : 16 * i + 16, :] = values
        fresh_stats = fresh_stats + (stats if i == 0 else pltpu.roll(stats, 8 * i, 1))
    rcv1[N_SEQ, 48:64, :] = fresh_stats.astype(BF16)

    sink = jnp.zeros((16, 128), F32)
    for j in range(8):
        here = ((row >> 2) == (j >> 1)) & ((lane >> 6) == (j & 1))
        sink = jnp.where(here, sinks[j], sink)

    wide_lane = iota((16, 512), 1)
    expert = wide_lane >> 4
    place = wide_lane & 15
    pick = (place >= 3).astype(jnp.int32) + (place >= 6).astype(jnp.int32)
    tile = place - 3 * pick
    named = jnp.zeros((16, 512), F32)
    share = jnp.zeros((16, 512), F32)
    for k in range(4):
        hit = ids[:, k : k + 1] == expert
        named = named + jnp.where(hit, 1.0, 0.0)
        share = share + jnp.where(hit, routes[:, k : k + 1], 0.0)
    below = (iota((16, 16), 1) < iota((16, 16), 0)).astype(F32).astype(BF16)
    earlier = dot(below, named.astype(BF16), NN)
    chosen = (named > 0.5) & (earlier == pick.astype(F32)) & (place < 9)
    chosen_tile = [chosen & (tile == c) for c in range(3)]
    select = jnp.concatenate([jnp.where(m, 1.0, 0.0) for m in chosen_tile], axis=0).astype(BF16)
    give = jnp.concatenate([jnp.where(m, share, 0.0) for m in chosen_tile], axis=0)
    give_hi = give.astype(BF16)
    give_lo = (give - give_hi.astype(F32)).astype(BF16)

    trow = iota((288, 512), 0)
    tcol = iota((288, 512), 1)
    ttile = (trow >= 96).astype(jnp.int32) + (trow >= 192).astype(jnp.int32)
    trest = trow - 96 * ttile
    spread = (
        ((trest & 31) == (tcol >> 4)) & ((tcol & 15) == 3 * (trest >> 5) + ttile)
    ).astype(F32).astype(BF16)

    load_ow.wait()
    ow_v[pl.ds(D, 3072 - D), :] = jnp.zeros((3072 - D, 512), BF16)
    load_gu.wait()
    load_dn.wait()
    dn_last[:, 0:LASTC] = dn_v[:, 7 * CH : 7 * CH + LASTC]
    dn_last[:, LASTC:CH] = jnp.zeros((FFL, CH - LASTC), BF16)

    others(N_SEQ, me, lambda s: seq_arrival(msg1, rcv1, send1, recv1, s).wait_recv())

    stat_rows = rcv1[:, 48:64, :].reshape((N_SEQ + 1) * 16, 128)
    er = iota((128, 384), 0)
    ec = iota((128, 384), 1)
    attended = []
    for i in range(3):
        spot = 8 * i + 4 * ((ec & 127) >> 6) + (ec >> 7)
        expand = (er == spot).astype(F32).astype(BF16)
        wide = dot(stat_rows, expand, NN)
        peaks = wide[:, 0:128].reshape(N_SEQ + 1, 16, 128)
        totals = (wide[:, 128:256] + wide[:, 256:384]).reshape(N_SEQ + 1, 16, 128)
        top = jnp.maximum(jnp.max(peaks, axis=0), sink)
        factor = jnp.exp(peaks - top[None])
        values = rcv1[:, 16 * i : 16 * i + 16, :].astype(F32)
        num = jnp.sum(values * factor, axis=0)
        den = jnp.sum(totals * factor, axis=0) + jnp.exp(sink - top)
        attended.append((num / den).astype(BF16))
    att = jnp.concatenate(attended, axis=0)
    rr = iota((64, 48), 0)
    rc = iota((64, 48), 1)
    want = ((rr & 15) >> 2) * 16 + (rr >> 4) * 4 + (rr & 3)
    regroup = (rc == want).astype(F32).astype(BF16)
    mixed = dot(regroup, att, NN).astype(BF16)
    flat = jnp.concatenate([mixed[16 * p : 16 * p + 16] for p in range(4)], axis=1)

    def project(j):
        rows = ow_v[pl.ds(pl.multiple_of(j * CH, CH), CH), :]
        return dot(flat, rows, NT).astype(BF16)

    def send_projection(j):
        msg2[j] = project(j)
        head_copy(msg2, j, rcv2, send2, recv2, j).start()

    others(N_HEAD, head, send_projection)
    rcv2[head] = project(head)
    others(N_HEAD, head, lambda s: head_arrival(msg2, s, rcv2, send2, recv2, s).wait_recv())
    total = resid[:, pl.ds(pl.multiple_of(head * CH, CH), CH)].astype(F32)
    total = total + jnp.sum(rcv2[...].astype(F32), axis=0)
    hidden = total.astype(BF16)
    hidden_rows = jnp.concatenate([hidden[:, 128 * c : 128 * c + 128] for c in range(3)], axis=0)

    msg3[...] = dot(select, hidden_rows, TN).astype(BF16).reshape(N_SEQ, 16, 128)
    others(N_SEQ, me, lambda o: seq_copy(msg3, rcv3, send3, recv3, o).start())
    rcv3[me] = msg3[me]
    others(N_SEQ, me, lambda s: seq_arrival(msg3, rcv3, send3, recv3, s).wait_recv())
    got = dot(spread, rcv3[...].reshape(512, 128), NN).astype(BF16)
    mine = jnp.concatenate([got[96 * c : 96 * c + 96] for c in range(3)], axis=1)
    msg4[...] = mine
    others(N_HEAD, head, lambda o: head_copy(msg4, None, rcv4, send4, recv4, o).start())
    rcv4[head] = mine

    gate = jnp.zeros((ROWS, FFL), F32)
    up = jnp.zeros((ROWS, FFL), F32)
    square = jnp.zeros((ROWS, 1), F32)
    for j in range(N_HEAD):

        @pl.when(head != j)
        def _():
            head_arrival(msg4, None, rcv4, send4, recv4, j).wait_recv()

        width = CH if j < N_HEAD - 1 else LASTC
        x = rcv4[j].astype(F32)
        square = square + jnp.sum(x * x, axis=1, keepdims=True)
        y = (x * gain[:, j * CH : j * CH + CH]).astype(BF16)[:, :width]
        gate = gate + dot(y, gu_v[0, :, j * CH : j * CH + width], NT)
        up = up + dot(y, gu_v[1, :, j * CH : j * CH + width], NT)
    scale = lax.rsqrt(square * (1.0 / D) + 1e-05)
    g = jnp.minimum(gate * scale, 7.0)
    u = jnp.clip(up * scale, -7.0, 7.0)
    active = ((u + 1.0) * g * jax.nn.sigmoid(1.702 * g)).astype(BF16)

    def send_expert(d, carry):
        j = lax.rem(head + d, N_HEAD)
        col = pl.multiple_of(jnp.minimum(j, N_HEAD - 2) * CH, CH)

        @pl.when(j < N_HEAD - 1)
        def _():
            msg5[j] = dot(active, dn_v[:, pl.ds(col, CH)], NN).astype(BF16)

        @pl.when(j == N_HEAD - 1)
        def _():
            msg5[j] = dot(active, dn_last[...], NN).astype(BF16)

        @pl.when(d < N_HEAD)
        def _():
            head_copy(msg5, j, rcv5, send5, recv5, j).start()

        return carry

    lax.fori_loop(1, N_HEAD + 1, send_expert, 0)
    rcv5[head] = msg5[head]
    others(N_HEAD, head, lambda s: head_arrival(msg5, s, rcv5, send5, recv5, s).wait_recv())
    summed = jnp.sum(rcv5[...].astype(F32), axis=0).astype(BF16)
    summed_rows = jnp.concatenate([summed[:, 128 * c : 128 * c + 128] for c in range(3)], axis=0)
    msg6[...] = dot(spread, summed_rows, TN).astype(BF16).reshape(N_SEQ, 16, 128)
    others(N_SEQ, me, lambda o: seq_copy(msg6, rcv6, send6, recv6, o).start())
    rcv6[me] = msg6[me]
    others(N_SEQ, me, lambda s: seq_arrival(msg6, rcv6, send6, recv6, s).wait_recv())
    back = rcv6[...].reshape(512, 128)
    added = dot(give_hi, back, NN) + dot(give_lo, back, NN)
    result = hidden_rows.astype(F32) + added
    result = jnp.concatenate([result[16 * c : 16 * c + 16] for c in range(3)], axis=1).astype(BF16)
    msg7[...] = result
    others(N_HEAD, head, lambda o: head_copy(msg7, None, rcv7, send7, recv7, o).start())
    rcv7[head] = result
    others(N_HEAD, head, lambda s: head_arrival(msg7, None, rcv7, send7, recv7, s).wait_recv())
    for j in range(N_HEAD):
        out_ref[:, j * CH : j * CH + CH] = rcv7[j]

    for msg, rcv, send, recv in (
        (msg1, rcv1, send1, recv1),
        (msg3, rcv3, send3, recv3),
        (msg6, rcv6, send6, recv6),
    ):
        others(N_SEQ, me, lambda o: seq_copy(msg, rcv, send, recv, o).wait_send())
    for msg, whole, rcv, send, recv in (
        (msg2, False, rcv2, send2, recv2),
        (msg4, True, rcv4, send4, recv4),
        (msg5, False, rcv5, send5, recv5),
        (msg7, True, rcv7, send7, recv7),
    ):
        others(
            N_HEAD,
            head,
            lambda o: head_copy(msg, None if whole else o, rcv, send, recv, o).wait_send(),
        )


def on_device(
    new_query,
    fresh_key_value,
    prompt_cache,
    decoded_tail_cache,
    sinks,
    prompt_group,
    prompt_lens,
    tail_lens,
    o_weight,
    resid,
    norm_gain,
    expert_ids,
    route_weights,
    gate_up,
    down_weight,
):
    me = lax.axis_index("seq")
    r = jnp.arange(REQ, dtype=jnp.int32)
    code = prompt_group * REQ + r
    rank = jnp.sum((code[None, :] < code[:, None]).astype(jnp.int32), axis=1)
    order = jnp.sum(jnp.where(rank[None, :] == r[:, None], r[None, :], 0), axis=1)
    hot = prompt_group[:, None] == jnp.arange(GROUPS, dtype=jnp.int32)[None, :]
    start = jnp.sum(jnp.where(hot, prompt_lens[None, :], 0), axis=1)
    base = (start + tail_lens).astype(F32)
    frequency = jnp.exp(jnp.arange(32, dtype=F32) * (-2.0 * math.log(150000.0) / 64))
    angle = base[:, None] * jnp.tile(frequency, 4)[None, :]
    cosb, sinb = jnp.cos(angle)[:, None, :], jnp.sin(angle)[:, None, :]
    freq = np.exp(np.arange(32) * (-2.0 * math.log(150000.0) / 64))
    step_angle = (np.arange(16) % 4)[:, None] * np.tile(freq, 4)[None, :]
    steps_cos = jnp.asarray(np.cos(step_angle), F32)
    steps_sin = jnp.asarray(np.sin(step_angle), F32)
    fresh = jnp.pad(fresh_key_value.reshape(12, 128), ((0, 4), (0, 0)))
    own_ids = lax.dynamic_slice_in_dim(expert_ids, me * 3, 3, 0).reshape(12, 4)
    own_ids = jnp.pad(own_ids, ((0, 4), (0, 0)), constant_values=-1)
    routes = jnp.pad(route_weights.reshape(12, 4), ((0, 4), (0, 0)))
    resid16 = jnp.pad(resid.reshape(12, D), ((0, 4), (0, 3072 - D)))
    gain = jnp.pad(norm_gain, (0, 3072 - D)).reshape(1, 3072)
    q = new_query.reshape(REQ, 4, 4, 128).transpose(0, 2, 1, 3).reshape(REQ, 16, 128)
    prompt = prompt_cache.transpose(0, 2, 1, 3).reshape(GROUPS, PBLOCK, 128)
    tail = decoded_tail_cache.transpose(0, 2, 1, 3).reshape(REQ, TBLOCK, 128)
    ow = o_weight.T
    gu = gate_up.transpose(0, 2, 3, 1).reshape(2, FFL, D)
    dn = down_weight.reshape(FFL, D)

    smem = pl.BlockSpec(memory_space=pltpu.SMEM)
    vmem = pl.BlockSpec(memory_space=pltpu.VMEM)
    hbm = pl.BlockSpec(memory_space=pl.ANY)
    seq_sem = pltpu.SemaphoreType.DMA((N_SEQ,))
    head_sem = pltpu.SemaphoreType.DMA((N_HEAD,))
    out = pl.pallas_call(
        layer_kernel,
        name="layer",
        out_shape=jax.ShapeDtypeStruct((16, 3072), BF16),
        in_specs=[smem] * 5 + [vmem] * 9 + [hbm] * 6,
        out_specs=vmem,
        scratch_shapes=[
            pltpu.VMEM((REQ, 16, 128), BF16),
            pltpu.VMEM((GROUPS, PBLOCK, 128), BF16),
            pltpu.VMEM((REQ, TBLOCK, 128), BF16),
            pltpu.VMEM((3072, 512), BF16),
            pltpu.VMEM((2, FFL, D), BF16),
            pltpu.VMEM((FFL, D), BF16),
            pltpu.VMEM((FFL, CH), BF16),
            pltpu.VMEM((REQ, 32, 128), BF16),
            pltpu.VMEM((REQ, 16, 128), BF16),
            pltpu.VMEM((REQ, 16, 128), F32),
            pltpu.VMEM((N_SEQ, 64, 128), BF16),
            pltpu.VMEM((N_SEQ + 1, 64, 128), BF16),
            pltpu.VMEM((N_HEAD, 16, CH), BF16),
            pltpu.VMEM((N_HEAD, 16, CH), BF16),
            pltpu.VMEM((N_SEQ, 16, 128), BF16),
            pltpu.VMEM((N_SEQ, 16, 128), BF16),
            pltpu.VMEM((ROWS, CH), BF16),
            pltpu.VMEM((N_HEAD, ROWS, CH), BF16),
            pltpu.VMEM((N_HEAD, ROWS, CH), BF16),
            pltpu.VMEM((N_HEAD, ROWS, CH), BF16),
            pltpu.VMEM((N_SEQ, 16, 128), BF16),
            pltpu.VMEM((N_SEQ, 16, 128), BF16),
            pltpu.VMEM((16, CH), BF16),
            pltpu.VMEM((N_HEAD, 16, CH), BF16),
            pltpu.SemaphoreType.DMA((5,)),
            pltpu.SemaphoreType.DMA((GROUPS,)),
            seq_sem,
            seq_sem,
            head_sem,
            head_sem,
            seq_sem,
            seq_sem,
            head_sem,
            head_sem,
            head_sem,
            head_sem,
            seq_sem,
            seq_sem,
            head_sem,
            head_sem,
        ],
        compiler_params=pltpu.CompilerParams(
            collective_id=0, has_side_effects=True, vmem_limit_bytes=56 * 1024 * 1024
        ),
    )(
        order,
        rank,
        tail_lens,
        prompt_lens,
        sinks,
        cosb,
        sinb,
        steps_cos,
        steps_sin,
        fresh,
        own_ids,
        routes,
        resid16,
        gain,
        q,
        prompt,
        tail,
        ow,
        gu,
        dn,
    )
    return out[:12, :D].reshape(3, 4, D)


def solution(mesh):
    return jax.shard_map(
        on_device,
        mesh=mesh,
        in_specs=(
            P(None, None, "head"),
            P("seq", None, "head", None),
            P(None, "seq", "head", None),
            P(None, "seq", "head", None),
            P("head"),
            P(),
            P(),
            P(),
            P("head", None),
            P("seq", None, None),
            P(),
            P(),
            P("seq", None, None),
            P("seq", None, None, "head"),
            P("seq", "head", None),
        ),
        out_specs=P("seq", None, None),
        check_vma=False,
    )
```

```python
import math

import jax
import jax.numpy as jnp
import numpy as np
from jax import lax
from jax.experimental import pallas as pl
from jax.experimental.pallas import tpu as pltpu
from jax.sharding import PartitionSpec as P

MESH = pl.DeviceIdType.MESH
LOW = -1e30
FLOOR = -1e29
F32 = jnp.float32
BF16 = jnp.bfloat16

N_SEQ = 32
N_HEAD = 8
REQ = 96
GROUPS = 8
MEMBERS = 12
PBLOCK = 1024
TBLOCK = 32
D = 2880
CH = 384
LASTC = 192
FFL = 360
ROWS = 96
HALF_PI = (1.5703125, 4.8351287841796875e-4, 3.1391647865048e-7)
NT = (((1,), (1,)), ((), ()))
NN = (((1,), (0,)), ((), ()))
TN = (((0,), (0,)), ((), ()))


def dot(a, b, dims):
    return lax.dot_general(a, b, dims, preferred_element_type=F32)


def iota(shape, axis):
    return lax.broadcasted_iota(jnp.int32, shape, axis)


def turned(x, cosine, sine, lane):
    ahead = pltpu.roll(x, 96, 1)
    behind = pltpu.roll(x, 32, 1)
    partner = jnp.where((lane & 63) < 32, -ahead, behind)
    return x * cosine + partner * sine


def cos_sin(angle):
    k = jnp.floor(angle * (2.0 / math.pi) + 0.5)
    r = angle - k * HALF_PI[0]
    r = r - k * HALF_PI[1]
    r = r - k * HALF_PI[2]
    r2 = r * r
    s = r + r * r2 * (-1.0 / 6 + r2 * (1.0 / 120 + r2 * (-1.0 / 5040 + r2 * (1.0 / 362880))))
    c = 1.0 + r2 * (-0.5 + r2 * (1.0 / 24 + r2 * (-1.0 / 720 + r2 * (1.0 / 40320))))
    quarter = k - 4.0 * jnp.floor(k * 0.25)
    odd = (quarter == 1.0) | (quarter == 3.0)
    cosine = jnp.where(odd, s, c)
    sine = jnp.where(odd, c, s)
    cosine = jnp.where((quarter == 1.0) | (quarter == 2.0), -cosine, cosine)
    sine = jnp.where(quarter >= 2.0, -sine, sine)
    return cosine, sine


def tiles_of(out, peak, lane):
    first, second = out[:16], out[16:]
    values = jnp.where(lane < 64, pltpu.roll(first, 64, 1), second).astype(BF16)
    hi0 = first.astype(BF16).astype(F32)
    hi1 = second.astype(BF16).astype(F32)
    lo0 = first - hi0
    lo1 = second - hi1
    stats = jnp.where(
        lane < 4,
        jnp.where(lane == 0, peak[:16], jnp.where(lane == 1, hi0, jnp.where(lane == 2, lo0, 0.0))),
        jnp.where(
            lane == 4, peak[16:], jnp.where(lane == 5, hi1, jnp.where(lane == 6, lo1, 0.0))
        ),
    )
    return values, jnp.where(lane < 8, stats, 0.0)


def layer_kernel(
    order,
    rank,
    prompt_group,
    tail_lens,
    prompt_lens,
    sinks,
    tables,
    fresh,
    ids,
    routes,
    resid,
    gain,
    q_hbm,
    prompt_hbm,
    tail_hbm,
    ow_hbm,
    gu_hbm,
    dn_hbm,
    out_ref,
    q_v,
    prompt_v,
    tail_v,
    ow_v,
    gu_v,
    dn_v,
    dn_last,
    cos_s,
    sin_s,
    small_s,
    route_s,
    resid_s,
    q_all,
    acc_s,
    stat_s,
    msg1,
    rcv1,
    msg2,
    rcv2,
    msg3,
    rcv3,
    msg4,
    rcv4,
    msg5,
    rcv5,
    msg6,
    rcv6,
    msg7,
    rcv7,
    load_sem,
    prompt_sem,
    send1,
    recv1,
    send2,
    recv2,
    send3,
    recv3,
    send4,
    recv4,
    send5,
    recv5,
    send6,
    recv6,
    send7,
    recv7,
):
    me = lax.axis_index("seq")
    head = lax.axis_index("head")
    barrier = pltpu.get_barrier_semaphore()

    def greet_seq(d, carry):
        pl.semaphore_signal(
            barrier, inc=1, device_id=(lax.rem(me + d, N_SEQ), head), device_id_type=MESH
        )
        return carry

    def greet_head(d, carry):
        pl.semaphore_signal(
            barrier, inc=1, device_id=(me, lax.rem(head + d, N_HEAD)), device_id_type=MESH
        )
        return carry

    load_q = pltpu.make_async_copy(q_hbm, q_v, load_sem.at[0])
    load_tail = pltpu.make_async_copy(tail_hbm, tail_v, load_sem.at[1])
    load_ow = pltpu.make_async_copy(ow_hbm, ow_v.at[pl.ds(0, D)], load_sem.at[2])
    load_gate = pltpu.make_async_copy(gu_hbm.at[0], gu_v.at[pl.ds(0, FFL)], load_sem.at[3])
    load_up = pltpu.make_async_copy(gu_hbm.at[1], gu_v.at[pl.ds(CH, FFL)], load_sem.at[5])
    load_dn = pltpu.make_async_copy(dn_hbm, dn_v.at[pl.ds(0, FFL)], load_sem.at[4])
    load_q.start()
    load_tail.start()

    def load_prompt(g):
        return pltpu.make_async_copy(prompt_hbm.at[g], prompt_v.at[g], prompt_sem.at[g])

    for g in range(GROUPS):
        load_prompt(g).start()
    load_ow.start()
    load_gate.start()
    load_up.start()
    load_dn.start()
    lax.fori_loop(1, N_SEQ, greet_seq, 0)
    lax.fori_loop(1, N_HEAD, greet_head, 0)

    lane = iota((16, 128), 1)
    row = iota((16, 128), 0)

    freq = tables[0:1, :]
    ct = tables[8:24, :]
    st = tables[24:40, :]

    def place(r):
        return (prompt_lens[prompt_group[r]] + tail_lens[r]).astype(F32)

    def put_angle(i, carry):
        cos_s[pl.ds(i, 1), :] = freq * place(order[i])
        return carry

    lax.fori_loop(0, REQ, put_angle, 0, unroll=8)
    cosine, sine = cos_sin(cos_s[...])
    cos_s[...] = cosine
    sin_s[...] = sine

    load_q.wait()

    unit = jnp.where(lane == 64, 1.0, 0.0)

    def rotate_one(i, carry):
        r = order[i]
        x = q_v[r].astype(F32)
        c0 = cos_s[pl.ds(i, 1), :]
        s0 = sin_s[pl.ds(i, 1), :]
        y = turned(x, c0 * ct - s0 * st, s0 * ct + c0 * st, lane)
        y = y.astype(BF16).astype(F32) * 0.125
        q_all[i, 0:16, :] = jnp.where(lane < 64, y, unit).astype(BF16)
        q_all[i, 16:32, :] = jnp.where(
            lane < 64, pltpu.roll(y, 64, 1), unit
        ).astype(BF16)
        return carry

    lax.fori_loop(0, REQ, rotate_one, 0, unroll=4)
    load_tail.wait()

    key_row = iota((PBLOCK, 128), 0) + me * PBLOCK
    key_lane = iota((PBLOCK, 128), 1)
    col128 = iota((1, 128), 1)
    tail_lane = iota((128, 128), 1)
    same_req = (iota((128, 128), 0) >> 5) == (iota((128, 128), 1) >> 5)

    def one_group(g, carry):
        load_prompt(g).wait()
        first = g * MEMBERS
        kv = prompt_v[g]
        bias = jnp.where(key_row < prompt_lens[g], 0.0, LOW).astype(BF16)
        kx = jnp.where(key_lane < 64, kv, bias)
        vx = jnp.where(key_lane < 64, jnp.ones_like(kv), kv)
        q = q_all[pl.ds(first, MEMBERS)].reshape(MEMBERS * 32, 128)
        s = dot(q, kx, NT)
        members = [order[first + i] for i in range(MEMBERS)]
        s2 = []
        vt = []
        for b in range(3):
            kt = jnp.concatenate([tail_v[r] for r in members[4 * b : 4 * b + 4]], axis=0)
            limit = jnp.zeros((1, 128), jnp.int32)
            for i in range(4):
                limit = jnp.where((col128 >> 5) == i, tail_lens[members[4 * b + i]], limit)
            seen = same_req & (((col128 & 31) + me * TBLOCK) < limit)
            qt = jnp.where(tail_lane < 64, q[128 * b : 128 * b + 128], jnp.zeros_like(kt))
            s2.append(jnp.where(seen, dot(qt, kt, NT), LOW))
            vt.append(jnp.where(tail_lane < 64, jnp.ones_like(kt), kt))
        s2 = jnp.concatenate(s2, axis=0)
        peak = jnp.maximum(jnp.max(s, axis=1, keepdims=True), jnp.max(s2, axis=1, keepdims=True))
        peak = jnp.maximum(peak, FLOOR).astype(BF16).astype(F32)
        w = jnp.exp(s - peak).astype(BF16)
        w2 = jnp.exp(s2 - peak).astype(BF16)
        o = dot(w, vx, NN)
        for b in range(3):
            ob = o[128 * b : 128 * b + 128] + dot(w2[128 * b : 128 * b + 128], vt[b], NN)
            pb = peak[128 * b : 128 * b + 128]
            for i in range(4):
                values, stats = tiles_of(
                    ob[32 * i : 32 * i + 32], pb[32 * i : 32 * i + 32], lane
                )
                acc_s[first + 4 * b + i] = values
                stat_s[first + 4 * b + i] = stats
        return carry

    lax.fori_loop(0, GROUPS, one_group, 0)

    pl.semaphore_wait(barrier, N_SEQ - 1 + N_HEAD - 1)

    def pack(dst, slot, o):
        total = jnp.zeros((16, 128), F32)
        for i in range(3):
            k = rank[3 * o + i]
            dst[slot, 16 * i : 16 * i + 16, :] = acc_s[k]
            piece = stat_s[k]
            total = total + (piece if i == 0 else pltpu.roll(piece, 8 * i, 1))
        dst[slot, 48:64, :] = total.astype(BF16)

    def seq_copy(msg, rcv, send, recv, to):
        return pltpu.make_async_remote_copy(
            src_ref=msg.at[to],
            dst_ref=rcv.at[me],
            send_sem=send.at[to],
            recv_sem=recv.at[me],
            device_id=(to, head),
            device_id_type=MESH,
        )

    def seq_arrival(msg, rcv, send, recv, source):
        return pltpu.make_async_remote_copy(
            src_ref=msg.at[source],
            dst_ref=rcv.at[source],
            send_sem=send.at[source],
            recv_sem=recv.at[source],
            device_id=(source, head),
            device_id_type=MESH,
        )

    def head_copy(msg, slot, rcv, send, recv, to):
        return pltpu.make_async_remote_copy(
            src_ref=msg if slot is None else msg.at[slot],
            dst_ref=rcv.at[head],
            send_sem=send.at[to],
            recv_sem=recv.at[head],
            device_id=(me, to),
            device_id_type=MESH,
        )

    def head_arrival(msg, slot, rcv, send, recv, source):
        return pltpu.make_async_remote_copy(
            src_ref=msg if slot is None else msg.at[slot],
            dst_ref=rcv.at[source],
            send_sem=send.at[source],
            recv_sem=recv.at[source],
            device_id=(me, source),
            device_id_type=MESH,
        )

    def others(count, mine, body):
        def step(d, carry):
            body(lax.rem(mine + d, count))
            return carry

        lax.fori_loop(1, count, step, 0)

    def send_partials(o):
        pack(msg1, o, o)
        seq_copy(msg1, rcv1, send1, recv1, o).start()

    others(N_SEQ, me, send_partials)
    pack(rcv1, me, me)

    angle = jnp.zeros((16, 128), F32)
    for i in range(3):
        angle = jnp.where((row >> 2) == i, freq * place(me * 3 + i), angle)
        small_s[4 * i : 4 * i + 4, :] = fresh[i].astype(F32)
    base_c, base_s = cos_sin(angle)
    small_s[12:16, :] = jnp.zeros((4, 128), F32)
    kv_new = small_s[...]
    key_new = turned(kv_new, base_c * ct - base_s * st, base_s * ct + base_c * st, lane)
    kn = jnp.where(lane < 64, key_new, kv_new).astype(BF16)
    vn = jnp.where(lane < 64, 1.0, kv_new).astype(BF16)
    fresh_stats = jnp.zeros((16, 128), F32)
    srow = iota((32, 16), 0)
    scol = iota((32, 16), 1)
    for i in range(3):
        k = rank[3 * me + i]
        q = q_all[k]
        seen = ((scol >> 2) == i) & ((scol & 3) <= (srow & 3))
        q = jnp.where(iota((32, 128), 1) < 64, q, jnp.zeros_like(q))
        s = jnp.where(seen, dot(q, kn, NT), LOW)
        peak = jnp.max(s, axis=1, keepdims=True).astype(BF16).astype(F32)
        w = jnp.exp(s - peak).astype(BF16)
        values, stats = tiles_of(dot(w, vn, NN), peak, lane)
        rcv1[N_SEQ, 16 * i : 16 * i + 16, :] = values
        fresh_stats = fresh_stats + (stats if i == 0 else pltpu.roll(stats, 8 * i, 1))
    rcv1[N_SEQ, 48:64, :] = fresh_stats.astype(BF16)

    sink = jnp.zeros((16, 128), F32)
    for j in range(8):
        here = ((row >> 2) == (j >> 1)) & ((lane >> 6) == (j & 1))
        sink = jnp.where(here, sinks[j], sink)

    wide_lane = iota((16, 512), 1)
    expert = wide_lane >> 4
    place = wide_lane & 15
    pick = (place >= 3).astype(jnp.int32) + (place >= 6).astype(jnp.int32)
    tile = place - 3 * pick
    own = (iota((REQ, 384), 0) == me * 3 + (iota((REQ, 384), 1) >> 7)).astype(F32).astype(BF16)
    flat_ids = jnp.concatenate([ids[t] for t in range(4)], axis=0).astype(F32).astype(BF16)
    own_ids = dot(flat_ids, own, NN).astype(BF16)
    xr = iota((64, 16), 0)
    xc = iota((64, 16), 1)
    names = jnp.full((64, 128), -1.0, F32) * ((iota((64, 128), 0) & 15) >= 12).astype(F32)
    for i in range(3):
        take = (xc == (xr & 3) * 4 + (xr >> 4)) & (((xr & 15) >> 2) == i)
        names = names + dot(
            take.astype(F32).astype(BF16), own_ids[:, 128 * i : 128 * i + 128], NN
        )
    names = jnp.concatenate([names] * 4, axis=1)
    route_s[...] = jnp.zeros((16, 128), F32)
    for i in range(3):
        route_s[4 * i : 4 * i + 4, 0:4] = routes[i]
    named = jnp.zeros((16, 512), F32)
    share = jnp.zeros((16, 512), F32)
    for k in range(4):
        hit = names[16 * k : 16 * k + 16] == expert.astype(F32)
        named = named + jnp.where(hit, 1.0, 0.0)
        share = share + jnp.where(hit, route_s[:, k : k + 1], 0.0)
    below = (iota((16, 16), 1) < iota((16, 16), 0)).astype(F32).astype(BF16)
    earlier = dot(below, named.astype(BF16), NN)
    chosen = (named > 0.5) & (earlier == pick.astype(F32)) & (place < 9)
    chosen_tile = [chosen & (tile == c) for c in range(3)]
    select = jnp.concatenate([jnp.where(m, 1.0, 0.0) for m in chosen_tile], axis=0)
    select = select.T.astype(BF16)
    give = jnp.concatenate([jnp.where(m, share, 0.0) for m in chosen_tile], axis=0)
    give_hi = give.astype(BF16)
    give_lo = (give - give_hi.astype(F32)).astype(BF16)

    trow = iota((288, 512), 0)
    tcol = iota((288, 512), 1)
    ttile = (trow >= 96).astype(jnp.int32) + (trow >= 192).astype(jnp.int32)
    trest = trow - 96 * ttile
    spread = (
        ((trest & 31) == (tcol >> 4)) & ((tcol & 15) == 3 * (trest >> 5) + ttile)
    ).astype(F32).astype(BF16)

    ucol = iota((512, 288), 1)
    urow = iota((512, 288), 0)
    utile = (ucol >= 96).astype(jnp.int32) + (ucol >= 192).astype(jnp.int32)
    urest = ucol - 96 * utile
    gather = (
        ((urest & 31) == (urow >> 4)) & ((urow & 15) == 3 * (urest >> 5) + utile)
    ).astype(F32).astype(BF16)
    resid_s[...] = jnp.zeros((16, 3072), F32)
    for i in range(3):
        resid_s[4 * i : 4 * i + 4, 0:D] = resid[i].astype(F32)

    load_ow.wait()
    ow_v[pl.ds(D, 3072 - D), :] = jnp.zeros((3072 - D, 512), BF16)
    load_gate.wait()
    load_up.wait()
    load_dn.wait()
    gu_v[FFL:CH, :] = jnp.zeros((CH - FFL, D), BF16)
    gu_v[CH + FFL : 2 * CH, :] = jnp.zeros((CH - FFL, D), BF16)
    dn_v[FFL:CH, :] = jnp.zeros((CH - FFL, D), BF16)
    dn_last[:, 0:LASTC] = dn_v[:, 7 * CH : 7 * CH + LASTC]
    dn_last[:, LASTC:CH] = jnp.zeros((CH, CH - LASTC), BF16)

    others(N_SEQ, me, lambda s: seq_arrival(msg1, rcv1, send1, recv1, s).wait_recv())

    stat_rows = rcv1[:, 48:64, :].reshape((N_SEQ + 1) * 16, 128)
    er = iota((128, 384), 0)
    ec = iota((128, 384), 1)
    attended = []
    for i in range(3):
        spot = 8 * i + 4 * ((ec & 127) >> 6) + (ec >> 7)
        expand = (er == spot).astype(F32).astype(BF16)
        wide = dot(stat_rows, expand, NN)
        peaks = wide[:, 0:128].reshape(N_SEQ + 1, 16, 128)
        totals = (wide[:, 128:256] + wide[:, 256:384]).reshape(N_SEQ + 1, 16, 128)
        top = jnp.maximum(jnp.max(peaks, axis=0), sink)
        factor = jnp.exp(peaks - top[None])
        values = rcv1[:, 16 * i : 16 * i + 16, :].astype(F32)
        num = jnp.sum(values * factor, axis=0)
        den = jnp.sum(totals * factor, axis=0) + jnp.exp(sink - top)
        attended.append((num / den).astype(BF16))
    att = jnp.concatenate(attended, axis=0)
    rr = iota((64, 48), 0)
    rc = iota((64, 48), 1)
    want = ((rr & 15) >> 2) * 16 + (rr >> 4) * 4 + (rr & 3)
    regroup = (rc == want).astype(F32).astype(BF16)
    mixed = dot(regroup, att, NN).astype(BF16)
    flat = jnp.concatenate([mixed[16 * p : 16 * p + 16] for p in range(4)], axis=1)

    def project(j):
        rows = ow_v[pl.ds(pl.multiple_of(j * CH, CH), CH), :]
        return dot(flat, rows, NT).astype(BF16)

    def send_projection(j):
        msg2[j] = project(j)
        head_copy(msg2, j, rcv2, send2, recv2, j).start()

    others(N_HEAD, head, send_projection)
    rcv2[head] = project(head)
    others(N_HEAD, head, lambda s: head_arrival(msg2, s, rcv2, send2, recv2, s).wait_recv())
    total = resid_s[:, pl.ds(pl.multiple_of(head * CH, CH), CH)]
    total = total + jnp.sum(rcv2[...].astype(F32), axis=0)
    hidden = total.astype(BF16)
    hidden_rows = jnp.concatenate([hidden[:, 128 * c : 128 * c + 128] for c in range(3)], axis=0)

    msg3[...] = dot(select, hidden_rows, NN).astype(BF16).reshape(N_SEQ, 16, 128)
    others(N_SEQ, me, lambda o: seq_copy(msg3, rcv3, send3, recv3, o).start())
    rcv3[me] = msg3[me]
    others(N_SEQ, me, lambda s: seq_arrival(msg3, rcv3, send3, recv3, s).wait_recv())
    got = dot(spread, rcv3[...].reshape(512, 128), NN).astype(BF16)
    mine = jnp.concatenate([got[96 * c : 96 * c + 96] for c in range(3)], axis=1)
    msg4[...] = mine
    others(N_HEAD, head, lambda o: head_copy(msg4, None, rcv4, send4, recv4, o).start())
    rcv4[head] = mine

    both = jnp.zeros((ROWS, 2 * CH), F32)
    square = jnp.zeros((ROWS, 1), F32)
    for half in range(2):
        parts = []
        for j in range(4 * half, 4 * half + 4):

            @pl.when(head != j)
            def _():
                head_arrival(msg4, None, rcv4, send4, recv4, j).wait_recv()

            width = CH if j < N_HEAD - 1 else LASTC
            x = rcv4[j, :, 0:width].astype(F32)
            square = square + jnp.sum(x * x, axis=1, keepdims=True)
            parts.append((x * gain[:, j * CH : j * CH + width]).astype(BF16))
        stop = min(D, 4 * (half + 1) * CH)
        both = both + dot(jnp.concatenate(parts, axis=1), gu_v[:, 4 * half * CH : stop], NT)
    scale = lax.rsqrt(square * (1.0 / D) + 1e-05)
    g = jnp.minimum(both[:, 0:CH] * scale, 7.0)
    u = jnp.clip(both[:, CH : 2 * CH] * scale, -7.0, 7.0)
    active = ((u + 1.0) * g * jax.nn.sigmoid(1.702 * g)).astype(BF16)

    def send_expert(d, carry):
        j = lax.rem(head + d, N_HEAD)
        col = pl.multiple_of(jnp.minimum(j, N_HEAD - 2) * CH, CH)

        @pl.when(j < N_HEAD - 1)
        def _():
            msg5[j] = dot(active, dn_v[:, pl.ds(col, CH)], NN).astype(BF16)

        @pl.when(j == N_HEAD - 1)
        def _():
            msg5[j] = dot(active, dn_last[...], NN).astype(BF16)

        @pl.when(d < N_HEAD)
        def _():
            head_copy(msg5, j, rcv5, send5, recv5, j).start()

        return carry

    lax.fori_loop(1, N_HEAD + 1, send_expert, 0)
    rcv5[head] = msg5[head]
    others(N_HEAD, head, lambda s: head_arrival(msg5, s, rcv5, send5, recv5, s).wait_recv())
    summed = jnp.sum(rcv5[...].astype(F32), axis=0).astype(BF16)
    summed_rows = jnp.concatenate([summed[:, 128 * c : 128 * c + 128] for c in range(3)], axis=0)
    msg6[...] = dot(gather, summed_rows, NN).astype(BF16).reshape(N_SEQ, 16, 128)
    others(N_SEQ, me, lambda o: seq_copy(msg6, rcv6, send6, recv6, o).start())
    rcv6[me] = msg6[me]
    others(N_SEQ, me, lambda s: seq_arrival(msg6, rcv6, send6, recv6, s).wait_recv())
    back = rcv6[...].reshape(512, 128)
    added = dot(give_hi, back, NN) + dot(give_lo, back, NN)
    result = hidden_rows.astype(F32) + added
    result = jnp.concatenate([result[16 * c : 16 * c + 16] for c in range(3)], axis=1).astype(BF16)
    msg7[...] = result
    others(N_HEAD, head, lambda o: head_copy(msg7, None, rcv7, send7, recv7, o).start())
    rcv7[head] = result
    others(N_HEAD, head, lambda s: head_arrival(msg7, None, rcv7, send7, recv7, s).wait_recv())
    for i in range(3):
        for j in range(N_HEAD):
            width = CH if j < N_HEAD - 1 else LASTC
            out_ref[i, :, j * CH : j * CH + width] = rcv7[j, 4 * i : 4 * i + 4, 0:width]

    for msg, rcv, send, recv in (
        (msg1, rcv1, send1, recv1),
        (msg3, rcv3, send3, recv3),
        (msg6, rcv6, send6, recv6),
    ):
        others(N_SEQ, me, lambda o: seq_copy(msg, rcv, send, recv, o).wait_send())
    for msg, whole, rcv, send, recv in (
        (msg2, False, rcv2, send2, recv2),
        (msg4, True, rcv4, send4, recv4),
        (msg5, False, rcv5, send5, recv5),
        (msg7, True, rcv7, send7, recv7),
    ):
        others(
            N_HEAD,
            head,
            lambda o: head_copy(msg, None if whole else o, rcv, send, recv, o).wait_send(),
        )


def on_device(
    new_query,
    fresh_key_value,
    prompt_cache,
    decoded_tail_cache,
    sinks,
    prompt_group,
    prompt_lens,
    tail_lens,
    o_weight,
    resid,
    norm_gain,
    expert_ids,
    route_weights,
    gate_up,
    down_weight,
):
    r = jnp.arange(REQ, dtype=jnp.int32)
    mine, other = prompt_group[:, None], prompt_group[None, :]
    ahead = (other < mine) | ((other == mine) & (r[None, :] < r[:, None]))
    rank = jnp.sum(ahead.astype(jnp.int32), axis=1)
    order = jnp.sum(jnp.where(rank[None, :] == r[:, None], r[None, :], 0), axis=1)
    freq = np.exp(np.arange(32) * (-2.0 * math.log(150000.0) / 64))
    freq = np.tile(freq.astype(np.float32), 4)
    step_angle = (np.arange(16) % 4)[:, None] * freq[None, :].astype(np.float64)
    tables = np.zeros((40, 128), np.float32)
    tables[0] = freq
    tables[8:24] = np.cos(step_angle)
    tables[24:40] = np.sin(step_angle)
    fresh = fresh_key_value.transpose(0, 2, 1, 3).reshape(3, 4, 128)
    ids = expert_ids.transpose(1, 2, 0)
    gain = norm_gain.reshape(1, D)
    q = new_query.reshape(REQ, 4, 4, 128).transpose(0, 2, 1, 3).reshape(REQ, 16, 128)
    prompt = prompt_cache.transpose(0, 2, 1, 3).reshape(GROUPS, PBLOCK, 128)
    tail = decoded_tail_cache.transpose(0, 2, 1, 3).reshape(REQ, TBLOCK, 128)
    ow = o_weight.T
    gu = gate_up.transpose(0, 2, 3, 1).reshape(2, FFL, D)
    dn = down_weight.reshape(FFL, D)

    smem = pl.BlockSpec(memory_space=pltpu.SMEM)
    vmem = pl.BlockSpec(memory_space=pltpu.VMEM)
    hbm = pl.BlockSpec(memory_space=pl.ANY)
    seq_sem = pltpu.SemaphoreType.DMA((N_SEQ,))
    head_sem = pltpu.SemaphoreType.DMA((N_HEAD,))
    out = pl.pallas_call(
        layer_kernel,
        name="layer",
        out_shape=jax.ShapeDtypeStruct((3, 4, D), BF16),
        in_specs=[smem] * 6 + [vmem] * 6 + [hbm] * 6,
        out_specs=vmem,
        scratch_shapes=[
            pltpu.VMEM((REQ, 16, 128), BF16),
            pltpu.VMEM((GROUPS, PBLOCK, 128), BF16),
            pltpu.VMEM((REQ, TBLOCK, 128), BF16),
            pltpu.VMEM((3072, 512), BF16),
            pltpu.VMEM((2 * CH, D), BF16),
            pltpu.VMEM((CH, D), BF16),
            pltpu.VMEM((CH, CH), BF16),
            pltpu.VMEM((REQ, 128), F32),
            pltpu.VMEM((REQ, 128), F32),
            pltpu.VMEM((16, 128), F32),
            pltpu.VMEM((16, 128), F32),
            pltpu.VMEM((16, 3072), F32),
            pltpu.VMEM((REQ, 32, 128), BF16),
            pltpu.VMEM((REQ, 16, 128), BF16),
            pltpu.VMEM((REQ, 16, 128), F32),
            pltpu.VMEM((N_SEQ, 64, 128), BF16),
            pltpu.VMEM((N_SEQ + 1, 64, 128), BF16),
            pltpu.VMEM((N_HEAD, 16, CH), BF16),
            pltpu.VMEM((N_HEAD, 16, CH), BF16),
            pltpu.VMEM((N_SEQ, 16, 128), BF16),
            pltpu.VMEM((N_SEQ, 16, 128), BF16),
            pltpu.VMEM((ROWS, CH), BF16),
            pltpu.VMEM((N_HEAD, ROWS, CH), BF16),
            pltpu.VMEM((N_HEAD, ROWS, CH), BF16),
            pltpu.VMEM((N_HEAD, ROWS, CH), BF16),
            pltpu.VMEM((N_SEQ, 16, 128), BF16),
            pltpu.VMEM((N_SEQ, 16, 128), BF16),
            pltpu.VMEM((16, CH), BF16),
            pltpu.VMEM((N_HEAD, 16, CH), BF16),
            pltpu.SemaphoreType.DMA((6,)),
            pltpu.SemaphoreType.DMA((GROUPS,)),
            seq_sem,
            seq_sem,
            head_sem,
            head_sem,
            seq_sem,
            seq_sem,
            head_sem,
            head_sem,
            head_sem,
            head_sem,
            seq_sem,
            seq_sem,
            head_sem,
            head_sem,
        ],
        compiler_params=pltpu.CompilerParams(
            collective_id=0, has_side_effects=True, vmem_limit_bytes=56 * 1024 * 1024
        ),
    )(
        order,
        rank,
        prompt_group,
        tail_lens,
        prompt_lens,
        sinks,
        jnp.asarray(tables),
        fresh,
        ids,
        route_weights,
        resid,
        gain,
        q,
        prompt,
        tail,
        ow,
        gu,
        dn,
    )
    return out


def solution(mesh):
    return jax.shard_map(
        on_device,
        mesh=mesh,
        in_specs=(
            P(None, None, "head"),
            P("seq", None, "head", None),
            P(None, "seq", "head", None),
            P(None, "seq", "head", None),
            P("head"),
            P(),
            P(),
            P(),
            P("head", None),
            P("seq", None, None),
            P(),
            P(),
            P("seq", None, None),
            P("seq", None, None, "head"),
            P("seq", "head", None),
        ),
        out_specs=P("seq", None, None),
        check_vma=False,
    )
```

```python
import math

import jax
import jax.numpy as jnp
import numpy as np
from jax import lax
from jax.experimental import pallas as pl
from jax.experimental.pallas import tpu as pltpu
from jax.sharding import PartitionSpec as P

MESH = pl.DeviceIdType.MESH
LOW = -1e30
FLOOR = -1e29
F32 = jnp.float32
BF16 = jnp.bfloat16

N_SEQ = 32
N_HEAD = 8
REQ = 96
GROUPS = 8
MEMBERS = 12
PBLOCK = 1024
TBLOCK = 32
D = 2880
CH = 384
LASTC = 192
FFL = 360
ROWS = 96
HALF_PI = (1.5703125, 4.8351287841796875e-4, 3.1391647865048e-7)
NT = (((1,), (1,)), ((), ()))
NN = (((1,), (0,)), ((), ()))
TN = (((0,), (0,)), ((), ()))


def dot(a, b, dims):
    return lax.dot_general(a, b, dims, preferred_element_type=F32)


def iota(shape, axis):
    return lax.broadcasted_iota(jnp.int32, shape, axis)


def turned(x, cosine, sine, lane):
    ahead = pltpu.roll(x, 96, 1)
    behind = pltpu.roll(x, 32, 1)
    partner = jnp.where((lane & 63) < 32, -ahead, behind)
    return x * cosine + partner * sine


def cos_sin(angle):
    k = jnp.floor(angle * (2.0 / math.pi) + 0.5)
    r = angle - k * HALF_PI[0]
    r = r - k * HALF_PI[1]
    r = r - k * HALF_PI[2]
    r2 = r * r
    s = r + r * r2 * (-1.0 / 6 + r2 * (1.0 / 120 + r2 * (-1.0 / 5040 + r2 * (1.0 / 362880))))
    c = 1.0 + r2 * (-0.5 + r2 * (1.0 / 24 + r2 * (-1.0 / 720 + r2 * (1.0 / 40320))))
    quarter = k - 4.0 * jnp.floor(k * 0.25)
    odd = (quarter == 1.0) | (quarter == 3.0)
    cosine = jnp.where(odd, s, c)
    sine = jnp.where(odd, c, s)
    cosine = jnp.where((quarter == 1.0) | (quarter == 2.0), -cosine, cosine)
    sine = jnp.where(quarter >= 2.0, -sine, sine)
    return cosine, sine


def tiles_of(out, peak, lane):
    first, second = out[:16], out[16:]
    values = jnp.where(lane < 64, pltpu.roll(first, 64, 1), second).astype(BF16)
    hi0 = first.astype(BF16).astype(F32)
    hi1 = second.astype(BF16).astype(F32)
    lo0 = first - hi0
    lo1 = second - hi1
    stats = jnp.where(
        lane < 4,
        jnp.where(lane == 0, peak[:16], jnp.where(lane == 1, hi0, jnp.where(lane == 2, lo0, 0.0))),
        jnp.where(
            lane == 4, peak[16:], jnp.where(lane == 5, hi1, jnp.where(lane == 6, lo1, 0.0))
        ),
    )
    return values, jnp.where(lane < 8, stats, 0.0)


def layer_kernel(
    order,
    rank,
    prompt_group,
    tail_lens,
    prompt_lens,
    sinks,
    tables,
    fresh,
    ids,
    routes,
    resid,
    gain,
    q_hbm,
    prompt_hbm,
    tail_hbm,
    ow_hbm,
    gu_hbm,
    dn_hbm,
    out_ref,
    q_v,
    prompt_v,
    tail_v,
    ow_v,
    gu_v,
    dn_v,
    dn_last,
    cos_s,
    sin_s,
    small_s,
    route_s,
    resid_s,
    both_s,
    square_s,
    q_all,
    even_s,
    odd_s,
    even_top,
    odd_top,
    acc_s,
    stat_s,
    msg1,
    rcv1,
    msg2,
    rcv2,
    msg3,
    rcv3,
    msg4,
    rcv4,
    msg5,
    rcv5,
    msg6,
    rcv6,
    msg7,
    rcv7,
    load_sem,
    prompt_sem,
    send1,
    recv1,
    send2,
    recv2,
    send3,
    recv3,
    send4,
    recv4,
    send5,
    recv5,
    send6,
    recv6,
    send7,
    recv7,
):
    me = lax.axis_index("seq")
    head = lax.axis_index("head")
    barrier = pltpu.get_barrier_semaphore()

    def greet_seq(d, carry):
        pl.semaphore_signal(
            barrier, inc=1, device_id=(lax.rem(me + d, N_SEQ), head), device_id_type=MESH
        )
        return carry

    def greet_head(d, carry):
        pl.semaphore_signal(
            barrier, inc=1, device_id=(me, lax.rem(head + d, N_HEAD)), device_id_type=MESH
        )
        return carry

    load_q = pltpu.make_async_copy(q_hbm, q_v, load_sem.at[0])
    load_tail = pltpu.make_async_copy(tail_hbm, tail_v, load_sem.at[1])
    load_ow = pltpu.make_async_copy(ow_hbm, ow_v.at[pl.ds(0, D)], load_sem.at[2])
    load_gate = pltpu.make_async_copy(gu_hbm.at[0], gu_v.at[pl.ds(0, FFL)], load_sem.at[3])
    load_up = pltpu.make_async_copy(gu_hbm.at[1], gu_v.at[pl.ds(CH, FFL)], load_sem.at[5])
    load_dn = pltpu.make_async_copy(dn_hbm, dn_v.at[pl.ds(0, FFL)], load_sem.at[4])
    load_q.start()
    load_tail.start()

    def load_prompt(g):
        return pltpu.make_async_copy(prompt_hbm.at[g], prompt_v.at[g], prompt_sem.at[g])

    for g in range(GROUPS):
        load_prompt(g).start()
    load_ow.start()
    load_gate.start()
    load_up.start()
    load_dn.start()
    lax.fori_loop(1, N_SEQ, greet_seq, 0)
    lax.fori_loop(1, N_HEAD, greet_head, 0)

    lane = iota((16, 128), 1)
    row = iota((16, 128), 0)

    freq = tables[0:1, :]
    ct = tables[8:24, :]
    st = tables[24:40, :]

    def place(r):
        return (prompt_lens[prompt_group[r]] + tail_lens[r]).astype(F32)

    def put_angle(i, carry):
        cos_s[pl.ds(i, 1), :] = freq * place(order[i])
        return carry

    lax.fori_loop(0, REQ, put_angle, 0, unroll=8)
    cosine, sine = cos_sin(cos_s[...])
    cos_s[...] = cosine
    sin_s[...] = sine

    load_q.wait()

    def rotate_one(i, carry):
        r = order[i]
        x = q_v[r].astype(F32)
        c0 = cos_s[pl.ds(i, 1), :]
        s0 = sin_s[pl.ds(i, 1), :]
        y = turned(x, c0 * ct - s0 * st, s0 * ct + c0 * st, lane)
        y = y.astype(BF16).astype(F32) * 0.125
        q_all[i, 0:16, :] = jnp.where(lane < 64, y, 0.0).astype(BF16)
        q_all[i, 16:32, :] = jnp.where(
            lane < 64, pltpu.roll(y, 64, 1), 0.0
        ).astype(BF16)
        return carry

    lax.fori_loop(0, REQ, rotate_one, 0, unroll=4)
    load_tail.wait()

    key_col = iota((1, PBLOCK), 1) + me * PBLOCK
    col128 = iota((1, 128), 1)
    upper = (iota((1, 128), 1) >= 64).astype(F32).astype(BF16)
    lower = (iota((1, 128), 1) < 64).astype(F32).astype(BF16)
    same_req = (iota((128, 128), 0) >> 5) == (iota((128, 128), 1) >> 5)

    def tails(g):
        members = [order[g * MEMBERS + i] for i in range(MEMBERS)]
        return [
            jnp.concatenate([tail_v[r] for r in members[4 * b : 4 * b + 4]], axis=0)
            for b in range(3)
        ], members

    def scores(g, buf, tops):
        kv = prompt_v[g]
        bias = jnp.where(key_col < prompt_lens[g], 0.0, LOW)
        q = q_all[pl.ds(g * MEMBERS, MEMBERS)].reshape(MEMBERS * 32, 128)
        high = None
        for h in range(4):
            cols = slice(256 * h, 256 * h + 256)
            part = dot(q, kv[cols], NT) + bias[:, cols]
            buf[:, cols] = part
            part = jnp.maximum(part[:, :128], part[:, 128:])
            high = part if high is None else jnp.maximum(high, part)
        keys, members = tails(g)
        for b in range(3):
            rows = slice(128 * b, 128 * b + 128)
            limit = jnp.zeros((1, 128), jnp.int32)
            for i in range(4):
                limit = jnp.where((col128 >> 5) == i, tail_lens[members[4 * b + i]], limit)
            seen = same_req & (((col128 & 31) + me * TBLOCK) < limit)
            part = jnp.where(seen, dot(q[rows], keys[b], NT), LOW)
            buf[rows, PBLOCK : PBLOCK + 128] = part
            top = jnp.max(jnp.maximum(high[rows], part), axis=1, keepdims=True)
            top = jnp.maximum(top, FLOOR).astype(BF16).astype(F32)
            tops[rows, :] = jnp.broadcast_to(top, (128, 128))

    def weigh(g, buf, tops):
        first = g * MEMBERS
        kv = prompt_v[g]
        vx = kv * upper + lower
        keys, members = tails(g)
        peaks = tops[...]
        w = jnp.concatenate(
            [
                jnp.exp(buf[:, 128 * h : 128 * h + 128] - peaks).astype(BF16)
                for h in range(PBLOCK // 128)
            ],
            axis=1,
        )
        w2 = jnp.exp(buf[:, PBLOCK : PBLOCK + 128] - peaks).astype(BF16)
        whole = dot(w, vx, NN)
        for b in range(3):
            rows = slice(128 * b, 128 * b + 128)
            peak = peaks[rows]
            o = whole[rows] + dot(w2[rows], keys[b] * upper + lower, NN)
            for i in range(4):
                values, stats = tiles_of(o[32 * i : 32 * i + 32], peak[32 * i : 32 * i + 32], lane)
                acc_s[first + 4 * b + i] = values
                stat_s[first + 4 * b + i] = stats

    for g in range(GROUPS):
        load_prompt(g).wait()
    scores(0, even_s, even_top)

    def two_groups(k, carry):
        g = 2 * k
        scores(g + 1, odd_s, odd_top)
        weigh(g, even_s, even_top)
        scores(jnp.minimum(g + 2, GROUPS - 1), even_s, even_top)
        weigh(g + 1, odd_s, odd_top)
        return carry

    lax.fori_loop(0, GROUPS // 2, two_groups, 0)

    pl.semaphore_wait(barrier, N_SEQ - 1 + N_HEAD - 1)

    def pack(dst, slot, o):
        total = jnp.zeros((16, 128), F32)
        for i in range(3):
            k = rank[3 * o + i]
            dst[slot, 16 * i : 16 * i + 16, :] = acc_s[k]
            piece = stat_s[k]
            total = total + (piece if i == 0 else pltpu.roll(piece, 8 * i, 1))
        dst[slot, 48:64, :] = total.astype(BF16)

    def seq_copy(msg, rcv, send, recv, to):
        return pltpu.make_async_remote_copy(
            src_ref=msg.at[to],
            dst_ref=rcv.at[me],
            send_sem=send.at[to],
            recv_sem=recv.at[me],
            device_id=(to, head),
            device_id_type=MESH,
        )

    def seq_arrival(msg, rcv, send, recv, source):
        return pltpu.make_async_remote_copy(
            src_ref=msg.at[source],
            dst_ref=rcv.at[source],
            send_sem=send.at[source],
            recv_sem=recv.at[source],
            device_id=(source, head),
            device_id_type=MESH,
        )

    def head_copy(msg, slot, rcv, send, recv, to):
        return pltpu.make_async_remote_copy(
            src_ref=msg if slot is None else msg.at[slot],
            dst_ref=rcv.at[head],
            send_sem=send.at[to],
            recv_sem=recv.at[head],
            device_id=(me, to),
            device_id_type=MESH,
        )

    def head_arrival(msg, slot, rcv, send, recv, source):
        return pltpu.make_async_remote_copy(
            src_ref=msg if slot is None else msg.at[slot],
            dst_ref=rcv.at[source],
            send_sem=send.at[source],
            recv_sem=recv.at[source],
            device_id=(me, source),
            device_id_type=MESH,
        )

    def others(count, mine, body):
        def step(d, carry):
            body(lax.rem(mine + d, count))
            return carry

        lax.fori_loop(1, count, step, 0)

    core = lax.rem(head, 2)
    chip = head // 2
    near = chip + 1 - 2 * lax.rem(chip, 2)
    peers = [2 * chip + 1 - core]
    for far in (near, 3 - chip, lax.rem(chip + 2, 4)):
        peers += [2 * far + core, 2 * far + 1 - core]

    def send_partials(o):
        pack(msg1, o, o)
        seq_copy(msg1, rcv1, send1, recv1, o).start()

    others(N_SEQ, me, send_partials)
    pack(rcv1, me, me)

    angle = jnp.zeros((16, 128), F32)
    for i in range(3):
        angle = jnp.where((row >> 2) == i, freq * place(me * 3 + i), angle)
        small_s[4 * i : 4 * i + 4, :] = fresh[i].astype(F32)
    base_c, base_s = cos_sin(angle)
    small_s[12:16, :] = jnp.zeros((4, 128), F32)
    kv_new = small_s[...]
    key_new = turned(kv_new, base_c * ct - base_s * st, base_s * ct + base_c * st, lane)
    kn = jnp.where(lane < 64, key_new, kv_new).astype(BF16)
    vn = jnp.where(lane < 64, 1.0, kv_new).astype(BF16)
    fresh_stats = jnp.zeros((16, 128), F32)
    srow = iota((32, 16), 0)
    scol = iota((32, 16), 1)
    for i in range(3):
        k = rank[3 * me + i]
        q = q_all[k]
        seen = ((scol >> 2) == i) & ((scol & 3) <= (srow & 3))
        s = jnp.where(seen, dot(q, kn, NT), LOW)
        peak = jnp.max(s, axis=1, keepdims=True).astype(BF16).astype(F32)
        w = jnp.exp(s - peak).astype(BF16)
        values, stats = tiles_of(dot(w, vn, NN), peak, lane)
        rcv1[N_SEQ, 16 * i : 16 * i + 16, :] = values
        fresh_stats = fresh_stats + (stats if i == 0 else pltpu.roll(stats, 8 * i, 1))
    rcv1[N_SEQ, 48:64, :] = fresh_stats.astype(BF16)

    sink = jnp.zeros((16, 128), F32)
    for j in range(8):
        here = ((row >> 2) == (j >> 1)) & ((lane >> 6) == (j & 1))
        sink = jnp.where(here, sinks[j], sink)

    wide_lane = iota((16, 512), 1)
    expert = wide_lane >> 4
    place = wide_lane & 15
    pick = (place >= 3).astype(jnp.int32) + (place >= 6).astype(jnp.int32)
    tile = place - 3 * pick
    own = (iota((REQ, 384), 0) == me * 3 + (iota((REQ, 384), 1) >> 7)).astype(F32).astype(BF16)
    flat_ids = jnp.concatenate([ids[t] for t in range(4)], axis=0).astype(F32).astype(BF16)
    own_ids = dot(flat_ids, own, NN).astype(BF16)
    xr = iota((64, 16), 0)
    xc = iota((64, 16), 1)
    names = jnp.full((64, 128), -1.0, F32) * ((iota((64, 128), 0) & 15) >= 12).astype(F32)
    for i in range(3):
        take = (xc == (xr & 3) * 4 + (xr >> 4)) & (((xr & 15) >> 2) == i)
        names = names + dot(
            take.astype(F32).astype(BF16), own_ids[:, 128 * i : 128 * i + 128], NN
        )
    names = jnp.concatenate([names] * 4, axis=1)
    route_s[...] = jnp.zeros((16, 128), F32)
    for i in range(3):
        route_s[4 * i : 4 * i + 4, 0:4] = routes[i]
    named = jnp.zeros((16, 512), F32)
    share = jnp.zeros((16, 512), F32)
    for k in range(4):
        hit = names[16 * k : 16 * k + 16] == expert.astype(F32)
        named = named + jnp.where(hit, 1.0, 0.0)
        share = share + jnp.where(hit, route_s[:, k : k + 1], 0.0)
    below = (iota((16, 16), 1) < iota((16, 16), 0)).astype(F32).astype(BF16)
    earlier = dot(below, named.astype(BF16), NN)
    chosen = (named > 0.5) & (earlier == pick.astype(F32)) & (place < 9)
    chosen_tile = [chosen & (tile == c) for c in range(3)]
    select = jnp.concatenate([jnp.where(m, 1.0, 0.0) for m in chosen_tile], axis=0)
    select = select.T.astype(BF16)
    give = jnp.concatenate([jnp.where(m, share, 0.0) for m in chosen_tile], axis=0)
    give_hi = give.astype(BF16)
    give_lo = (give - give_hi.astype(F32)).astype(BF16)

    trow = iota((288, 512), 0)
    tcol = iota((288, 512), 1)
    ttile = (trow >= 96).astype(jnp.int32) + (trow >= 192).astype(jnp.int32)
    trest = trow - 96 * ttile
    spread = (
        ((trest & 31) == (tcol >> 4)) & ((tcol & 15) == 3 * (trest >> 5) + ttile)
    ).astype(F32).astype(BF16)

    ucol = iota((512, 288), 1)
    urow = iota((512, 288), 0)
    utile = (ucol >= 96).astype(jnp.int32) + (ucol >= 192).astype(jnp.int32)
    urest = ucol - 96 * utile
    gather = (
        ((urest & 31) == (urow >> 4)) & ((urow & 15) == 3 * (urest >> 5) + utile)
    ).astype(F32).astype(BF16)
    resid_s[...] = jnp.zeros((16, 3072), F32)
    for i in range(3):
        resid_s[4 * i : 4 * i + 4, 0:D] = resid[i].astype(F32)

    load_ow.wait()
    ow_v[pl.ds(D, 3072 - D), :] = jnp.zeros((3072 - D, 512), BF16)
    load_gate.wait()
    load_up.wait()
    load_dn.wait()
    gu_v[FFL:CH, :] = jnp.zeros((CH - FFL, D), BF16)
    gu_v[CH + FFL : 2 * CH, :] = jnp.zeros((CH - FFL, D), BF16)
    dn_v[FFL:CH, :] = jnp.zeros((CH - FFL, D), BF16)
    dn_last[:, 0:LASTC] = dn_v[:, 7 * CH : 7 * CH + LASTC]
    dn_last[:, LASTC:CH] = jnp.zeros((CH, CH - LASTC), BF16)

    others(N_SEQ, me, lambda s: seq_arrival(msg1, rcv1, send1, recv1, s).wait_recv())

    stat_rows = rcv1[:, 48:64, :].reshape((N_SEQ + 1) * 16, 128)
    er = iota((128, 384), 0)
    ec = iota((128, 384), 1)
    attended = []
    for i in range(3):
        spot = 8 * i + 4 * ((ec & 127) >> 6) + (ec >> 7)
        expand = (er == spot).astype(F32).astype(BF16)
        wide = dot(stat_rows, expand, NN)
        peaks = wide[:, 0:128].reshape(N_SEQ + 1, 16, 128)
        totals = (wide[:, 128:256] + wide[:, 256:384]).reshape(N_SEQ + 1, 16, 128)
        top = jnp.maximum(jnp.max(peaks, axis=0), sink)
        factor = jnp.exp(peaks - top[None])
        values = rcv1[:, 16 * i : 16 * i + 16, :].astype(F32)
        num = jnp.sum(values * factor, axis=0)
        den = jnp.sum(totals * factor, axis=0) + jnp.exp(sink - top)
        attended.append((num / den).astype(BF16))
    att = jnp.concatenate(attended, axis=0)
    rr = iota((64, 48), 0)
    rc = iota((64, 48), 1)
    want = ((rr & 15) >> 2) * 16 + (rr >> 4) * 4 + (rr & 3)
    regroup = (rc == want).astype(F32).astype(BF16)
    mixed = dot(regroup, att, NN).astype(BF16)
    flat = jnp.concatenate([mixed[16 * p : 16 * p + 16] for p in range(4)], axis=1)

    def project(j):
        rows = ow_v[pl.ds(pl.multiple_of(j * CH, CH), CH), :]
        return dot(flat, rows, NT).astype(BF16)

    def send_projection(j):
        msg2[j] = project(j)
        head_copy(msg2, j, rcv2, send2, recv2, j).start()

    others(N_HEAD, head, send_projection)
    rcv2[head] = project(head)
    others(N_HEAD, head, lambda s: head_arrival(msg2, s, rcv2, send2, recv2, s).wait_recv())
    total = resid_s[:, pl.ds(pl.multiple_of(head * CH, CH), CH)]
    total = total + jnp.sum(rcv2[...].astype(F32), axis=0)
    hidden = total.astype(BF16)
    hidden_rows = jnp.concatenate([hidden[:, 128 * c : 128 * c + 128] for c in range(3)], axis=0)

    msg3[...] = dot(select, hidden_rows, NN).astype(BF16).reshape(N_SEQ, 16, 128)
    others(N_SEQ, me, lambda o: seq_copy(msg3, rcv3, send3, recv3, o).start())
    rcv3[me] = msg3[me]
    others(N_SEQ, me, lambda s: seq_arrival(msg3, rcv3, send3, recv3, s).wait_recv())
    got = dot(spread, rcv3[...].reshape(512, 128), NN).astype(BF16)
    mine = jnp.concatenate([got[96 * c : 96 * c + 96] for c in range(3)], axis=1)
    msg4[...] = mine
    others(N_HEAD, head, lambda o: head_copy(msg4, None, rcv4, send4, recv4, o).start())
    rcv4[head] = mine

    both_s[...] = jnp.zeros((ROWS, 2 * CH), F32)
    square_s[...] = jnp.zeros((ROWS, 128), F32)

    def take_chunk(j, weights, width, gains):
        x = rcv4[j, :, 0:width].astype(F32)
        square_s[...] += jnp.broadcast_to(jnp.sum(x * x, axis=1, keepdims=True), (ROWS, 128))
        both_s[...] += dot((x * gains).astype(BF16), weights, NT)

    def use_chunk(j):
        @pl.when(j < N_HEAD - 1)
        def _():
            cols = pl.ds(pl.multiple_of(jnp.minimum(j, N_HEAD - 2) * CH, CH), CH)
            take_chunk(j, gu_v[:, cols], CH, gain[:, cols])

        @pl.when(j == N_HEAD - 1)
        def _():
            cols = slice((N_HEAD - 1) * CH, D)
            take_chunk(N_HEAD - 1, gu_v[:, cols], LASTC, gain[:, cols])

    use_chunk(head)
    for j in peers:
        head_arrival(msg4, None, rcv4, send4, recv4, j).wait_recv()
        use_chunk(j)
    both = both_s[...]
    square = square_s[:, 0:1]
    scale = lax.rsqrt(square * (1.0 / D) + 1e-05)
    g = jnp.minimum(both[:, 0:CH] * scale, 7.0)
    u = jnp.clip(both[:, CH : 2 * CH] * scale, -7.0, 7.0)
    active = ((u + 1.0) * g * jax.nn.sigmoid(1.702 * g)).astype(BF16)

    def send_expert(d, carry):
        j = lax.rem(head + d, N_HEAD)
        col = pl.multiple_of(jnp.minimum(j, N_HEAD - 2) * CH, CH)

        @pl.when(j < N_HEAD - 1)
        def _():
            msg5[j] = dot(active, dn_v[:, pl.ds(col, CH)], NN).astype(BF16)

        @pl.when(j == N_HEAD - 1)
        def _():
            msg5[j] = dot(active, dn_last[...], NN).astype(BF16)

        @pl.when(d < N_HEAD)
        def _():
            head_copy(msg5, j, rcv5, send5, recv5, j).start()

        return carry

    lax.fori_loop(1, N_HEAD + 1, send_expert, 0)
    rcv5[head] = msg5[head]
    others(N_HEAD, head, lambda s: head_arrival(msg5, s, rcv5, send5, recv5, s).wait_recv())
    summed = jnp.sum(rcv5[...].astype(F32), axis=0).astype(BF16)
    summed_rows = jnp.concatenate([summed[:, 128 * c : 128 * c + 128] for c in range(3)], axis=0)
    msg6[...] = dot(gather, summed_rows, NN).astype(BF16).reshape(N_SEQ, 16, 128)
    others(N_SEQ, me, lambda o: seq_copy(msg6, rcv6, send6, recv6, o).start())
    rcv6[me] = msg6[me]
    others(N_SEQ, me, lambda s: seq_arrival(msg6, rcv6, send6, recv6, s).wait_recv())
    back = rcv6[...].reshape(512, 128)
    added = dot(give_hi, back, NN) + dot(give_lo, back, NN)
    result = hidden_rows.astype(F32) + added
    result = jnp.concatenate([result[16 * c : 16 * c + 16] for c in range(3)], axis=1).astype(BF16)
    msg7[...] = result
    others(N_HEAD, head, lambda o: head_copy(msg7, None, rcv7, send7, recv7, o).start())
    rcv7[head] = result
    others(N_HEAD, head, lambda s: head_arrival(msg7, None, rcv7, send7, recv7, s).wait_recv())
    for i in range(3):
        for j in range(N_HEAD):
            width = CH if j < N_HEAD - 1 else LASTC
            out_ref[i, :, j * CH : j * CH + width] = rcv7[j, 4 * i : 4 * i + 4, 0:width]

    for msg, rcv, send, recv in (
        (msg1, rcv1, send1, recv1),
        (msg3, rcv3, send3, recv3),
        (msg6, rcv6, send6, recv6),
    ):
        others(N_SEQ, me, lambda o: seq_copy(msg, rcv, send, recv, o).wait_send())
    for msg, whole, rcv, send, recv in (
        (msg2, False, rcv2, send2, recv2),
        (msg4, True, rcv4, send4, recv4),
        (msg5, False, rcv5, send5, recv5),
        (msg7, True, rcv7, send7, recv7),
    ):
        others(
            N_HEAD,
            head,
            lambda o: head_copy(msg, None if whole else o, rcv, send, recv, o).wait_send(),
        )


def on_device(
    new_query,
    fresh_key_value,
    prompt_cache,
    decoded_tail_cache,
    sinks,
    prompt_group,
    prompt_lens,
    tail_lens,
    o_weight,
    resid,
    norm_gain,
    expert_ids,
    route_weights,
    gate_up,
    down_weight,
):
    r = jnp.arange(REQ, dtype=jnp.int32)
    mine, other = prompt_group[:, None], prompt_group[None, :]
    ahead = (other < mine) | ((other == mine) & (r[None, :] < r[:, None]))
    rank = jnp.sum(ahead.astype(jnp.int32), axis=1)
    order = jnp.sum(jnp.where(rank[None, :] == r[:, None], r[None, :], 0), axis=1)
    freq = np.exp(np.arange(32) * (-2.0 * math.log(150000.0) / 64))
    freq = np.tile(freq.astype(np.float32), 4)
    step_angle = (np.arange(16) % 4)[:, None] * freq[None, :].astype(np.float64)
    tables = np.zeros((40, 128), np.float32)
    tables[0] = freq
    tables[8:24] = np.cos(step_angle)
    tables[24:40] = np.sin(step_angle)
    fresh = fresh_key_value.transpose(0, 2, 1, 3).reshape(3, 4, 128)
    ids = expert_ids.transpose(1, 2, 0)
    gain = norm_gain.reshape(1, D)
    q = new_query.reshape(REQ, 4, 4, 128).transpose(0, 2, 1, 3).reshape(REQ, 16, 128)
    prompt = prompt_cache.transpose(0, 2, 1, 3).reshape(GROUPS, PBLOCK, 128)
    tail = decoded_tail_cache.transpose(0, 2, 1, 3).reshape(REQ, TBLOCK, 128)
    ow = o_weight.T
    gu = gate_up.transpose(0, 2, 3, 1).reshape(2, FFL, D)
    dn = down_weight.reshape(FFL, D)

    smem = pl.BlockSpec(memory_space=pltpu.SMEM)
    vmem = pl.BlockSpec(memory_space=pltpu.VMEM)
    hbm = pl.BlockSpec(memory_space=pl.ANY)
    seq_sem = pltpu.SemaphoreType.DMA((N_SEQ,))
    head_sem = pltpu.SemaphoreType.DMA((N_HEAD,))
    out = pl.pallas_call(
        layer_kernel,
        name="layer",
        out_shape=jax.ShapeDtypeStruct((3, 4, D), BF16),
        in_specs=[smem] * 6 + [vmem] * 6 + [hbm] * 6,
        out_specs=vmem,
        scratch_shapes=[
            pltpu.VMEM((REQ, 16, 128), BF16),
            pltpu.VMEM((GROUPS, PBLOCK, 128), BF16),
            pltpu.VMEM((REQ, TBLOCK, 128), BF16),
            pltpu.VMEM((3072, 512), BF16),
            pltpu.VMEM((2 * CH, D), BF16),
            pltpu.VMEM((CH, D), BF16),
            pltpu.VMEM((CH, CH), BF16),
            pltpu.VMEM((REQ, 128), F32),
            pltpu.VMEM((REQ, 128), F32),
            pltpu.VMEM((16, 128), F32),
            pltpu.VMEM((16, 128), F32),
            pltpu.VMEM((16, 3072), F32),
            pltpu.VMEM((ROWS, 2 * CH), F32),
            pltpu.VMEM((ROWS, 128), F32),
            pltpu.VMEM((REQ, 32, 128), BF16),
            pltpu.VMEM((MEMBERS * 32, PBLOCK + 128), F32),
            pltpu.VMEM((MEMBERS * 32, PBLOCK + 128), F32),
            pltpu.VMEM((MEMBERS * 32, 128), F32),
            pltpu.VMEM((MEMBERS * 32, 128), F32),
            pltpu.VMEM((REQ, 16, 128), BF16),
            pltpu.VMEM((REQ, 16, 128), F32),
            pltpu.VMEM((N_SEQ, 64, 128), BF16),
            pltpu.VMEM((N_SEQ + 1, 64, 128), BF16),
            pltpu.VMEM((N_HEAD, 16, CH), BF16),
            pltpu.VMEM((N_HEAD, 16, CH), BF16),
            pltpu.VMEM((N_SEQ, 16, 128), BF16),
            pltpu.VMEM((N_SEQ, 16, 128), BF16),
            pltpu.VMEM((ROWS, CH), BF16),
            pltpu.VMEM((N_HEAD, ROWS, CH), BF16),
            pltpu.VMEM((N_HEAD, ROWS, CH), BF16),
            pltpu.VMEM((N_HEAD, ROWS, CH), BF16),
            pltpu.VMEM((N_SEQ, 16, 128), BF16),
            pltpu.VMEM((N_SEQ, 16, 128), BF16),
            pltpu.VMEM((16, CH), BF16),
            pltpu.VMEM((N_HEAD, 16, CH), BF16),
            pltpu.SemaphoreType.DMA((6,)),
            pltpu.SemaphoreType.DMA((GROUPS,)),
            seq_sem,
            seq_sem,
            head_sem,
            head_sem,
            seq_sem,
            seq_sem,
            head_sem,
            head_sem,
            head_sem,
            head_sem,
            seq_sem,
            seq_sem,
            head_sem,
            head_sem,
        ],
        compiler_params=pltpu.CompilerParams(
            collective_id=0, has_side_effects=True, vmem_limit_bytes=56 * 1024 * 1024
        ),
    )(
        order,
        rank,
        prompt_group,
        tail_lens,
        prompt_lens,
        sinks,
        jnp.asarray(tables),
        fresh,
        ids,
        route_weights,
        resid,
        gain,
        q,
        prompt,
        tail,
        ow,
        gu,
        dn,
    )
    return out


def solution(mesh):
    return jax.shard_map(
        on_device,
        mesh=mesh,
        in_specs=(
            P(None, None, "head"),
            P("seq", None, "head", None),
            P(None, "seq", "head", None),
            P(None, "seq", "head", None),
            P("head"),
            P(),
            P(),
            P(),
            P("head", None),
            P("seq", None, None),
            P(),
            P(),
            P("seq", None, None),
            P("seq", None, None, "head"),
            P("seq", "head", None),
        ),
        out_specs=P("seq", None, None),
        check_vma=False,
    )
```

```python
import math

import jax
import jax.numpy as jnp
import numpy as np
from jax import lax
from jax.experimental import pallas as pl
from jax.experimental.pallas import tpu as pltpu
from jax.sharding import PartitionSpec as P

MESH = pl.DeviceIdType.MESH
LOW = -1e30
FLOOR = -1e29
F32 = jnp.float32
BF16 = jnp.bfloat16

N_SEQ = 32
N_HEAD = 8
REQ = 96
GROUPS = 8
MEMBERS = 12
PBLOCK = 1024
TBLOCK = 32
D = 2880
CH = 384
LASTC = 192
FFL = 360
ROWS = 96
HALF_PI = (1.5703125, 4.8351287841796875e-4, 3.1391647865048e-7)
NT = (((1,), (1,)), ((), ()))
NN = (((1,), (0,)), ((), ()))
TN = (((0,), (0,)), ((), ()))


def dot(a, b, dims):
    return lax.dot_general(a, b, dims, preferred_element_type=F32)


def iota(shape, axis):
    return lax.broadcasted_iota(jnp.int32, shape, axis)


def turned(x, cosine, sine, lane):
    ahead = pltpu.roll(x, 96, 1)
    behind = pltpu.roll(x, 32, 1)
    partner = jnp.where((lane & 63) < 32, -ahead, behind)
    return x * cosine + partner * sine


def cos_sin(angle):
    k = jnp.floor(angle * (2.0 / math.pi) + 0.5)
    r = angle - k * HALF_PI[0]
    r = r - k * HALF_PI[1]
    r = r - k * HALF_PI[2]
    r2 = r * r
    s = r + r * r2 * (-1.0 / 6 + r2 * (1.0 / 120 + r2 * (-1.0 / 5040 + r2 * (1.0 / 362880))))
    c = 1.0 + r2 * (-0.5 + r2 * (1.0 / 24 + r2 * (-1.0 / 720 + r2 * (1.0 / 40320))))
    quarter = k - 4.0 * jnp.floor(k * 0.25)
    odd = (quarter == 1.0) | (quarter == 3.0)
    cosine = jnp.where(odd, s, c)
    sine = jnp.where(odd, c, s)
    cosine = jnp.where((quarter == 1.0) | (quarter == 2.0), -cosine, cosine)
    sine = jnp.where(quarter >= 2.0, -sine, sine)
    return cosine, sine


def tiles_of(out, peak, lane):
    first, second = out[:16], out[16:]
    values = jnp.where(lane < 64, pltpu.roll(first, 64, 1), second).astype(BF16)
    hi0 = first.astype(BF16).astype(F32)
    hi1 = second.astype(BF16).astype(F32)
    lo0 = first - hi0
    lo1 = second - hi1
    stats = jnp.where(
        lane < 4,
        jnp.where(lane == 0, peak[:16], jnp.where(lane == 1, hi0, jnp.where(lane == 2, lo0, 0.0))),
        jnp.where(
            lane == 4, peak[16:], jnp.where(lane == 5, hi1, jnp.where(lane == 6, lo1, 0.0))
        ),
    )
    return values, jnp.where(lane < 8, stats, 0.0)


def layer_kernel(
    order,
    rank,
    prompt_group,
    tail_lens,
    prompt_lens,
    sinks,
    tables,
    fresh,
    ids,
    routes,
    resid,
    gain,
    q_hbm,
    prompt_hbm,
    tail_hbm,
    ow_hbm,
    gu_hbm,
    dn_hbm,
    out_ref,
    q_v,
    prompt_v,
    tail_v,
    ow_v,
    gu_v,
    dn_v,
    dn_w,
    gu_w,
    gain_s,
    cos_s,
    sin_s,
    small_s,
    route_s,
    resid_s,
    both_s,
    square_s,
    q_all,
    even_s,
    odd_s,
    even_top,
    odd_top,
    acc_s,
    stat_s,
    msg1,
    rcv1,
    msg2,
    rcv2,
    msg3,
    rcv3,
    msg4,
    rcv4,
    msg_p,
    rcv_p,
    msg5,
    rcv5,
    msg6,
    rcv6,
    msg7,
    rcv7,
    load_sem,
    prompt_sem,
    send1,
    recv1,
    send2,
    recv2,
    send3,
    recv3,
    send4,
    recv4,
    send_f,
    send_p,
    recv_p,
    send5,
    recv5,
    send6,
    recv6,
    send7,
    recv7,
):
    me = lax.axis_index("seq")
    head = lax.axis_index("head")
    barrier = pltpu.get_barrier_semaphore()

    def greet_seq(d, carry):
        pl.semaphore_signal(
            barrier, inc=1, device_id=(lax.rem(me + d, N_SEQ), head), device_id_type=MESH
        )
        return carry

    def greet_head(d, carry):
        pl.semaphore_signal(
            barrier, inc=1, device_id=(me, lax.rem(head + d, N_HEAD)), device_id_type=MESH
        )
        return carry

    load_q = pltpu.make_async_copy(q_hbm, q_v, load_sem.at[0])
    load_tail = pltpu.make_async_copy(tail_hbm, tail_v, load_sem.at[1])
    load_ow = pltpu.make_async_copy(ow_hbm, ow_v.at[pl.ds(0, D)], load_sem.at[2])
    load_gate = pltpu.make_async_copy(gu_hbm.at[0], gu_v.at[pl.ds(0, FFL)], load_sem.at[3])
    load_up = pltpu.make_async_copy(gu_hbm.at[1], gu_v.at[pl.ds(CH, FFL)], load_sem.at[5])
    load_dn = pltpu.make_async_copy(dn_hbm, dn_v.at[pl.ds(0, FFL)], load_sem.at[4])
    load_q.start()
    load_tail.start()

    def load_prompt(g):
        return pltpu.make_async_copy(prompt_hbm.at[g], prompt_v.at[g], prompt_sem.at[g])

    for g in range(GROUPS):
        load_prompt(g).start()
    load_ow.start()
    load_gate.start()
    load_up.start()
    load_dn.start()
    lax.fori_loop(1, N_SEQ, greet_seq, 0)
    lax.fori_loop(1, N_HEAD, greet_head, 0)

    lane = iota((16, 128), 1)
    row = iota((16, 128), 0)

    freq = tables[0:1, :]
    ct = tables[8:24, :]
    st = tables[24:40, :]

    def place(r):
        return (prompt_lens[prompt_group[r]] + tail_lens[r]).astype(F32)

    def put_angle(i, carry):
        cos_s[pl.ds(i, 1), :] = freq * place(order[i])
        return carry

    lax.fori_loop(0, REQ, put_angle, 0, unroll=8)
    cosine, sine = cos_sin(cos_s[...])
    cos_s[...] = cosine
    sin_s[...] = sine

    load_q.wait()

    def rotate_one(i, carry):
        r = order[i]
        x = q_v[r].astype(F32)
        c0 = cos_s[pl.ds(i, 1), :]
        s0 = sin_s[pl.ds(i, 1), :]
        y = turned(x, c0 * ct - s0 * st, s0 * ct + c0 * st, lane)
        y = y.astype(BF16).astype(F32) * 0.125
        q_all[i, 0:16, :] = jnp.where(lane < 64, y, 0.0).astype(BF16)
        q_all[i, 16:32, :] = jnp.where(
            lane < 64, pltpu.roll(y, 64, 1), 0.0
        ).astype(BF16)
        return carry

    lax.fori_loop(0, REQ, rotate_one, 0, unroll=4)
    load_tail.wait()

    key_col = iota((1, PBLOCK), 1) + me * PBLOCK
    col128 = iota((1, 128), 1)
    upper = (iota((1, 128), 1) >= 64).astype(F32).astype(BF16)
    lower = (iota((1, 128), 1) < 64).astype(F32).astype(BF16)
    same_req = (iota((128, 128), 0) >> 5) == (iota((128, 128), 1) >> 5)

    def tails(g):
        members = [order[g * MEMBERS + i] for i in range(MEMBERS)]
        return [
            jnp.concatenate([tail_v[r] for r in members[4 * b : 4 * b + 4]], axis=0)
            for b in range(3)
        ], members

    def scores(g, buf, tops):
        kv = prompt_v[g]
        bias = jnp.where(key_col < prompt_lens[g], 0.0, LOW)
        q = q_all[pl.ds(g * MEMBERS, MEMBERS)].reshape(MEMBERS * 32, 128)
        high = None
        for h in range(4):
            cols = slice(256 * h, 256 * h + 256)
            part = dot(q, kv[cols], NT) + bias[:, cols]
            buf[:, cols] = part
            part = jnp.maximum(part[:, :128], part[:, 128:])
            high = part if high is None else jnp.maximum(high, part)
        keys, members = tails(g)
        for b in range(3):
            rows = slice(128 * b, 128 * b + 128)
            limit = jnp.zeros((1, 128), jnp.int32)
            for i in range(4):
                limit = jnp.where((col128 >> 5) == i, tail_lens[members[4 * b + i]], limit)
            seen = same_req & (((col128 & 31) + me * TBLOCK) < limit)
            part = jnp.where(seen, dot(q[rows], keys[b], NT), LOW)
            buf[rows, PBLOCK : PBLOCK + 128] = part
            top = jnp.max(jnp.maximum(high[rows], part), axis=1, keepdims=True)
            top = jnp.maximum(top, FLOOR).astype(BF16).astype(F32)
            tops[rows, :] = jnp.broadcast_to(top, (128, 128))

    def weigh(g, buf, tops):
        first = g * MEMBERS
        kv = prompt_v[g]
        vx = kv * upper + lower
        keys, members = tails(g)
        peaks = tops[...]
        w = jnp.concatenate(
            [
                jnp.exp(buf[:, 128 * h : 128 * h + 128] - peaks).astype(BF16)
                for h in range(PBLOCK // 128)
            ],
            axis=1,
        )
        w2 = jnp.exp(buf[:, PBLOCK : PBLOCK + 128] - peaks).astype(BF16)
        whole = dot(w, vx, NN)
        for b in range(3):
            rows = slice(128 * b, 128 * b + 128)
            peak = peaks[rows]
            o = whole[rows] + dot(w2[rows], keys[b] * upper + lower, NN)
            for i in range(4):
                values, stats = tiles_of(o[32 * i : 32 * i + 32], peak[32 * i : 32 * i + 32], lane)
                acc_s[first + 4 * b + i] = values
                stat_s[first + 4 * b + i] = stats

    for g in range(GROUPS):
        load_prompt(g).wait()
    scores(0, even_s, even_top)

    def two_groups(k, carry):
        g = 2 * k
        scores(g + 1, odd_s, odd_top)
        weigh(g, even_s, even_top)
        scores(jnp.minimum(g + 2, GROUPS - 1), even_s, even_top)
        weigh(g + 1, odd_s, odd_top)
        return carry

    lax.fori_loop(0, GROUPS // 2, two_groups, 0)

    pl.semaphore_wait(barrier, N_SEQ - 1 + N_HEAD - 1)

    def pack(dst, slot, o):
        total = jnp.zeros((16, 128), F32)
        for i in range(3):
            k = rank[3 * o + i]
            dst[slot, 16 * i : 16 * i + 16, :] = acc_s[k]
            piece = stat_s[k]
            total = total + (piece if i == 0 else pltpu.roll(piece, 8 * i, 1))
        dst[slot, 48:56, :] = (total[:8] + pltpu.roll(total[8:], 64, 1)).astype(BF16)

    def seq_copy(msg, rcv, send, recv, to):
        return pltpu.make_async_remote_copy(
            src_ref=msg.at[to],
            dst_ref=rcv.at[me],
            send_sem=send.at[to],
            recv_sem=recv.at[me],
            device_id=(to, head),
            device_id_type=MESH,
        )

    def seq_arrival(msg, rcv, send, recv, source):
        return pltpu.make_async_remote_copy(
            src_ref=msg.at[source],
            dst_ref=rcv.at[source],
            send_sem=send.at[source],
            recv_sem=recv.at[source],
            device_id=(source, head),
            device_id_type=MESH,
        )

    def head_copy(msg, slot, rcv, send, recv, to):
        return pltpu.make_async_remote_copy(
            src_ref=msg if slot is None else msg.at[slot],
            dst_ref=rcv.at[head],
            send_sem=send.at[to],
            recv_sem=recv.at[head],
            device_id=(me, to),
            device_id_type=MESH,
        )

    def head_arrival(msg, slot, rcv, send, recv, source):
        return pltpu.make_async_remote_copy(
            src_ref=msg if slot is None else msg.at[slot],
            dst_ref=rcv.at[source],
            send_sem=send.at[source],
            recv_sem=recv.at[source],
            device_id=(me, source),
            device_id_type=MESH,
        )

    def others(count, mine, body):
        def step(d, carry):
            body(lax.rem(mine + d, count))
            return carry

        lax.fori_loop(1, count, step, 0)

    core = lax.rem(head, 2)
    chip = head // 2
    near = chip + 1 - 2 * lax.rem(chip, 2)
    sibling = 2 * chip + 1 - core
    far = [near, 3 - chip, lax.rem(chip + 2, 4)]

    def send_partials(o):
        pack(msg1, o, o)
        seq_copy(msg1, rcv1, send1, recv1, o).start()

    others(N_SEQ, me, send_partials)
    pack(rcv1, me, me)

    angle = jnp.zeros((16, 128), F32)
    for i in range(3):
        angle = jnp.where((row >> 2) == i, freq * place(me * 3 + i), angle)
        small_s[4 * i : 4 * i + 4, :] = fresh[i].astype(F32)
    base_c, base_s = cos_sin(angle)
    small_s[12:16, :] = jnp.zeros((4, 128), F32)
    kv_new = small_s[...]
    key_new = turned(kv_new, base_c * ct - base_s * st, base_s * ct + base_c * st, lane)
    kn = jnp.where(lane < 64, key_new, kv_new).astype(BF16)
    vn = jnp.where(lane < 64, 1.0, kv_new).astype(BF16)
    fresh_stats = jnp.zeros((16, 128), F32)
    srow = iota((32, 16), 0)
    scol = iota((32, 16), 1)
    for i in range(3):
        k = rank[3 * me + i]
        q = q_all[k]
        seen = ((scol >> 2) == i) & ((scol & 3) <= (srow & 3))
        s = jnp.where(seen, dot(q, kn, NT), LOW)
        peak = jnp.max(s, axis=1, keepdims=True).astype(BF16).astype(F32)
        w = jnp.exp(s - peak).astype(BF16)
        values, stats = tiles_of(dot(w, vn, NN), peak, lane)
        rcv1[N_SEQ, 16 * i : 16 * i + 16, :] = values
        fresh_stats = fresh_stats + (stats if i == 0 else pltpu.roll(stats, 8 * i, 1))
    folded = fresh_stats[:8] + pltpu.roll(fresh_stats[8:], 64, 1)
    rcv1[N_SEQ, 48:56, :] = folded.astype(BF16)

    sink = jnp.zeros((16, 128), F32)
    for j in range(8):
        here = ((row >> 2) == (j >> 1)) & ((lane >> 6) == (j & 1))
        sink = jnp.where(here, sinks[j], sink)

    wide_lane = iota((16, 512), 1)
    expert = wide_lane >> 4
    place = wide_lane & 15
    pick = (place >= 3).astype(jnp.int32) + (place >= 6).astype(jnp.int32)
    tile = place - 3 * pick
    own = (iota((REQ, 384), 0) == me * 3 + (iota((REQ, 384), 1) >> 7)).astype(F32).astype(BF16)
    flat_ids = jnp.concatenate([ids[t] for t in range(4)], axis=0).astype(F32).astype(BF16)
    own_ids = dot(flat_ids, own, NN).astype(BF16)
    xr = iota((64, 16), 0)
    xc = iota((64, 16), 1)
    names = jnp.full((64, 128), -1.0, F32) * ((iota((64, 128), 0) & 15) >= 12).astype(F32)
    for i in range(3):
        take = (xc == (xr & 3) * 4 + (xr >> 4)) & (((xr & 15) >> 2) == i)
        names = names + dot(
            take.astype(F32).astype(BF16), own_ids[:, 128 * i : 128 * i + 128], NN
        )
    names = jnp.concatenate([names] * 4, axis=1)
    route_s[...] = jnp.zeros((16, 128), F32)
    for i in range(3):
        route_s[4 * i : 4 * i + 4, 0:4] = routes[i]
    named = jnp.zeros((16, 512), F32)
    share = jnp.zeros((16, 512), F32)
    for k in range(4):
        hit = names[16 * k : 16 * k + 16] == expert.astype(F32)
        named = named + jnp.where(hit, 1.0, 0.0)
        share = share + jnp.where(hit, route_s[:, k : k + 1], 0.0)
    below = (iota((16, 16), 1) < iota((16, 16), 0)).astype(F32).astype(BF16)
    earlier = dot(below, named.astype(BF16), NN)
    chosen = (named > 0.5) & (earlier == pick.astype(F32)) & (place < 9)
    chosen_tile = [chosen & (tile == c) for c in range(3)]
    select = jnp.concatenate([jnp.where(m, 1.0, 0.0) for m in chosen_tile], axis=0)
    select = select.T.astype(BF16)
    give = jnp.concatenate([jnp.where(m, share, 0.0) for m in chosen_tile], axis=0)
    give_hi = give.astype(BF16)
    give_lo = (give - give_hi.astype(F32)).astype(BF16)

    trow = iota((288, 512), 0)
    tcol = iota((288, 512), 1)
    ttile = (trow >= 96).astype(jnp.int32) + (trow >= 192).astype(jnp.int32)
    trest = trow - 96 * ttile
    spread = (
        ((trest & 31) == (tcol >> 4)) & ((tcol & 15) == 3 * (trest >> 5) + ttile)
    ).astype(F32).astype(BF16)

    ucol = iota((512, 288), 1)
    urow = iota((512, 288), 0)
    utile = (ucol >= 96).astype(jnp.int32) + (ucol >= 192).astype(jnp.int32)
    urest = ucol - 96 * utile
    gather = (
        ((urest & 31) == (urow >> 4)) & ((urow & 15) == 3 * (urest >> 5) + utile)
    ).astype(F32).astype(BF16)
    resid_s[...] = jnp.zeros((16, 3072), F32)
    for i in range(3):
        resid_s[4 * i : 4 * i + 4, 0:D] = resid[i].astype(F32)

    load_ow.wait()
    ow_v[pl.ds(D, 3072 - D), :] = jnp.zeros((3072 - D, 512), BF16)
    load_gate.wait()
    load_up.wait()
    load_dn.wait()
    gu_v[FFL:CH, :] = jnp.zeros((CH - FFL, D), BF16)
    gu_v[CH + FFL : 2 * CH, :] = jnp.zeros((CH - FFL, D), BF16)
    dn_v[FFL:CH, :] = jnp.zeros((CH - FFL, D), BF16)
    dn_w[:, 2816:3072] = jnp.zeros((CH, 256), BF16)
    dn_w[:, 0:D] = dn_v[...]
    gu_w[:, 2816:3072] = jnp.zeros((2 * CH, 256), BF16)
    gu_w[:, 0:D] = gu_v[...]
    gain_s[:, 2816:3072] = jnp.zeros((1, 256), F32)
    gain_s[:, 0:D] = gain[...]

    others(N_SEQ, me, lambda s: seq_arrival(msg1, rcv1, send1, recv1, s).wait_recv())

    stat_rows = rcv1[:, 48:56, :].reshape((N_SEQ + 1) * 8, 128)
    er = iota((128, 384), 0)
    ec = iota((128, 384), 1)
    attended = []
    for i in range(3):
        for half in range(2):
            spot = 64 * half + 8 * i + 4 * ((ec & 127) >> 6) + (ec >> 7)
            expand = (er == spot).astype(F32).astype(BF16)
            wide = dot(stat_rows, expand, NN)
            peaks = wide[:, 0:128].reshape(N_SEQ + 1, 8, 128)
            totals = (wide[:, 128:256] + wide[:, 256:384]).reshape(N_SEQ + 1, 8, 128)
            sunk = sink[8 * half : 8 * half + 8]
            top = jnp.maximum(jnp.max(peaks, axis=0), sunk)
            factor = jnp.exp(peaks - top[None])
            start = 16 * i + 8 * half
            values = rcv1[:, start : start + 8, :].astype(F32)
            num = jnp.sum(values * factor, axis=0)
            den = jnp.sum(totals * factor, axis=0) + jnp.exp(sunk - top)
            attended.append(num / den)
    att = jnp.concatenate(attended, axis=0).astype(BF16)
    rr = iota((64, 48), 0)
    rc = iota((64, 48), 1)
    want = ((rr & 15) >> 2) * 16 + (rr >> 4) * 4 + (rr & 3)
    regroup = (rc == want).astype(F32).astype(BF16)
    mixed = dot(regroup, att, NN).astype(BF16)
    flat = jnp.concatenate([mixed[16 * p : 16 * p + 16] for p in range(4)], axis=1)

    def project(j):
        rows = ow_v[pl.ds(pl.multiple_of(j * CH, CH), CH), :]
        return dot(flat, rows, NT).astype(BF16)

    def send_projection(j):
        msg2[j] = project(j)
        head_copy(msg2, j, rcv2, send2, recv2, j).start()

    others(N_HEAD, head, send_projection)
    rcv2[head] = project(head)
    others(N_HEAD, head, lambda s: head_arrival(msg2, s, rcv2, send2, recv2, s).wait_recv())
    total = resid_s[:, pl.ds(pl.multiple_of(head * CH, CH), CH)]
    total = total + jnp.sum(rcv2[...].astype(F32), axis=0)
    hidden = total.astype(BF16)
    hidden_rows = jnp.concatenate([hidden[:, 128 * c : 128 * c + 128] for c in range(3)], axis=0)

    msg3[...] = dot(select, hidden_rows, NN).astype(BF16).reshape(N_SEQ, 16, 128)
    others(N_SEQ, me, lambda o: seq_copy(msg3, rcv3, send3, recv3, o).start())
    rcv3[me] = msg3[me]
    others(N_SEQ, me, lambda s: seq_arrival(msg3, rcv3, send3, recv3, s).wait_recv())
    got = dot(spread, rcv3[...].reshape(512, 128), NN).astype(BF16)
    mine = jnp.concatenate([got[96 * c : 96 * c + 96] for c in range(3)], axis=1)
    msg4[...] = mine
    gather_to = [2 * far[2] + core, 2 * far[0] + core, 2 * far[1] + core, sibling]
    for j in gather_to:
        head_copy(msg4, None, rcv4, send4, recv4, j).start()
    rcv4[head] = mine

    both_s[...] = jnp.zeros((ROWS, 2 * CH), F32)
    square_s[...] = jnp.zeros((ROWS, 128), F32)

    def use_chunk(j):
        cols = pl.ds(pl.multiple_of(j * CH, CH), CH)
        x = rcv4[j].astype(F32)
        square_s[...] += jnp.broadcast_to(jnp.sum(x * x, axis=1, keepdims=True), (ROWS, 128))
        both_s[...] += dot((x * gain_s[:, cols]).astype(BF16), gu_w[:, cols], NT)

    def forward(k, j):
        return pltpu.make_async_remote_copy(
            src_ref=rcv4.at[j],
            dst_ref=rcv4.at[j],
            send_sem=send_f.at[k],
            recv_sem=recv4.at[j],
            device_id=(me, sibling),
            device_id_type=MESH,
        )

    use_chunk(head)
    head_arrival(msg4, None, rcv4, send4, recv4, sibling).wait_recv()
    use_chunk(sibling)
    for k in range(3):
        j = 2 * far[k] + core
        head_arrival(msg4, None, rcv4, send4, recv4, j).wait_recv()
        forward(k, j).start()
        use_chunk(j)
    for k in range(3):
        j = 2 * far[k] + 1 - core
        forward(k, j).wait_recv()
        use_chunk(j)
    both = both_s[...]
    square = square_s[:, 0:1]
    scale = lax.rsqrt(square * (1.0 / D) + 1e-05)
    g = jnp.minimum(both[:, 0:CH] * scale, 7.0)
    u = jnp.clip(both[:, CH : 2 * CH] * scale, -7.0, 7.0)
    active = ((u + 1.0) * g * jax.nn.sigmoid(1.702 * g)).astype(BF16)

    def product(j):
        return dot(active, dn_w[:, pl.ds(pl.multiple_of(j * CH, CH), CH)], NN)

    def pair_copy(c):
        return pltpu.make_async_remote_copy(
            src_ref=msg_p.at[c],
            dst_ref=rcv_p.at[c],
            send_sem=send_p.at[c],
            recv_sem=recv_p.at[c],
            device_id=(me, sibling),
            device_id_type=MESH,
        )

    def chip_copy(c, slot):
        return pltpu.make_async_remote_copy(
            src_ref=msg5.at[c],
            dst_ref=rcv5.at[slot],
            send_sem=send5.at[c],
            recv_sem=recv5.at[slot],
            device_id=(me, 2 * c + core),
            device_id_type=MESH,
        )

    turns = [far[2], far[0], far[1], chip]
    for c in turns:
        msg_p[c] = product(2 * c + 1 - core).astype(BF16)
        pair_copy(c).start()
    for k, c in enumerate(turns):
        own = product(2 * c + core)
        pair_copy(c).wait_recv()
        both_cores = (own + rcv_p[c].astype(F32)).astype(BF16)
        if k < 3:
            msg5[c] = both_cores
            chip_copy(c, chip).start()
        else:
            rcv5[chip] = both_cores
    for c in far:
        chip_copy(c, c).wait_recv()
    summed = jnp.sum(rcv5[...].astype(F32), axis=0).astype(BF16)
    summed_rows = jnp.concatenate([summed[:, 128 * c : 128 * c + 128] for c in range(3)], axis=0)
    msg6[...] = dot(gather, summed_rows, NN).astype(BF16).reshape(N_SEQ, 16, 128)
    others(N_SEQ, me, lambda o: seq_copy(msg6, rcv6, send6, recv6, o).start())
    rcv6[me] = msg6[me]
    others(N_SEQ, me, lambda s: seq_arrival(msg6, rcv6, send6, recv6, s).wait_recv())
    back = rcv6[...].reshape(512, 128)
    added = dot(give_hi, back, NN) + dot(give_lo, back, NN)
    result = hidden_rows.astype(F32) + added
    result = jnp.concatenate([result[16 * c : 16 * c + 16] for c in range(3)], axis=1).astype(BF16)
    msg7[...] = result
    others(N_HEAD, head, lambda o: head_copy(msg7, None, rcv7, send7, recv7, o).start())
    rcv7[head] = result
    others(N_HEAD, head, lambda s: head_arrival(msg7, None, rcv7, send7, recv7, s).wait_recv())
    for i in range(3):
        for j in range(N_HEAD):
            width = CH if j < N_HEAD - 1 else LASTC
            out_ref[i, :, j * CH : j * CH + width] = rcv7[j, 4 * i : 4 * i + 4, 0:width]

    for msg, rcv, send, recv in (
        (msg1, rcv1, send1, recv1),
        (msg3, rcv3, send3, recv3),
        (msg6, rcv6, send6, recv6),
    ):
        others(N_SEQ, me, lambda o: seq_copy(msg, rcv, send, recv, o).wait_send())
    for j in gather_to:
        head_copy(msg4, None, rcv4, send4, recv4, j).wait_send()
    for k in range(3):
        forward(k, 2 * far[k] + core).wait_send()
    for k, c in enumerate(turns):
        pair_copy(c).wait_send()
        if k < 3:
            chip_copy(c, chip).wait_send()
    others(N_HEAD, head, lambda o: head_copy(msg2, o, rcv2, send2, recv2, o).wait_send())
    others(N_HEAD, head, lambda o: head_copy(msg7, None, rcv7, send7, recv7, o).wait_send())


def on_device(
    new_query,
    fresh_key_value,
    prompt_cache,
    decoded_tail_cache,
    sinks,
    prompt_group,
    prompt_lens,
    tail_lens,
    o_weight,
    resid,
    norm_gain,
    expert_ids,
    route_weights,
    gate_up,
    down_weight,
):
    r = jnp.arange(REQ, dtype=jnp.int32)
    mine, other = prompt_group[:, None], prompt_group[None, :]
    ahead = (other < mine) | ((other == mine) & (r[None, :] < r[:, None]))
    rank = jnp.sum(ahead.astype(jnp.int32), axis=1)
    order = jnp.sum(jnp.where(rank[None, :] == r[:, None], r[None, :], 0), axis=1)
    freq = np.exp(np.arange(32) * (-2.0 * math.log(150000.0) / 64))
    freq = np.tile(freq.astype(np.float32), 4)
    step_angle = (np.arange(16) % 4)[:, None] * freq[None, :].astype(np.float64)
    tables = np.zeros((40, 128), np.float32)
    tables[0] = freq
    tables[8:24] = np.cos(step_angle)
    tables[24:40] = np.sin(step_angle)
    fresh = fresh_key_value.transpose(0, 2, 1, 3).reshape(3, 4, 128)
    ids = expert_ids.transpose(1, 2, 0)
    gain = norm_gain.reshape(1, D)
    q = new_query.reshape(REQ, 4, 4, 128).transpose(0, 2, 1, 3).reshape(REQ, 16, 128)
    prompt = prompt_cache.transpose(0, 2, 1, 3).reshape(GROUPS, PBLOCK, 128)
    tail = decoded_tail_cache.transpose(0, 2, 1, 3).reshape(REQ, TBLOCK, 128)
    ow = o_weight.T
    gu = gate_up.transpose(0, 2, 3, 1).reshape(2, FFL, D)
    dn = down_weight.reshape(FFL, D)

    smem = pl.BlockSpec(memory_space=pltpu.SMEM)
    vmem = pl.BlockSpec(memory_space=pltpu.VMEM)
    hbm = pl.BlockSpec(memory_space=pl.ANY)
    seq_sem = pltpu.SemaphoreType.DMA((N_SEQ,))
    head_sem = pltpu.SemaphoreType.DMA((N_HEAD,))
    chip_sem = pltpu.SemaphoreType.DMA((4,))
    out = pl.pallas_call(
        layer_kernel,
        name="layer",
        out_shape=jax.ShapeDtypeStruct((3, 4, D), BF16),
        in_specs=[smem] * 6 + [vmem] * 6 + [hbm] * 6,
        out_specs=vmem,
        scratch_shapes=[
            pltpu.VMEM((REQ, 16, 128), BF16),
            pltpu.VMEM((GROUPS, PBLOCK, 128), BF16),
            pltpu.VMEM((REQ, TBLOCK, 128), BF16),
            pltpu.VMEM((3072, 512), BF16),
            pltpu.VMEM((2 * CH, D), BF16),
            pltpu.VMEM((CH, D), BF16),
            pltpu.VMEM((CH, 3072), BF16),
            pltpu.VMEM((2 * CH, 3072), BF16),
            pltpu.VMEM((1, 3072), F32),
            pltpu.VMEM((REQ, 128), F32),
            pltpu.VMEM((REQ, 128), F32),
            pltpu.VMEM((16, 128), F32),
            pltpu.VMEM((16, 128), F32),
            pltpu.VMEM((16, 3072), F32),
            pltpu.VMEM((ROWS, 2 * CH), F32),
            pltpu.VMEM((ROWS, 128), F32),
            pltpu.VMEM((REQ, 32, 128), BF16),
            pltpu.VMEM((MEMBERS * 32, PBLOCK + 128), F32),
            pltpu.VMEM((MEMBERS * 32, PBLOCK + 128), F32),
            pltpu.VMEM((MEMBERS * 32, 128), F32),
            pltpu.VMEM((MEMBERS * 32, 128), F32),
            pltpu.VMEM((REQ, 16, 128), BF16),
            pltpu.VMEM((REQ, 16, 128), F32),
            pltpu.VMEM((N_SEQ, 56, 128), BF16),
            pltpu.VMEM((N_SEQ + 1, 56, 128), BF16),
            pltpu.VMEM((N_HEAD, 16, CH), BF16),
            pltpu.VMEM((N_HEAD, 16, CH), BF16),
            pltpu.VMEM((N_SEQ, 16, 128), BF16),
            pltpu.VMEM((N_SEQ, 16, 128), BF16),
            pltpu.VMEM((ROWS, CH), BF16),
            pltpu.VMEM((N_HEAD, ROWS, CH), BF16),
            pltpu.VMEM((4, ROWS, CH), BF16),
            pltpu.VMEM((4, ROWS, CH), BF16),
            pltpu.VMEM((4, ROWS, CH), BF16),
            pltpu.VMEM((4, ROWS, CH), BF16),
            pltpu.VMEM((N_SEQ, 16, 128), BF16),
            pltpu.VMEM((N_SEQ, 16, 128), BF16),
            pltpu.VMEM((16, CH), BF16),
            pltpu.VMEM((N_HEAD, 16, CH), BF16),
            pltpu.SemaphoreType.DMA((6,)),
            pltpu.SemaphoreType.DMA((GROUPS,)),
            seq_sem,
            seq_sem,
            head_sem,
            head_sem,
            seq_sem,
            seq_sem,
            head_sem,
            head_sem,
            chip_sem,
            chip_sem,
            chip_sem,
            chip_sem,
            chip_sem,
            seq_sem,
            seq_sem,
            head_sem,
            head_sem,
        ],
        compiler_params=pltpu.CompilerParams(
            collective_id=0, has_side_effects=True, vmem_limit_bytes=56 * 1024 * 1024
        ),
    )(
        order,
        rank,
        prompt_group,
        tail_lens,
        prompt_lens,
        sinks,
        jnp.asarray(tables),
        fresh,
        ids,
        route_weights,
        resid,
        gain,
        q,
        prompt,
        tail,
        ow,
        gu,
        dn,
    )
    return out


def solution(mesh):
    return jax.shard_map(
        on_device,
        mesh=mesh,
        in_specs=(
            P(None, None, "head"),
            P("seq", None, "head", None),
            P(None, "seq", "head", None),
            P(None, "seq", "head", None),
            P("head"),
            P(),
            P(),
            P(),
            P("head", None),
            P("seq", None, None),
            P(),
            P(),
            P("seq", None, None),
            P("seq", None, None, "head"),
            P("seq", "head", None),
        ),
        out_specs=P("seq", None, None),
        check_vma=False,
    )
```

```python
import math

import jax
import jax.numpy as jnp
import numpy as np
from jax import lax
from jax.experimental import pallas as pl
from jax.experimental.pallas import tpu as pltpu
from jax.sharding import PartitionSpec as P

MESH = pl.DeviceIdType.MESH
LOW = -1e30
FLOOR = -1e29
F32 = jnp.float32
BF16 = jnp.bfloat16

N_SEQ = 32
N_HEAD = 8
REQ = 96
GROUPS = 8
MEMBERS = 12
PBLOCK = 1024
TBLOCK = 32
D = 2880
CH = 384
LASTC = 192
FFL = 360
ROWS = 96
HALF_PI = (1.5703125, 4.8351287841796875e-4, 3.1391647865048e-7)
NT = (((1,), (1,)), ((), ()))
NN = (((1,), (0,)), ((), ()))
TN = (((0,), (0,)), ((), ()))


def dot(a, b, dims):
    return lax.dot_general(a, b, dims, preferred_element_type=F32)


def iota(shape, axis):
    return lax.broadcasted_iota(jnp.int32, shape, axis)


def turned(x, cosine, sine, lane):
    ahead = pltpu.roll(x, 96, 1)
    behind = pltpu.roll(x, 32, 1)
    partner = jnp.where((lane & 63) < 32, -ahead, behind)
    return x * cosine + partner * sine


def cos_sin(angle):
    k = jnp.floor(angle * (2.0 / math.pi) + 0.5)
    r = angle - k * HALF_PI[0]
    r = r - k * HALF_PI[1]
    r = r - k * HALF_PI[2]
    r2 = r * r
    s = r + r * r2 * (-1.0 / 6 + r2 * (1.0 / 120 + r2 * (-1.0 / 5040 + r2 * (1.0 / 362880))))
    c = 1.0 + r2 * (-0.5 + r2 * (1.0 / 24 + r2 * (-1.0 / 720 + r2 * (1.0 / 40320))))
    quarter = k - 4.0 * jnp.floor(k * 0.25)
    odd = (quarter == 1.0) | (quarter == 3.0)
    cosine = jnp.where(odd, s, c)
    sine = jnp.where(odd, c, s)
    cosine = jnp.where((quarter == 1.0) | (quarter == 2.0), -cosine, cosine)
    sine = jnp.where(quarter >= 2.0, -sine, sine)
    return cosine, sine


def tiles_of(out, peak, lane):
    first, second = out[:8], out[8:]
    values = jnp.where(lane < 64, pltpu.roll(first, 64, 1), second).astype(BF16)
    hi0 = first.astype(BF16).astype(F32)
    hi1 = second.astype(BF16).astype(F32)
    lo0 = first - hi0
    lo1 = second - hi1
    left = jnp.where(lane == 0, peak[:8], jnp.where(lane == 1, hi0, lo0))
    right = jnp.where(lane == 4, peak[8:], jnp.where(lane == 5, hi1, lo1))
    stats = jnp.where(lane < 3, left, jnp.where((lane >= 4) & (lane < 7), right, 0.0))
    return values, stats


def layer_kernel(
    order,
    rank,
    prompt_group,
    tail_lens,
    prompt_lens,
    sinks,
    tables,
    fresh,
    ids,
    routes,
    resid,
    gain,
    q_hbm,
    prompt_hbm,
    tail_hbm,
    ow_hbm,
    gu_hbm,
    dn_hbm,
    out_ref,
    q_v,
    prompt_v,
    tail_v,
    ow_v,
    gu_v,
    dn_v,
    dn_w,
    gu_w,
    gain_s,
    cos_s,
    sin_s,
    small_s,
    att_s,
    route_s,
    resid_s,
    both_s,
    square_s,
    q_all,
    even_s,
    odd_s,
    even_top,
    odd_top,
    acc_s,
    stat_s,
    msg1,
    rcv1,
    msg2,
    rcv2,
    msg3,
    rcv3,
    msg4,
    rcv4,
    msg_p,
    rcv_p,
    msg5,
    rcv5,
    msg6,
    rcv6,
    msg7,
    rcv7,
    load_sem,
    prompt_sem,
    send0,
    recv0,
    send1,
    recv1,
    send2,
    recv2,
    send3,
    recv3,
    send4,
    recv4,
    send_f,
    send_p,
    recv_p,
    send5,
    recv5,
    send6,
    recv6,
    send7,
    recv7,
):
    me = lax.axis_index("seq")
    head = lax.axis_index("head")
    barrier = pltpu.get_barrier_semaphore()

    def greet_seq(d, carry):
        pl.semaphore_signal(
            barrier, inc=1, device_id=(lax.rem(me + d, N_SEQ), head), device_id_type=MESH
        )
        return carry

    def greet_head(d, carry):
        pl.semaphore_signal(
            barrier, inc=1, device_id=(me, lax.rem(head + d, N_HEAD)), device_id_type=MESH
        )
        return carry

    load_q = pltpu.make_async_copy(q_hbm, q_v, load_sem.at[0])
    load_tail = pltpu.make_async_copy(tail_hbm, tail_v, load_sem.at[1])
    load_ow = pltpu.make_async_copy(ow_hbm, ow_v.at[pl.ds(0, D)], load_sem.at[2])
    load_gate = pltpu.make_async_copy(gu_hbm.at[0], gu_v.at[pl.ds(0, FFL)], load_sem.at[3])
    load_up = pltpu.make_async_copy(gu_hbm.at[1], gu_v.at[pl.ds(CH, FFL)], load_sem.at[5])
    load_dn = pltpu.make_async_copy(dn_hbm, dn_v.at[pl.ds(0, FFL)], load_sem.at[4])
    load_q.start()
    load_tail.start()

    def load_prompt(g):
        return pltpu.make_async_copy(prompt_hbm.at[g], prompt_v.at[g], prompt_sem.at[g])

    for g in range(GROUPS):
        load_prompt(g).start()
    load_ow.start()
    load_gate.start()
    load_up.start()
    load_dn.start()
    lax.fori_loop(1, N_SEQ, greet_seq, 0)
    lax.fori_loop(1, N_HEAD, greet_head, 0)

    lane = iota((16, 128), 1)
    row = iota((16, 128), 0)

    freq = tables[0:1, :]
    ct = tables[8:24, :]
    st = tables[24:40, :]

    def place(r):
        return (prompt_lens[prompt_group[r]] + tail_lens[r]).astype(F32)

    def put_angle(i, carry):
        cos_s[pl.ds(i, 1), :] = freq * place(order[i])
        return carry

    lax.fori_loop(0, REQ, put_angle, 0, unroll=8)
    cosine, sine = cos_sin(cos_s[...])
    cos_s[...] = cosine
    sin_s[...] = sine

    load_q.wait()

    def rotate_one(i, carry):
        r = order[i]
        x = q_v[r].astype(F32)
        c0 = cos_s[pl.ds(i, 1), :]
        s0 = sin_s[pl.ds(i, 1), :]
        y = turned(x, c0 * ct - s0 * st, s0 * ct + c0 * st, lane)
        y = y.astype(BF16).astype(F32) * 0.125
        even = jnp.where(lane < 64, y, 0.0)
        odd = jnp.where(lane < 64, pltpu.roll(y, 64, 1), 0.0)
        for h in range(2):
            part = slice(8 * h, 8 * h + 8)
            q_all[h * REQ + i] = jnp.concatenate([even[part], odd[part]], axis=0).astype(BF16)
        return carry

    lax.fori_loop(0, REQ, rotate_one, 0, unroll=4)
    load_tail.wait()

    key_col = iota((1, PBLOCK), 1) + me * PBLOCK
    col128 = iota((1, 128), 1)
    upper = (iota((1, 128), 1) >= 64).astype(F32).astype(BF16)
    lower = (iota((1, 128), 1) < 64).astype(F32).astype(BF16)
    same_req = (iota((64, 128), 0) >> 4) == (iota((64, 128), 1) >> 5)
    lane8 = lane[:8]

    def tails(g):
        members = [order[g * MEMBERS + i] for i in range(MEMBERS)]
        return [
            jnp.concatenate([tail_v[r] for r in members[4 * b : 4 * b + 4]], axis=0)
            for b in range(3)
        ], members

    def scores(n, buf, tops):
        g = lax.rem(n, GROUPS)
        kv = prompt_v[g]
        bias = jnp.where(key_col < prompt_lens[g], 0.0, LOW)
        q = q_all[pl.ds(n * MEMBERS, MEMBERS)].reshape(MEMBERS * 16, 128)
        high = None
        for h in range(4):
            cols = slice(256 * h, 256 * h + 256)
            part = dot(q, kv[cols], NT) + bias[:, cols]
            buf[:, cols] = part
            part = jnp.maximum(part[:, :128], part[:, 128:])
            high = part if high is None else jnp.maximum(high, part)
        keys, members = tails(g)
        for b in range(3):
            rows = slice(64 * b, 64 * b + 64)
            limit = jnp.zeros((1, 128), jnp.int32)
            for i in range(4):
                limit = jnp.where((col128 >> 5) == i, tail_lens[members[4 * b + i]], limit)
            seen = same_req & (((col128 & 31) + me * TBLOCK) < limit)
            part = jnp.where(seen, dot(q[rows], keys[b], NT), LOW)
            buf[rows, PBLOCK : PBLOCK + 128] = part
            top = jnp.max(jnp.maximum(high[rows], part), axis=1, keepdims=True)
            top = jnp.maximum(top, FLOOR).astype(BF16).astype(F32)
            tops[rows, :] = jnp.broadcast_to(top, (64, 128))

    def weigh(n, buf, tops):
        g = lax.rem(n, GROUPS)
        first = n * MEMBERS
        kv = prompt_v[g]
        vx = kv * upper + lower
        keys, members = tails(g)
        peaks = tops[...]
        w = jnp.concatenate(
            [
                jnp.exp(buf[:, 128 * h : 128 * h + 128] - peaks).astype(BF16)
                for h in range(PBLOCK // 128)
            ],
            axis=1,
        )
        w2 = jnp.exp(buf[:, PBLOCK : PBLOCK + 128] - peaks).astype(BF16)
        whole = dot(w, vx, NN)
        for b in range(3):
            rows = slice(64 * b, 64 * b + 64)
            peak = peaks[rows]
            o = whole[rows] + dot(w2[rows], keys[b] * upper + lower, NN)
            for i in range(4):
                values, stats = tiles_of(
                    o[16 * i : 16 * i + 16], peak[16 * i : 16 * i + 16], lane8
                )
                acc_s[first + 4 * b + i] = values
                stat_s[first + 4 * b + i] = stats

    for g in range(GROUPS):
        load_prompt(g).wait()
    scores(0, even_s, even_top)

    def two_steps(k, carry):
        n = 2 * k
        scores(n + 1, odd_s, odd_top)
        weigh(n, even_s, even_top)
        scores(jnp.minimum(n + 2, 2 * GROUPS - 1), even_s, even_top)
        weigh(n + 1, odd_s, odd_top)
        return carry

    lax.fori_loop(0, GROUPS // 2, two_steps, 0)

    pl.semaphore_wait(barrier, N_SEQ - 1 + N_HEAD - 1)

    def pack(dst, half, slot, o):
        total = jnp.zeros((8, 128), F32)
        for i in range(3):
            k = half * REQ + rank[3 * o + i]
            dst[half, slot, 8 * i : 8 * i + 8, :] = acc_s[k]
            piece = stat_s[k]
            total = total + (piece if i == 0 else pltpu.roll(piece, 8 * i, 1))
        dst[half, slot, 24:32, :] = total.astype(BF16)

    def seq_copy(msg, rcv, send, recv, to):
        return pltpu.make_async_remote_copy(
            src_ref=msg.at[to],
            dst_ref=rcv.at[me],
            send_sem=send.at[to],
            recv_sem=recv.at[me],
            device_id=(to, head),
            device_id_type=MESH,
        )

    def seq_arrival(msg, rcv, send, recv, source):
        return pltpu.make_async_remote_copy(
            src_ref=msg.at[source],
            dst_ref=rcv.at[source],
            send_sem=send.at[source],
            recv_sem=recv.at[source],
            device_id=(source, head),
            device_id_type=MESH,
        )

    def head_copy(msg, slot, rcv, send, recv, to):
        return pltpu.make_async_remote_copy(
            src_ref=msg if slot is None else msg.at[slot],
            dst_ref=rcv.at[head],
            send_sem=send.at[to],
            recv_sem=recv.at[head],
            device_id=(me, to),
            device_id_type=MESH,
        )

    def head_arrival(msg, slot, rcv, send, recv, source):
        return pltpu.make_async_remote_copy(
            src_ref=msg if slot is None else msg.at[slot],
            dst_ref=rcv.at[source],
            send_sem=send.at[source],
            recv_sem=recv.at[source],
            device_id=(me, source),
            device_id_type=MESH,
        )

    def others(count, mine, body):
        def step(d, carry):
            body(lax.rem(mine + d, count))
            return carry

        lax.fori_loop(1, count, step, 0)

    core = lax.rem(head, 2)
    chip = head // 2
    near = chip + 1 - 2 * lax.rem(chip, 2)
    sibling = 2 * chip + 1 - core
    far = [near, 3 - chip, lax.rem(chip + 2, 4)]

    def exchange(half):
        sends, recvs = (send1, recv1) if half == 0 else (send0, recv0)
        return msg1.at[half], rcv1.at[half], sends, recvs

    def send_partials(half):
        def one(o):
            pack(msg1, half, o, o)
            seq_copy(*exchange(half), o).start()

        others(N_SEQ, me, one)
        pack(rcv1, half, me, me)

    send_partials(0)
    lax.fori_loop(GROUPS // 2, GROUPS, two_steps, 0)
    send_partials(1)

    angle = jnp.zeros((16, 128), F32)
    for i in range(3):
        angle = jnp.where((row >> 2) == i, freq * place(me * 3 + i), angle)
        small_s[4 * i : 4 * i + 4, :] = fresh[i].astype(F32)
    base_c, base_s = cos_sin(angle)
    small_s[12:16, :] = jnp.zeros((4, 128), F32)
    kv_new = small_s[...]
    key_new = turned(kv_new, base_c * ct - base_s * st, base_s * ct + base_c * st, lane)
    kn = jnp.where(lane < 64, key_new, kv_new).astype(BF16)
    vn = jnp.where(lane < 64, 1.0, kv_new).astype(BF16)
    fresh_stats = [jnp.zeros((8, 128), F32)] * 2
    srow = iota((16, 16), 0)
    scol = iota((16, 16), 1)
    for i, half in ((i, half) for i in range(3) for half in range(2)):
        q = q_all[half * REQ + rank[3 * me + i]]
        seen = ((scol >> 2) == i) & ((scol & 3) <= (srow & 3))
        s = jnp.where(seen, dot(q, kn, NT), LOW)
        peak = jnp.max(s, axis=1, keepdims=True).astype(BF16).astype(F32)
        w = jnp.exp(s - peak).astype(BF16)
        peak = jnp.broadcast_to(peak, (16, 128))
        values, stats = tiles_of(dot(w, vn, NN), peak, lane8)
        rcv1[half, N_SEQ, 8 * i : 8 * i + 8, :] = values
        fresh_stats[half] = fresh_stats[half] + (stats if i == 0 else pltpu.roll(stats, 8 * i, 1))
    for half in range(2):
        rcv1[half, N_SEQ, 24:32, :] = fresh_stats[half].astype(BF16)

    sink = jnp.zeros((16, 128), F32)
    for j in range(8):
        here = ((row >> 2) == (j >> 1)) & ((lane >> 6) == (j & 1))
        sink = jnp.where(here, sinks[j], sink)

    wide_lane = iota((16, 512), 1)
    expert = wide_lane >> 4
    place = wide_lane & 15
    pick = (place >= 3).astype(jnp.int32) + (place >= 6).astype(jnp.int32)
    tile = place - 3 * pick
    own = (iota((REQ, 384), 0) == me * 3 + (iota((REQ, 384), 1) >> 7)).astype(F32).astype(BF16)
    flat_ids = jnp.concatenate([ids[t] for t in range(4)], axis=0).astype(F32).astype(BF16)
    own_ids = dot(flat_ids, own, NN).astype(BF16)
    xr = iota((64, 16), 0)
    xc = iota((64, 16), 1)
    names = jnp.full((64, 128), -1.0, F32) * ((iota((64, 128), 0) & 15) >= 12).astype(F32)
    for i in range(3):
        take = (xc == (xr & 3) * 4 + (xr >> 4)) & (((xr & 15) >> 2) == i)
        names = names + dot(
            take.astype(F32).astype(BF16), own_ids[:, 128 * i : 128 * i + 128], NN
        )
    names = jnp.concatenate([names] * 4, axis=1)
    route_s[...] = jnp.zeros((16, 128), F32)
    for i in range(3):
        route_s[4 * i : 4 * i + 4, 0:4] = routes[i]
    named = jnp.zeros((16, 512), F32)
    share = jnp.zeros((16, 512), F32)
    for k in range(4):
        hit = names[16 * k : 16 * k + 16] == expert.astype(F32)
        named = named + jnp.where(hit, 1.0, 0.0)
        share = share + jnp.where(hit, route_s[:, k : k + 1], 0.0)
    below = (iota((16, 16), 1) < iota((16, 16), 0)).astype(F32).astype(BF16)
    earlier = dot(below, named.astype(BF16), NN)
    chosen = (named > 0.5) & (earlier == pick.astype(F32)) & (place < 9)
    chosen_tile = [chosen & (tile == c) for c in range(3)]
    select = jnp.concatenate([jnp.where(m, 1.0, 0.0) for m in chosen_tile], axis=0)
    select = select.T.astype(BF16)
    give = jnp.concatenate([jnp.where(m, share, 0.0) for m in chosen_tile], axis=0)
    give_hi = give.astype(BF16)
    give_lo = (give - give_hi.astype(F32)).astype(BF16)

    trow = iota((288, 512), 0)
    tcol = iota((288, 512), 1)
    ttile = (trow >= 96).astype(jnp.int32) + (trow >= 192).astype(jnp.int32)
    trest = trow - 96 * ttile
    spread = (
        ((trest & 31) == (tcol >> 4)) & ((tcol & 15) == 3 * (trest >> 5) + ttile)
    ).astype(F32).astype(BF16)

    ucol = iota((512, 288), 1)
    urow = iota((512, 288), 0)
    utile = (ucol >= 96).astype(jnp.int32) + (ucol >= 192).astype(jnp.int32)
    urest = ucol - 96 * utile
    gather = (
        ((urest & 31) == (urow >> 4)) & ((urow & 15) == 3 * (urest >> 5) + utile)
    ).astype(F32).astype(BF16)
    resid_s[...] = jnp.zeros((16, 3072), F32)
    for i in range(3):
        resid_s[4 * i : 4 * i + 4, 0:D] = resid[i].astype(F32)

    load_ow.wait()
    ow_v[pl.ds(D, 3072 - D), :] = jnp.zeros((3072 - D, 512), BF16)
    load_gate.wait()
    load_up.wait()
    load_dn.wait()
    gu_v[FFL:CH, :] = jnp.zeros((CH - FFL, D), BF16)
    gu_v[CH + FFL : 2 * CH, :] = jnp.zeros((CH - FFL, D), BF16)
    dn_v[FFL:CH, :] = jnp.zeros((CH - FFL, D), BF16)
    dn_w[:, 2816:3072] = jnp.zeros((CH, 256), BF16)
    dn_w[:, 0:D] = dn_v[...]
    gu_w[:, 2816:3072] = jnp.zeros((2 * CH, 256), BF16)
    gu_w[:, 0:D] = gu_v[...]
    gain_s[:, 2816:3072] = jnp.zeros((1, 256), F32)
    gain_s[:, 0:D] = gain[...]

    er = iota((128, 384), 0)
    ec = iota((128, 384), 1)
    expand = [
        (er == 8 * i + 4 * ((ec & 127) >> 6) + (ec >> 7)).astype(F32).astype(BF16)
        for i in range(3)
    ]
    for half in range(2):
        others(N_SEQ, me, lambda o: seq_arrival(*exchange(half), o).wait_recv())
        stat_rows = rcv1[half, :, 24:32, :].reshape((N_SEQ + 1) * 8, 128)
        sunk = sink[8 * half : 8 * half + 8]
        for i in range(3):
            wide = dot(stat_rows, expand[i], NN)
            peaks = wide[:, 0:128].reshape(N_SEQ + 1, 8, 128)
            totals = (wide[:, 128:256] + wide[:, 256:384]).reshape(N_SEQ + 1, 8, 128)
            top = jnp.maximum(jnp.max(peaks, axis=0), sunk)
            factor = jnp.exp(peaks - top[None])
            values = rcv1[half, :, 8 * i : 8 * i + 8, :].astype(F32)
            num = jnp.sum(values * factor, axis=0)
            den = jnp.sum(totals * factor, axis=0) + jnp.exp(sunk - top)
            att_s[16 * i + 8 * half : 16 * i + 8 * half + 8, :] = num / den
    att = att_s[...].astype(BF16)
    rr = iota((64, 48), 0)
    rc = iota((64, 48), 1)
    want = ((rr & 15) >> 2) * 16 + (rr >> 4) * 4 + (rr & 3)
    regroup = (rc == want).astype(F32).astype(BF16)
    mixed = dot(regroup, att, NN).astype(BF16)
    flat = jnp.concatenate([mixed[16 * p : 16 * p + 16] for p in range(4)], axis=1)

    def project(j):
        rows = ow_v[pl.ds(pl.multiple_of(j * CH, CH), CH), :]
        return dot(flat, rows, NT).astype(BF16)

    def send_projection(j):
        msg2[j] = project(j)
        head_copy(msg2, j, rcv2, send2, recv2, j).start()

    others(N_HEAD, head, send_projection)
    rcv2[head] = project(head)
    others(N_HEAD, head, lambda s: head_arrival(msg2, s, rcv2, send2, recv2, s).wait_recv())
    total = resid_s[:, pl.ds(pl.multiple_of(head * CH, CH), CH)]
    total = total + jnp.sum(rcv2[...].astype(F32), axis=0)
    hidden = total.astype(BF16)
    hidden_rows = jnp.concatenate([hidden[:, 128 * c : 128 * c + 128] for c in range(3)], axis=0)

    msg3[...] = dot(select, hidden_rows, NN).astype(BF16).reshape(N_SEQ, 16, 128)
    others(N_SEQ, me, lambda o: seq_copy(msg3, rcv3, send3, recv3, o).start())
    rcv3[me] = msg3[me]
    others(N_SEQ, me, lambda s: seq_arrival(msg3, rcv3, send3, recv3, s).wait_recv())
    got = dot(spread, rcv3[...].reshape(512, 128), NN).astype(BF16)
    mine = jnp.concatenate([got[96 * c : 96 * c + 96] for c in range(3)], axis=1)
    msg4[...] = mine
    gather_to = [2 * far[2] + core, 2 * far[0] + core, 2 * far[1] + core, sibling]
    for j in gather_to:
        head_copy(msg4, None, rcv4, send4, recv4, j).start()
    rcv4[head] = mine

    both_s[...] = jnp.zeros((ROWS, 2 * CH), F32)
    square_s[...] = jnp.zeros((ROWS, 128), F32)

    def use_chunk(j):
        cols = pl.ds(pl.multiple_of(j * CH, CH), CH)
        x = rcv4[j].astype(F32)
        square_s[...] += jnp.broadcast_to(jnp.sum(x * x, axis=1, keepdims=True), (ROWS, 128))
        both_s[...] += dot((x * gain_s[:, cols]).astype(BF16), gu_w[:, cols], NT)

    def forward(k, j):
        return pltpu.make_async_remote_copy(
            src_ref=rcv4.at[j],
            dst_ref=rcv4.at[j],
            send_sem=send_f.at[k],
            recv_sem=recv4.at[j],
            device_id=(me, sibling),
            device_id_type=MESH,
        )

    use_chunk(head)
    head_arrival(msg4, None, rcv4, send4, recv4, sibling).wait_recv()
    use_chunk(sibling)
    for k in range(3):
        j = 2 * far[k] + core
        head_arrival(msg4, None, rcv4, send4, recv4, j).wait_recv()
        forward(k, j).start()
        use_chunk(j)
    for k in range(3):
        j = 2 * far[k] + 1 - core
        forward(k, j).wait_recv()
        use_chunk(j)
    both = both_s[...]
    square = square_s[:, 0:1]
    scale = lax.rsqrt(square * (1.0 / D) + 1e-05)
    g = jnp.minimum(both[:, 0:CH] * scale, 7.0)
    u = jnp.clip(both[:, CH : 2 * CH] * scale, -7.0, 7.0)
    active = ((u + 1.0) * g * jax.nn.sigmoid(1.702 * g)).astype(BF16)

    def product(j):
        return dot(active, dn_w[:, pl.ds(pl.multiple_of(j * CH, CH), CH)], NN)

    def pair_copy(c):
        return pltpu.make_async_remote_copy(
            src_ref=msg_p.at[c],
            dst_ref=rcv_p.at[c],
            send_sem=send_p.at[c],
            recv_sem=recv_p.at[c],
            device_id=(me, sibling),
            device_id_type=MESH,
        )

    def chip_copy(c, slot):
        return pltpu.make_async_remote_copy(
            src_ref=msg5.at[c],
            dst_ref=rcv5.at[slot],
            send_sem=send5.at[c],
            recv_sem=recv5.at[slot],
            device_id=(me, 2 * c + core),
            device_id_type=MESH,
        )

    turns = [far[2], far[0], far[1], chip]
    for c in turns:
        msg_p[c] = product(2 * c + 1 - core).astype(BF16)
        pair_copy(c).start()
    for k, c in enumerate(turns):
        own = product(2 * c + core)
        pair_copy(c).wait_recv()
        both_cores = (own + rcv_p[c].astype(F32)).astype(BF16)
        if k < 3:
            msg5[c] = both_cores
            chip_copy(c, chip).start()
        else:
            rcv5[chip] = both_cores
    for c in far:
        chip_copy(c, c).wait_recv()
    summed = jnp.sum(rcv5[...].astype(F32), axis=0).astype(BF16)
    summed_rows = jnp.concatenate([summed[:, 128 * c : 128 * c + 128] for c in range(3)], axis=0)
    msg6[...] = dot(gather, summed_rows, NN).astype(BF16).reshape(N_SEQ, 16, 128)
    others(N_SEQ, me, lambda o: seq_copy(msg6, rcv6, send6, recv6, o).start())
    rcv6[me] = msg6[me]
    others(N_SEQ, me, lambda s: seq_arrival(msg6, rcv6, send6, recv6, s).wait_recv())
    back = rcv6[...].reshape(512, 128)
    added = dot(give_hi, back, NN) + dot(give_lo, back, NN)
    result = hidden_rows.astype(F32) + added
    result = jnp.concatenate([result[16 * c : 16 * c + 16] for c in range(3)], axis=1).astype(BF16)
    msg7[...] = result
    others(N_HEAD, head, lambda o: head_copy(msg7, None, rcv7, send7, recv7, o).start())
    rcv7[head] = result
    others(N_HEAD, head, lambda s: head_arrival(msg7, None, rcv7, send7, recv7, s).wait_recv())
    for i in range(3):
        for j in range(N_HEAD):
            width = CH if j < N_HEAD - 1 else LASTC
            out_ref[i, :, j * CH : j * CH + width] = rcv7[j, 4 * i : 4 * i + 4, 0:width]

    for msg, rcv, send, recv in (
        exchange(0),
        exchange(1),
        (msg3, rcv3, send3, recv3),
        (msg6, rcv6, send6, recv6),
    ):
        others(N_SEQ, me, lambda o: seq_copy(msg, rcv, send, recv, o).wait_send())
    for j in gather_to:
        head_copy(msg4, None, rcv4, send4, recv4, j).wait_send()
    for k in range(3):
        forward(k, 2 * far[k] + core).wait_send()
    for k, c in enumerate(turns):
        pair_copy(c).wait_send()
        if k < 3:
            chip_copy(c, chip).wait_send()
    others(N_HEAD, head, lambda o: head_copy(msg2, o, rcv2, send2, recv2, o).wait_send())
    others(N_HEAD, head, lambda o: head_copy(msg7, None, rcv7, send7, recv7, o).wait_send())


def on_device(
    new_query,
    fresh_key_value,
    prompt_cache,
    decoded_tail_cache,
    sinks,
    prompt_group,
    prompt_lens,
    tail_lens,
    o_weight,
    resid,
    norm_gain,
    expert_ids,
    route_weights,
    gate_up,
    down_weight,
):
    r = jnp.arange(REQ, dtype=jnp.int32)
    mine, other = prompt_group[:, None], prompt_group[None, :]
    ahead = (other < mine) | ((other == mine) & (r[None, :] < r[:, None]))
    rank = jnp.sum(ahead.astype(jnp.int32), axis=1)
    order = jnp.sum(jnp.where(rank[None, :] == r[:, None], r[None, :], 0), axis=1)
    freq = np.exp(np.arange(32) * (-2.0 * math.log(150000.0) / 64))
    freq = np.tile(freq.astype(np.float32), 4)
    step_angle = (np.arange(16) % 4)[:, None] * freq[None, :].astype(np.float64)
    tables = np.zeros((40, 128), np.float32)
    tables[0] = freq
    tables[8:24] = np.cos(step_angle)
    tables[24:40] = np.sin(step_angle)
    fresh = fresh_key_value.transpose(0, 2, 1, 3).reshape(3, 4, 128)
    ids = expert_ids.transpose(1, 2, 0)
    gain = norm_gain.reshape(1, D)
    q = new_query.reshape(REQ, 4, 4, 128).transpose(0, 2, 1, 3).reshape(REQ, 16, 128)
    prompt = prompt_cache.transpose(0, 2, 1, 3).reshape(GROUPS, PBLOCK, 128)
    tail = decoded_tail_cache.transpose(0, 2, 1, 3).reshape(REQ, TBLOCK, 128)
    ow = o_weight.T
    gu = gate_up.transpose(0, 2, 3, 1).reshape(2, FFL, D)
    dn = down_weight.reshape(FFL, D)

    smem = pl.BlockSpec(memory_space=pltpu.SMEM)
    vmem = pl.BlockSpec(memory_space=pltpu.VMEM)
    hbm = pl.BlockSpec(memory_space=pl.ANY)
    seq_sem = pltpu.SemaphoreType.DMA((N_SEQ,))
    head_sem = pltpu.SemaphoreType.DMA((N_HEAD,))
    chip_sem = pltpu.SemaphoreType.DMA((4,))
    out = pl.pallas_call(
        layer_kernel,
        name="layer",
        out_shape=jax.ShapeDtypeStruct((3, 4, D), BF16),
        in_specs=[smem] * 6 + [vmem] * 6 + [hbm] * 6,
        out_specs=vmem,
        scratch_shapes=[
            pltpu.VMEM((REQ, 16, 128), BF16),
            pltpu.VMEM((GROUPS, PBLOCK, 128), BF16),
            pltpu.VMEM((REQ, TBLOCK, 128), BF16),
            pltpu.VMEM((3072, 512), BF16),
            pltpu.VMEM((2 * CH, D), BF16),
            pltpu.VMEM((CH, D), BF16),
            pltpu.VMEM((CH, 3072), BF16),
            pltpu.VMEM((2 * CH, 3072), BF16),
            pltpu.VMEM((1, 3072), F32),
            pltpu.VMEM((REQ, 128), F32),
            pltpu.VMEM((REQ, 128), F32),
            pltpu.VMEM((16, 128), F32),
            pltpu.VMEM((48, 128), F32),
            pltpu.VMEM((16, 128), F32),
            pltpu.VMEM((16, 3072), F32),
            pltpu.VMEM((ROWS, 2 * CH), F32),
            pltpu.VMEM((ROWS, 128), F32),
            pltpu.VMEM((2 * REQ, 16, 128), BF16),
            pltpu.VMEM((MEMBERS * 16, PBLOCK + 128), F32),
            pltpu.VMEM((MEMBERS * 16, PBLOCK + 128), F32),
            pltpu.VMEM((MEMBERS * 16, 128), F32),
            pltpu.VMEM((MEMBERS * 16, 128), F32),
            pltpu.VMEM((2 * REQ, 8, 128), BF16),
            pltpu.VMEM((2 * REQ, 8, 128), F32),
            pltpu.VMEM((2, N_SEQ, 32, 128), BF16),
            pltpu.VMEM((2, N_SEQ + 1, 32, 128), BF16),
            pltpu.VMEM((N_HEAD, 16, CH), BF16),
            pltpu.VMEM((N_HEAD, 16, CH), BF16),
            pltpu.VMEM((N_SEQ, 16, 128), BF16),
            pltpu.VMEM((N_SEQ, 16, 128), BF16),
            pltpu.VMEM((ROWS, CH), BF16),
            pltpu.VMEM((N_HEAD, ROWS, CH), BF16),
            pltpu.VMEM((4, ROWS, CH), BF16),
            pltpu.VMEM((4, ROWS, CH), BF16),
            pltpu.VMEM((4, ROWS, CH), BF16),
            pltpu.VMEM((4, ROWS, CH), BF16),
            pltpu.VMEM((N_SEQ, 16, 128), BF16),
            pltpu.VMEM((N_SEQ, 16, 128), BF16),
            pltpu.VMEM((16, CH), BF16),
            pltpu.VMEM((N_HEAD, 16, CH), BF16),
            pltpu.SemaphoreType.DMA((6,)),
            pltpu.SemaphoreType.DMA((GROUPS,)),
            seq_sem,
            seq_sem,
            seq_sem,
            seq_sem,
            head_sem,
            head_sem,
            seq_sem,
            seq_sem,
            head_sem,
            head_sem,
            chip_sem,
            chip_sem,
            chip_sem,
            chip_sem,
            chip_sem,
            seq_sem,
            seq_sem,
            head_sem,
            head_sem,
        ],
        compiler_params=pltpu.CompilerParams(
            collective_id=0, has_side_effects=True, vmem_limit_bytes=56 * 1024 * 1024
        ),
    )(
        order,
        rank,
        prompt_group,
        tail_lens,
        prompt_lens,
        sinks,
        jnp.asarray(tables),
        fresh,
        ids,
        route_weights,
        resid,
        gain,
        q,
        prompt,
        tail,
        ow,
        gu,
        dn,
    )
    return out


def solution(mesh):
    return jax.shard_map(
        on_device,
        mesh=mesh,
        in_specs=(
            P(None, None, "head"),
            P("seq", None, "head", None),
            P(None, "seq", "head", None),
            P(None, "seq", "head", None),
            P("head"),
            P(),
            P(),
            P(),
            P("head", None),
            P("seq", None, None),
            P(),
            P(),
            P("seq", None, None),
            P("seq", None, None, "head"),
            P("seq", "head", None),
        ),
        out_specs=P("seq", None, None),
        check_vma=False,
    )
```

```python
import math

import jax
import jax.numpy as jnp
import numpy as np
from jax import lax
from jax.experimental import pallas as pl
from jax.experimental.pallas import tpu as pltpu
from jax.sharding import PartitionSpec as P

MESH = pl.DeviceIdType.MESH
LOW = -1e30
FLOOR = -1e29
F32 = jnp.float32
BF16 = jnp.bfloat16

N_SEQ = 32
N_HEAD = 8
REQ = 96
GROUPS = 8
MEMBERS = 12
PBLOCK = 1024
TBLOCK = 32
D = 2880
CH = 384
LASTC = 192
FFL = 360
ROWS = 96
HALF_PI = (1.5703125, 4.8351287841796875e-4, 3.1391647865048e-7)
NT = (((1,), (1,)), ((), ()))
NN = (((1,), (0,)), ((), ()))
TN = (((0,), (0,)), ((), ()))


def dot(a, b, dims):
    return lax.dot_general(a, b, dims, preferred_element_type=F32)


def iota(shape, axis):
    return lax.broadcasted_iota(jnp.int32, shape, axis)


def turned(x, cosine, sine, lane):
    ahead = pltpu.roll(x, 96, 1)
    behind = pltpu.roll(x, 32, 1)
    partner = jnp.where((lane & 63) < 32, -ahead, behind)
    return x * cosine + partner * sine


def cos_sin(angle):
    k = jnp.floor(angle * (2.0 / math.pi) + 0.5)
    r = angle - k * HALF_PI[0]
    r = r - k * HALF_PI[1]
    r = r - k * HALF_PI[2]
    r2 = r * r
    s = r + r * r2 * (-1.0 / 6 + r2 * (1.0 / 120 + r2 * (-1.0 / 5040 + r2 * (1.0 / 362880))))
    c = 1.0 + r2 * (-0.5 + r2 * (1.0 / 24 + r2 * (-1.0 / 720 + r2 * (1.0 / 40320))))
    quarter = k - 4.0 * jnp.floor(k * 0.25)
    odd = (quarter == 1.0) | (quarter == 3.0)
    cosine = jnp.where(odd, s, c)
    sine = jnp.where(odd, c, s)
    cosine = jnp.where((quarter == 1.0) | (quarter == 2.0), -cosine, cosine)
    sine = jnp.where(quarter >= 2.0, -sine, sine)
    return cosine, sine


def tiles_of(out, peak, lane):
    first, second = out[:16], out[16:]
    values = jnp.where(lane < 64, pltpu.roll(first, 64, 1), second).astype(BF16)
    hi0 = first.astype(BF16).astype(F32)
    hi1 = second.astype(BF16).astype(F32)
    lo0 = first - hi0
    lo1 = second - hi1
    stats = jnp.where(
        lane < 4,
        jnp.where(lane == 0, peak[:16], jnp.where(lane == 1, hi0, jnp.where(lane == 2, lo0, 0.0))),
        jnp.where(
            lane == 4, peak[16:], jnp.where(lane == 5, hi1, jnp.where(lane == 6, lo1, 0.0))
        ),
    )
    return values, jnp.where(lane < 8, stats, 0.0)


def layer_kernel(
    order,
    rank,
    prompt_group,
    tail_lens,
    prompt_lens,
    sinks,
    tables,
    fresh,
    ids,
    routes,
    resid,
    gain,
    q_hbm,
    prompt_hbm,
    tail_hbm,
    ow_hbm,
    gu_hbm,
    dn_hbm,
    out_ref,
    q_v,
    prompt_v,
    tail_v,
    ow_v,
    gu_v,
    dn_v,
    dn_w,
    gu_w,
    gain_s,
    cos_s,
    sin_s,
    small_s,
    route_s,
    resid_s,
    both_s,
    square_s,
    q_all,
    even_s,
    odd_s,
    even_top,
    odd_top,
    acc_s,
    stat_s,
    msg1,
    rcv1,
    msg2,
    rcv2,
    msg3,
    rcv3,
    msg4,
    rcv4,
    msg_p,
    rcv_p,
    msg5,
    rcv5,
    msg6,
    rcv6,
    msg7,
    rcv7,
    load_sem,
    prompt_sem,
    send1,
    recv1,
    send2,
    recv2,
    send3,
    recv3,
    send4,
    recv4,
    send_f,
    send_p,
    recv_p,
    send5,
    recv5,
    send6,
    recv6,
    send7,
    recv7,
):
    me = lax.axis_index("seq")
    head = lax.axis_index("head")
    barrier = pltpu.get_barrier_semaphore()

    def greet_seq(d, carry):
        pl.semaphore_signal(
            barrier, inc=1, device_id=(lax.rem(me + d, N_SEQ), head), device_id_type=MESH
        )
        return carry

    def greet_head(d, carry):
        pl.semaphore_signal(
            barrier, inc=1, device_id=(me, lax.rem(head + d, N_HEAD)), device_id_type=MESH
        )
        return carry

    load_q = pltpu.make_async_copy(q_hbm, q_v, load_sem.at[0])
    load_tail = pltpu.make_async_copy(tail_hbm, tail_v, load_sem.at[1])
    load_ow = pltpu.make_async_copy(ow_hbm, ow_v.at[pl.ds(0, D)], load_sem.at[2])
    load_gate = pltpu.make_async_copy(gu_hbm.at[0], gu_v.at[pl.ds(0, FFL)], load_sem.at[3])
    load_up = pltpu.make_async_copy(gu_hbm.at[1], gu_v.at[pl.ds(CH, FFL)], load_sem.at[5])
    load_dn = pltpu.make_async_copy(dn_hbm, dn_v.at[pl.ds(0, FFL)], load_sem.at[4])
    load_q.start()
    load_tail.start()

    def load_prompt(g):
        return pltpu.make_async_copy(prompt_hbm.at[g], prompt_v.at[g], prompt_sem.at[g])

    for g in range(GROUPS):
        load_prompt(g).start()
    load_ow.start()
    load_gate.start()
    load_up.start()
    load_dn.start()
    for d in range(1, N_SEQ):
        greet_seq(d, 0)
    for d in range(1, N_HEAD):
        greet_head(d, 0)

    lane = iota((16, 128), 1)
    row = iota((16, 128), 0)

    freq = tables[0:1, :]
    ct = tables[8:24, :]
    st = tables[24:40, :]

    def place(r):
        return (prompt_lens[prompt_group[r]] + tail_lens[r]).astype(F32)

    def put_angle(i, carry):
        cos_s[pl.ds(i, 1), :] = freq * place(order[i])
        return carry

    lax.fori_loop(0, REQ, put_angle, 0, unroll=8)
    cosine, sine = cos_sin(cos_s[...])
    cos_s[...] = cosine
    sin_s[...] = sine

    load_q.wait()

    def rotate_one(i, carry):
        r = order[i]
        x = q_v[r].astype(F32)
        c0 = cos_s[pl.ds(i, 1), :]
        s0 = sin_s[pl.ds(i, 1), :]
        y = turned(x, c0 * ct - s0 * st, s0 * ct + c0 * st, lane)
        y = y.astype(BF16).astype(F32) * 0.125
        q_all[i, 0:16, :] = jnp.where(lane < 64, y, 0.0).astype(BF16)
        q_all[i, 16:32, :] = jnp.where(
            lane < 64, pltpu.roll(y, 64, 1), 0.0
        ).astype(BF16)
        return carry

    lax.fori_loop(0, REQ, rotate_one, 0, unroll=4)
    load_tail.wait()

    key_col = iota((1, PBLOCK), 1) + me * PBLOCK
    col128 = iota((1, 128), 1)
    upper = (iota((1, 128), 1) >= 64).astype(F32).astype(BF16)
    lower = (iota((1, 128), 1) < 64).astype(F32).astype(BF16)
    same_req = (iota((128, 128), 0) >> 5) == (iota((128, 128), 1) >> 5)

    def tails(g):
        members = [order[g * MEMBERS + i] for i in range(MEMBERS)]
        return [
            jnp.concatenate([tail_v[r] for r in members[4 * b : 4 * b + 4]], axis=0)
            for b in range(3)
        ], members

    def scores(g, buf, tops):
        kv = prompt_v[g]
        bias = jnp.where(key_col < prompt_lens[g], 0.0, LOW)
        q = q_all[pl.ds(g * MEMBERS, MEMBERS)].reshape(MEMBERS * 32, 128)
        high = None
        for h in range(4):
            cols = slice(256 * h, 256 * h + 256)
            part = dot(q, kv[cols], NT) + bias[:, cols]
            buf[:, cols] = part
            part = jnp.maximum(part[:, :128], part[:, 128:])
            high = part if high is None else jnp.maximum(high, part)
        keys, members = tails(g)
        for b in range(3):
            rows = slice(128 * b, 128 * b + 128)
            limit = jnp.zeros((1, 128), jnp.int32)
            for i in range(4):
                limit = jnp.where((col128 >> 5) == i, tail_lens[members[4 * b + i]], limit)
            seen = same_req & (((col128 & 31) + me * TBLOCK) < limit)
            part = jnp.where(seen, dot(q[rows], keys[b], NT), LOW)
            buf[rows, PBLOCK : PBLOCK + 128] = part
            top = jnp.max(jnp.maximum(high[rows], part), axis=1, keepdims=True)
            top = jnp.maximum(top, FLOOR).astype(BF16).astype(F32)
            tops[rows, :] = jnp.broadcast_to(top, (128, 128))

    def weigh(g, buf, tops):
        first = g * MEMBERS
        kv = prompt_v[g]
        vx = kv * upper + lower
        keys, members = tails(g)
        peaks = tops[...]
        w = jnp.concatenate(
            [
                jnp.exp(buf[:, 128 * h : 128 * h + 128] - peaks).astype(BF16)
                for h in range(PBLOCK // 128)
            ],
            axis=1,
        )
        w2 = jnp.exp(buf[:, PBLOCK : PBLOCK + 128] - peaks).astype(BF16)
        whole = dot(w, vx, NN)
        for b in range(3):
            rows = slice(128 * b, 128 * b + 128)
            peak = peaks[rows]
            o = whole[rows] + dot(w2[rows], keys[b] * upper + lower, NN)
            for i in range(4):
                values, stats = tiles_of(o[32 * i : 32 * i + 32], peak[32 * i : 32 * i + 32], lane)
                acc_s[first + 4 * b + i] = values
                stat_s[first + 4 * b + i] = stats

    for g in range(GROUPS):
        load_prompt(g).wait()
    scores(0, even_s, even_top)

    def two_groups(k, carry):
        g = 2 * k
        scores(g + 1, odd_s, odd_top)
        weigh(g, even_s, even_top)
        scores(jnp.minimum(g + 2, GROUPS - 1), even_s, even_top)
        weigh(g + 1, odd_s, odd_top)
        return carry

    lax.fori_loop(0, GROUPS // 2, two_groups, 0)

    pl.semaphore_wait(barrier, N_SEQ - 1 + N_HEAD - 1)

    def pack(dst, slot, o):
        total = jnp.zeros((16, 128), F32)
        for i in range(3):
            k = rank[3 * o + i]
            dst[slot, 16 * i : 16 * i + 16, :] = acc_s[k]
            piece = stat_s[k]
            total = total + (piece if i == 0 else pltpu.roll(piece, 8 * i, 1))
        dst[slot, 48:56, :] = (total[:8] + pltpu.roll(total[8:], 64, 1)).astype(BF16)

    def seq_copy(msg, rcv, send, recv, to):
        return pltpu.make_async_remote_copy(
            src_ref=msg.at[to],
            dst_ref=rcv.at[me],
            send_sem=send.at[to],
            recv_sem=recv.at[me],
            device_id=(to, head),
            device_id_type=MESH,
        )

    def seq_arrival(msg, rcv, send, recv, source):
        return pltpu.make_async_remote_copy(
            src_ref=msg.at[source],
            dst_ref=rcv.at[source],
            send_sem=send.at[source],
            recv_sem=recv.at[source],
            device_id=(source, head),
            device_id_type=MESH,
        )

    def head_copy(msg, slot, rcv, send, recv, to):
        return pltpu.make_async_remote_copy(
            src_ref=msg if slot is None else msg.at[slot],
            dst_ref=rcv.at[head],
            send_sem=send.at[to],
            recv_sem=recv.at[head],
            device_id=(me, to),
            device_id_type=MESH,
        )

    def head_arrival(msg, slot, rcv, send, recv, source):
        return pltpu.make_async_remote_copy(
            src_ref=msg if slot is None else msg.at[slot],
            dst_ref=rcv.at[source],
            send_sem=send.at[source],
            recv_sem=recv.at[source],
            device_id=(me, source),
            device_id_type=MESH,
        )

    def others(count, mine, body):
        for d in range(1, count):
            body(lax.rem(mine + d, count))

    core = lax.rem(head, 2)
    chip = head // 2
    near = chip + 1 - 2 * lax.rem(chip, 2)
    sibling = 2 * chip + 1 - core
    far = [near, 3 - chip, lax.rem(chip + 2, 4)]

    def send_partials(o):
        pack(msg1, o, o)
        seq_copy(msg1, rcv1, send1, recv1, o).start()

    others(N_SEQ, me, send_partials)
    pack(rcv1, me, me)

    angle = jnp.zeros((16, 128), F32)
    for i in range(3):
        angle = jnp.where((row >> 2) == i, freq * place(me * 3 + i), angle)
        small_s[4 * i : 4 * i + 4, :] = fresh[i].astype(F32)
    base_c, base_s = cos_sin(angle)
    small_s[12:16, :] = jnp.zeros((4, 128), F32)
    kv_new = small_s[...]
    key_new = turned(kv_new, base_c * ct - base_s * st, base_s * ct + base_c * st, lane)
    kn = jnp.where(lane < 64, key_new, kv_new).astype(BF16)
    vn = jnp.where(lane < 64, 1.0, kv_new).astype(BF16)
    fresh_stats = jnp.zeros((16, 128), F32)
    srow = iota((32, 16), 0)
    scol = iota((32, 16), 1)
    for i in range(3):
        k = rank[3 * me + i]
        q = q_all[k]
        seen = ((scol >> 2) == i) & ((scol & 3) <= (srow & 3))
        s = jnp.where(seen, dot(q, kn, NT), LOW)
        peak = jnp.max(s, axis=1, keepdims=True).astype(BF16).astype(F32)
        w = jnp.exp(s - peak).astype(BF16)
        values, stats = tiles_of(dot(w, vn, NN), peak, lane)
        rcv1[N_SEQ, 16 * i : 16 * i + 16, :] = values
        fresh_stats = fresh_stats + (stats if i == 0 else pltpu.roll(stats, 8 * i, 1))
    folded = fresh_stats[:8] + pltpu.roll(fresh_stats[8:], 64, 1)
    rcv1[N_SEQ, 48:56, :] = folded.astype(BF16)

    sink = jnp.zeros((16, 128), F32)
    for j in range(8):
        here = ((row >> 2) == (j >> 1)) & ((lane >> 6) == (j & 1))
        sink = jnp.where(here, sinks[j], sink)

    wide_lane = iota((16, 512), 1)
    expert = wide_lane >> 4
    place = wide_lane & 15
    pick = (place >= 3).astype(jnp.int32) + (place >= 6).astype(jnp.int32)
    tile = place - 3 * pick
    own = (iota((REQ, 384), 0) == me * 3 + (iota((REQ, 384), 1) >> 7)).astype(F32).astype(BF16)
    flat_ids = jnp.concatenate([ids[t] for t in range(4)], axis=0).astype(F32).astype(BF16)
    own_ids = dot(flat_ids, own, NN).astype(BF16)
    xr = iota((64, 16), 0)
    xc = iota((64, 16), 1)
    names = jnp.full((64, 128), -1.0, F32) * ((iota((64, 128), 0) & 15) >= 12).astype(F32)
    for i in range(3):
        take = (xc == (xr & 3) * 4 + (xr >> 4)) & (((xr & 15) >> 2) == i)
        names = names + dot(
            take.astype(F32).astype(BF16), own_ids[:, 128 * i : 128 * i + 128], NN
        )
    names = jnp.concatenate([names] * 4, axis=1)
    route_s[...] = jnp.zeros((16, 128), F32)
    for i in range(3):
        route_s[4 * i : 4 * i + 4, 0:4] = routes[i]
    named = jnp.zeros((16, 512), F32)
    share = jnp.zeros((16, 512), F32)
    for k in range(4):
        hit = names[16 * k : 16 * k + 16] == expert.astype(F32)
        named = named + jnp.where(hit, 1.0, 0.0)
        share = share + jnp.where(hit, route_s[:, k : k + 1], 0.0)
    below = (iota((16, 16), 1) < iota((16, 16), 0)).astype(F32).astype(BF16)
    earlier = dot(below, named.astype(BF16), NN)
    chosen = (named > 0.5) & (earlier == pick.astype(F32)) & (place < 9)
    chosen_tile = [chosen & (tile == c) for c in range(3)]
    select = jnp.concatenate([jnp.where(m, 1.0, 0.0) for m in chosen_tile], axis=0)
    select = select.T.astype(BF16)
    give = jnp.concatenate([jnp.where(m, share, 0.0) for m in chosen_tile], axis=0)
    give_hi = give.astype(BF16)
    give_lo = (give - give_hi.astype(F32)).astype(BF16)

    trow = iota((288, 512), 0)
    tcol = iota((288, 512), 1)
    ttile = (trow >= 96).astype(jnp.int32) + (trow >= 192).astype(jnp.int32)
    trest = trow - 96 * ttile
    spread = (
        ((trest & 31) == (tcol >> 4)) & ((tcol & 15) == 3 * (trest >> 5) + ttile)
    ).astype(F32).astype(BF16)

    ucol = iota((512, 288), 1)
    urow = iota((512, 288), 0)
    utile = (ucol >= 96).astype(jnp.int32) + (ucol >= 192).astype(jnp.int32)
    urest = ucol - 96 * utile
    gather = (
        ((urest & 31) == (urow >> 4)) & ((urow & 15) == 3 * (urest >> 5) + utile)
    ).astype(F32).astype(BF16)
    resid_s[...] = jnp.zeros((16, 3072), F32)
    for i in range(3):
        resid_s[4 * i : 4 * i + 4, 0:D] = resid[i].astype(F32)

    load_ow.wait()
    ow_v[pl.ds(D, 3072 - D), :] = jnp.zeros((3072 - D, 512), BF16)
    load_gate.wait()
    load_up.wait()
    load_dn.wait()
    gu_v[FFL:CH, :] = jnp.zeros((CH - FFL, D), BF16)
    gu_v[CH + FFL : 2 * CH, :] = jnp.zeros((CH - FFL, D), BF16)
    dn_v[FFL:CH, :] = jnp.zeros((CH - FFL, D), BF16)
    dn_w[:, 2816:3072] = jnp.zeros((CH, 256), BF16)
    dn_w[:, 0:D] = dn_v[...]
    gu_w[:, 2816:3072] = jnp.zeros((2 * CH, 256), BF16)
    gu_w[:, 0:D] = gu_v[...]
    gain_s[:, 2816:3072] = jnp.zeros((1, 256), F32)
    gain_s[:, 0:D] = gain[...].reshape(1, D)

    others(N_SEQ, me, lambda s: seq_arrival(msg1, rcv1, send1, recv1, s).wait_recv())

    stat_rows = rcv1[:, 48:56, :].reshape((N_SEQ + 1) * 8, 128)
    er = iota((128, 384), 0)
    ec = iota((128, 384), 1)
    attended = []
    for i in range(3):
        for half in range(2):
            spot = 64 * half + 8 * i + 4 * ((ec & 127) >> 6) + (ec >> 7)
            expand = (er == spot).astype(F32).astype(BF16)
            wide = dot(stat_rows, expand, NN)
            peaks = wide[:, 0:128].reshape(N_SEQ + 1, 8, 128)
            totals = (wide[:, 128:256] + wide[:, 256:384]).reshape(N_SEQ + 1, 8, 128)
            sunk = sink[8 * half : 8 * half + 8]
            top = jnp.maximum(jnp.max(peaks, axis=0), sunk)
            factor = jnp.exp(peaks - top[None])
            start = 16 * i + 8 * half
            values = rcv1[:, start : start + 8, :].astype(F32)
            num = jnp.sum(values * factor, axis=0)
            den = jnp.sum(totals * factor, axis=0) + jnp.exp(sunk - top)
            attended.append(num / den)
    att = jnp.concatenate(attended, axis=0).astype(BF16)
    rr = iota((64, 48), 0)
    rc = iota((64, 48), 1)
    want = ((rr & 15) >> 2) * 16 + (rr >> 4) * 4 + (rr & 3)
    regroup = (rc == want).astype(F32).astype(BF16)
    mixed = dot(regroup, att, NN).astype(BF16)
    flat = jnp.concatenate([mixed[16 * p : 16 * p + 16] for p in range(4)], axis=1)

    def project(j):
        rows = ow_v[pl.ds(pl.multiple_of(j * CH, CH), CH), :]
        return dot(flat, rows, NT).astype(BF16)

    def send_projection(j):
        msg2[j] = project(j)
        head_copy(msg2, j, rcv2, send2, recv2, j).start()

    others(N_HEAD, head, send_projection)
    rcv2[head] = project(head)
    others(N_HEAD, head, lambda s: head_arrival(msg2, s, rcv2, send2, recv2, s).wait_recv())
    total = resid_s[:, pl.ds(pl.multiple_of(head * CH, CH), CH)]
    total = total + jnp.sum(rcv2[...].astype(F32), axis=0)
    hidden = total.astype(BF16)
    hidden_rows = jnp.concatenate([hidden[:, 128 * c : 128 * c + 128] for c in range(3)], axis=0)

    msg3[...] = dot(select, hidden_rows, NN).astype(BF16).reshape(N_SEQ, 16, 128)
    others(N_SEQ, me, lambda o: seq_copy(msg3, rcv3, send3, recv3, o).start())
    rcv3[me] = msg3[me]
    others(N_SEQ, me, lambda s: seq_arrival(msg3, rcv3, send3, recv3, s).wait_recv())
    got = dot(spread, rcv3[...].reshape(512, 128), NN).astype(BF16)
    mine = jnp.concatenate([got[96 * c : 96 * c + 96] for c in range(3)], axis=1)
    msg4[...] = mine
    gather_to = [2 * far[2] + core, 2 * far[0] + core, 2 * far[1] + core, sibling]
    for j in gather_to:
        head_copy(msg4, None, rcv4, send4, recv4, j).start()
    rcv4[head] = mine

    both_s[...] = jnp.zeros((ROWS, 2 * CH), F32)
    square_s[...] = jnp.zeros((ROWS, 128), F32)

    def use_chunk(j):
        cols = pl.ds(pl.multiple_of(j * CH, CH), CH)
        x = rcv4[j].astype(F32)
        square_s[...] += jnp.broadcast_to(jnp.sum(x * x, axis=1, keepdims=True), (ROWS, 128))
        both_s[...] += dot((x * gain_s[:, cols]).astype(BF16), gu_w[:, cols], NT)

    def forward(k, j):
        return pltpu.make_async_remote_copy(
            src_ref=rcv4.at[j],
            dst_ref=rcv4.at[j],
            send_sem=send_f.at[k],
            recv_sem=recv4.at[j],
            device_id=(me, sibling),
            device_id_type=MESH,
        )

    use_chunk(head)
    head_arrival(msg4, None, rcv4, send4, recv4, sibling).wait_recv()
    use_chunk(sibling)
    for k in range(3):
        j = 2 * far[k] + core
        head_arrival(msg4, None, rcv4, send4, recv4, j).wait_recv()
        forward(k, j).start()
        use_chunk(j)
    for k in range(3):
        j = 2 * far[k] + 1 - core
        forward(k, j).wait_recv()
        use_chunk(j)
    both = both_s[...]
    square = square_s[:, 0:1]
    scale = lax.rsqrt(square * (1.0 / D) + 1e-05)
    g = jnp.minimum(both[:, 0:CH] * scale, 7.0)
    u = jnp.clip(both[:, CH : 2 * CH] * scale, -7.0, 7.0)
    active = ((u + 1.0) * g * jax.nn.sigmoid(1.702 * g)).astype(BF16)

    def product(j):
        return dot(active, dn_w[:, pl.ds(pl.multiple_of(j * CH, CH), CH)], NN)

    def pair_copy(c):
        return pltpu.make_async_remote_copy(
            src_ref=msg_p.at[c],
            dst_ref=rcv_p.at[c],
            send_sem=send_p.at[c],
            recv_sem=recv_p.at[c],
            device_id=(me, sibling),
            device_id_type=MESH,
        )

    def chip_copy(c, slot):
        return pltpu.make_async_remote_copy(
            src_ref=msg5.at[c],
            dst_ref=rcv5.at[slot],
            send_sem=send5.at[c],
            recv_sem=recv5.at[slot],
            device_id=(me, 2 * c + core),
            device_id_type=MESH,
        )

    turns = [far[2], far[0], far[1], chip]
    for c in turns:
        msg_p[c] = product(2 * c + 1 - core).astype(BF16)
        pair_copy(c).start()
    for k, c in enumerate(turns):
        own = product(2 * c + core)
        pair_copy(c).wait_recv()
        both_cores = (own + rcv_p[c].astype(F32)).astype(BF16)
        if k < 3:
            msg5[c] = both_cores
            chip_copy(c, chip).start()
        else:
            rcv5[chip] = both_cores
    for c in far:
        chip_copy(c, c).wait_recv()
    summed = jnp.sum(rcv5[...].astype(F32), axis=0).astype(BF16)
    summed_rows = jnp.concatenate([summed[:, 128 * c : 128 * c + 128] for c in range(3)], axis=0)
    msg6[...] = dot(gather, summed_rows, NN).astype(BF16).reshape(N_SEQ, 16, 128)
    others(N_SEQ, me, lambda o: seq_copy(msg6, rcv6, send6, recv6, o).start())
    rcv6[me] = msg6[me]
    others(N_SEQ, me, lambda s: seq_arrival(msg6, rcv6, send6, recv6, s).wait_recv())
    back = rcv6[...].reshape(512, 128)
    added = dot(give_hi, back, NN) + dot(give_lo, back, NN)
    result = hidden_rows.astype(F32) + added
    result = jnp.concatenate([result[16 * c : 16 * c + 16] for c in range(3)], axis=1).astype(BF16)
    msg7[...] = result
    others(N_HEAD, head, lambda o: head_copy(msg7, None, rcv7, send7, recv7, o).start())
    rcv7[head] = result
    others(N_HEAD, head, lambda s: head_arrival(msg7, None, rcv7, send7, recv7, s).wait_recv())
    for i in range(3):
        for j in range(N_HEAD):
            out_ref[i, :, j * CH : j * CH + CH] = rcv7[j, 4 * i : 4 * i + 4, :]

    for msg, rcv, send, recv in (
        (msg1, rcv1, send1, recv1),
        (msg3, rcv3, send3, recv3),
        (msg6, rcv6, send6, recv6),
    ):
        others(N_SEQ, me, lambda o: seq_copy(msg, rcv, send, recv, o).wait_send())
    for j in gather_to:
        head_copy(msg4, None, rcv4, send4, recv4, j).wait_send()
    for k in range(3):
        forward(k, 2 * far[k] + core).wait_send()
    for k, c in enumerate(turns):
        pair_copy(c).wait_send()
        if k < 3:
            chip_copy(c, chip).wait_send()
    others(N_HEAD, head, lambda o: head_copy(msg2, o, rcv2, send2, recv2, o).wait_send())
    others(N_HEAD, head, lambda o: head_copy(msg7, None, rcv7, send7, recv7, o).wait_send())


def on_device(
    new_query,
    fresh_key_value,
    prompt_cache,
    decoded_tail_cache,
    sinks,
    prompt_group,
    prompt_lens,
    tail_lens,
    o_weight,
    resid,
    norm_gain,
    expert_ids,
    route_weights,
    gate_up,
    down_weight,
):
    r = jnp.arange(REQ, dtype=jnp.int32)
    mine, other = prompt_group[:, None], prompt_group[None, :]
    ahead = (other < mine) | ((other == mine) & (r[None, :] < r[:, None]))
    rank = jnp.sum(ahead.astype(jnp.int32), axis=1)
    order = jnp.sum(jnp.where(rank[None, :] == r[:, None], r[None, :], 0), axis=1)
    freq = np.exp(np.arange(32) * (-2.0 * math.log(150000.0) / 64))
    freq = np.tile(freq.astype(np.float32), 4)
    step_angle = (np.arange(16) % 4)[:, None] * freq[None, :].astype(np.float64)
    tables = np.zeros((40, 128), np.float32)
    tables[0] = freq
    tables[8:24] = np.cos(step_angle)
    tables[24:40] = np.sin(step_angle)
    fresh = fresh_key_value.transpose(0, 2, 1, 3).reshape(3, 4, 128)
    ids = expert_ids.transpose(1, 2, 0)
    q = new_query.reshape(REQ, 4, 4, 128).transpose(0, 2, 1, 3).reshape(REQ, 16, 128)
    prompt = prompt_cache.transpose(0, 2, 1, 3).reshape(GROUPS, PBLOCK, 128)
    tail = decoded_tail_cache.transpose(0, 2, 1, 3).reshape(REQ, TBLOCK, 128)
    ow = o_weight.T
    gu = gate_up.transpose(0, 2, 3, 1).reshape(2, FFL, D)
    dn = down_weight.reshape(FFL, D)

    smem = pl.BlockSpec(memory_space=pltpu.SMEM)
    vmem = pl.BlockSpec(memory_space=pltpu.VMEM)
    hbm = pl.BlockSpec(memory_space=pl.ANY)
    seq_sem = pltpu.SemaphoreType.DMA((N_SEQ,))
    head_sem = pltpu.SemaphoreType.DMA((N_HEAD,))
    chip_sem = pltpu.SemaphoreType.DMA((4,))
    out = pl.pallas_call(
        layer_kernel,
        name="layer",
        out_shape=jax.ShapeDtypeStruct((3, 4, 3072), BF16),
        in_specs=[smem] * 6 + [vmem] * 6 + [hbm] * 6,
        out_specs=vmem,
        scratch_shapes=[
            pltpu.VMEM((REQ, 16, 128), BF16),
            pltpu.VMEM((GROUPS, PBLOCK, 128), BF16),
            pltpu.VMEM((REQ, TBLOCK, 128), BF16),
            pltpu.VMEM((3072, 512), BF16),
            pltpu.VMEM((2 * CH, D), BF16),
            pltpu.VMEM((CH, D), BF16),
            pltpu.VMEM((CH, 3072), BF16),
            pltpu.VMEM((2 * CH, 3072), BF16),
            pltpu.VMEM((1, 3072), F32),
            pltpu.VMEM((REQ, 128), F32),
            pltpu.VMEM((REQ, 128), F32),
            pltpu.VMEM((16, 128), F32),
            pltpu.VMEM((16, 128), F32),
            pltpu.VMEM((16, 3072), F32),
            pltpu.VMEM((ROWS, 2 * CH), F32),
            pltpu.VMEM((ROWS, 128), F32),
            pltpu.VMEM((REQ, 32, 128), BF16),
            pltpu.VMEM((MEMBERS * 32, PBLOCK + 128), F32),
            pltpu.VMEM((MEMBERS * 32, PBLOCK + 128), F32),
            pltpu.VMEM((MEMBERS * 32, 128), F32),
            pltpu.VMEM((MEMBERS * 32, 128), F32),
            pltpu.VMEM((REQ, 16, 128), BF16),
            pltpu.VMEM((REQ, 16, 128), F32),
            pltpu.VMEM((N_SEQ, 56, 128), BF16),
            pltpu.VMEM((N_SEQ + 1, 56, 128), BF16),
            pltpu.VMEM((N_HEAD, 16, CH), BF16),
            pltpu.VMEM((N_HEAD, 16, CH), BF16),
            pltpu.VMEM((N_SEQ, 16, 128), BF16),
            pltpu.VMEM((N_SEQ, 16, 128), BF16),
            pltpu.VMEM((ROWS, CH), BF16),
            pltpu.VMEM((N_HEAD, ROWS, CH), BF16),
            pltpu.VMEM((4, ROWS, CH), BF16),
            pltpu.VMEM((4, ROWS, CH), BF16),
            pltpu.VMEM((4, ROWS, CH), BF16),
            pltpu.VMEM((4, ROWS, CH), BF16),
            pltpu.VMEM((N_SEQ, 16, 128), BF16),
            pltpu.VMEM((N_SEQ, 16, 128), BF16),
            pltpu.VMEM((16, CH), BF16),
            pltpu.VMEM((N_HEAD, 16, CH), BF16),
            pltpu.SemaphoreType.DMA((6,)),
            pltpu.SemaphoreType.DMA((GROUPS,)),
            seq_sem,
            seq_sem,
            head_sem,
            head_sem,
            seq_sem,
            seq_sem,
            head_sem,
            head_sem,
            chip_sem,
            chip_sem,
            chip_sem,
            chip_sem,
            chip_sem,
            seq_sem,
            seq_sem,
            head_sem,
            head_sem,
        ],
        compiler_params=pltpu.CompilerParams(
            collective_id=0, has_side_effects=True, vmem_limit_bytes=56 * 1024 * 1024
        ),
    )(
        order,
        rank,
        prompt_group,
        tail_lens,
        prompt_lens,
        sinks,
        jnp.asarray(tables),
        fresh,
        ids,
        route_weights,
        resid,
        norm_gain,
        q,
        prompt,
        tail,
        ow,
        gu,
        dn,
    )
    return out[:, :, :D]


def solution(mesh):
    return jax.shard_map(
        on_device,
        mesh=mesh,
        in_specs=(
            P(None, None, "head"),
            P("seq", None, "head", None),
            P(None, "seq", "head", None),
            P(None, "seq", "head", None),
            P("head"),
            P(),
            P(),
            P(),
            P("head", None),
            P("seq", None, None),
            P(),
            P(),
            P("seq", None, None),
            P("seq", None, None, "head"),
            P("seq", "head", None),
        ),
        out_specs=P("seq", None, None),
        check_vma=False,
    )
```

```python
import math

import jax
import jax.numpy as jnp
import numpy as np
from jax import lax
from jax.experimental import pallas as pl
from jax.experimental.pallas import tpu as pltpu
from jax.sharding import PartitionSpec as P

MESH = pl.DeviceIdType.MESH
LOW = -1e30
FLOOR = -1e29
F32 = jnp.float32
BF16 = jnp.bfloat16

N_SEQ = 32
N_HEAD = 8
REQ = 96
GROUPS = 8
MEMBERS = 12
PBLOCK = 1024
TBLOCK = 32
D = 2880
CH = 384
LASTC = 192
FFL = 360
ROWS = 96
HALF_PI = (1.5703125, 4.8351287841796875e-4, 3.1391647865048e-7)
NT = (((1,), (1,)), ((), ()))
NN = (((1,), (0,)), ((), ()))
TN = (((0,), (0,)), ((), ()))


SEQ_ORDER = sorted(
    ((dy, dz) for dy in range(4) for dz in range(8) if dy or dz),
    key=lambda o: (-min(o[0], 4 - o[0]) - min(o[1], 8 - o[1]), (o[0] * 3 + o[1] * 5) % 8),
)


def dot(a, b, dims):
    return lax.dot_general(a, b, dims, preferred_element_type=F32)


def iota(shape, axis):
    return lax.broadcasted_iota(jnp.int32, shape, axis)


def turned(x, cosine, sine, lane):
    ahead = pltpu.roll(x, 96, 1)
    behind = pltpu.roll(x, 32, 1)
    partner = jnp.where((lane & 63) < 32, -ahead, behind)
    return x * cosine + partner * sine


def cos_sin(angle):
    k = jnp.floor(angle * (2.0 / math.pi) + 0.5)
    r = angle - k * HALF_PI[0]
    r = r - k * HALF_PI[1]
    r = r - k * HALF_PI[2]
    r2 = r * r
    s = r + r * r2 * (-1.0 / 6 + r2 * (1.0 / 120 + r2 * (-1.0 / 5040 + r2 * (1.0 / 362880))))
    c = 1.0 + r2 * (-0.5 + r2 * (1.0 / 24 + r2 * (-1.0 / 720 + r2 * (1.0 / 40320))))
    quarter = k - 4.0 * jnp.floor(k * 0.25)
    odd = (quarter == 1.0) | (quarter == 3.0)
    cosine = jnp.where(odd, s, c)
    sine = jnp.where(odd, c, s)
    cosine = jnp.where((quarter == 1.0) | (quarter == 2.0), -cosine, cosine)
    sine = jnp.where(quarter >= 2.0, -sine, sine)
    return cosine, sine


def tiles_of(out, peak, lane):
    first, second = out[:16], out[16:]
    values = jnp.where(lane < 64, pltpu.roll(first, 64, 1), second).astype(BF16)
    hi0 = first.astype(BF16).astype(F32)
    hi1 = second.astype(BF16).astype(F32)
    lo0 = first - hi0
    lo1 = second - hi1
    stats = jnp.where(
        lane < 4,
        jnp.where(lane == 0, peak[:16], jnp.where(lane == 1, hi0, jnp.where(lane == 2, lo0, 0.0))),
        jnp.where(
            lane == 4, peak[16:], jnp.where(lane == 5, hi1, jnp.where(lane == 6, lo1, 0.0))
        ),
    )
    return values, jnp.where(lane < 8, stats, 0.0)


def layer_kernel(
    order,
    rank,
    prompt_group,
    tail_lens,
    prompt_lens,
    sinks,
    tables,
    fresh,
    ids,
    routes,
    resid,
    gain,
    q_hbm,
    prompt_hbm,
    tail_hbm,
    ow_hbm,
    gu_hbm,
    dn_hbm,
    out_ref,
    q_v,
    prompt_v,
    tail_v,
    ow_v,
    gu_v,
    dn_v,
    dn_w,
    gu_w,
    gain_s,
    cos_s,
    sin_s,
    small_s,
    route_s,
    resid_s,
    both_s,
    square_s,
    q_all,
    even_s,
    odd_s,
    even_top,
    odd_top,
    acc_s,
    stat_s,
    msg1,
    rcv1,
    msg2,
    rcv2,
    msg3,
    rcv3,
    msg4,
    rcv4,
    msg_p,
    rcv_p,
    msg5,
    rcv5,
    msg6,
    rcv6,
    msg7,
    rcv7,
    load_sem,
    prompt_sem,
    send1,
    recv1,
    send2,
    recv2,
    send3,
    recv3,
    send4,
    recv4,
    send_f,
    send_p,
    recv_p,
    send5,
    recv5,
    send6,
    recv6,
    send7,
    recv7,
):
    me = lax.axis_index("seq")
    head = lax.axis_index("head")
    barrier = pltpu.get_barrier_semaphore()

    def greet_seq(d, carry):
        pl.semaphore_signal(
            barrier, inc=1, device_id=(lax.rem(me + d, N_SEQ), head), device_id_type=MESH
        )
        return carry

    def greet_head(d, carry):
        pl.semaphore_signal(
            barrier, inc=1, device_id=(me, lax.rem(head + d, N_HEAD)), device_id_type=MESH
        )
        return carry

    load_q = pltpu.make_async_copy(q_hbm, q_v, load_sem.at[0])
    load_tail = pltpu.make_async_copy(tail_hbm, tail_v, load_sem.at[1])
    load_ow = pltpu.make_async_copy(ow_hbm, ow_v.at[pl.ds(0, D)], load_sem.at[2])
    load_gate = pltpu.make_async_copy(gu_hbm.at[0], gu_v.at[pl.ds(0, FFL)], load_sem.at[3])
    load_up = pltpu.make_async_copy(gu_hbm.at[1], gu_v.at[pl.ds(CH, FFL)], load_sem.at[5])
    load_dn = pltpu.make_async_copy(dn_hbm, dn_v.at[pl.ds(0, FFL)], load_sem.at[4])
    load_q.start()
    load_tail.start()

    def load_prompt(g):
        return pltpu.make_async_copy(prompt_hbm.at[g], prompt_v.at[g], prompt_sem.at[g])

    for g in range(GROUPS):
        load_prompt(g).start()
    load_ow.start()
    load_gate.start()
    load_up.start()
    load_dn.start()
    for d in range(1, N_SEQ):
        greet_seq(d, 0)
    for d in range(1, N_HEAD):
        greet_head(d, 0)

    lane = iota((16, 128), 1)
    row = iota((16, 128), 0)

    freq = tables[0:1, :]
    ct = tables[8:24, :]
    st = tables[24:40, :]

    def place(r):
        return (prompt_lens[prompt_group[r]] + tail_lens[r]).astype(F32)

    def put_angle(i, carry):
        cos_s[pl.ds(i, 1), :] = freq * place(order[i])
        return carry

    lax.fori_loop(0, REQ, put_angle, 0, unroll=8)
    cosine, sine = cos_sin(cos_s[...])
    cos_s[...] = cosine
    sin_s[...] = sine

    load_q.wait()

    def rotate_one(i, carry):
        r = order[i]
        x = q_v[r].astype(F32)
        c0 = cos_s[pl.ds(i, 1), :]
        s0 = sin_s[pl.ds(i, 1), :]
        y = turned(x, c0 * ct - s0 * st, s0 * ct + c0 * st, lane)
        y = y.astype(BF16).astype(F32) * 0.125
        q_all[i, 0:16, :] = jnp.where(lane < 64, y, 0.0).astype(BF16)
        q_all[i, 16:32, :] = jnp.where(
            lane < 64, pltpu.roll(y, 64, 1), 0.0
        ).astype(BF16)
        return carry

    lax.fori_loop(0, REQ, rotate_one, 0, unroll=4)
    load_tail.wait()

    key_col = iota((1, PBLOCK), 1) + me * PBLOCK
    col128 = iota((1, 128), 1)
    upper = (iota((1, 128), 1) >= 64).astype(F32).astype(BF16)
    lower = (iota((1, 128), 1) < 64).astype(F32).astype(BF16)
    same_req = (iota((128, 128), 0) >> 5) == (iota((128, 128), 1) >> 5)

    def tails(g):
        members = [order[g * MEMBERS + i] for i in range(MEMBERS)]
        return [
            jnp.concatenate([tail_v[r] for r in members[4 * b : 4 * b + 4]], axis=0)
            for b in range(3)
        ], members

    def scores(g, buf, tops):
        kv = prompt_v[g]
        bias = jnp.where(key_col < prompt_lens[g], 0.0, LOW)
        q = q_all[pl.ds(g * MEMBERS, MEMBERS)].reshape(MEMBERS * 32, 128)
        high = None
        for h in range(4):
            cols = slice(256 * h, 256 * h + 256)
            part = dot(q, kv[cols], NT) + bias[:, cols]
            buf[:, cols] = part
            part = jnp.maximum(part[:, :128], part[:, 128:])
            high = part if high is None else jnp.maximum(high, part)
        keys, members = tails(g)
        for b in range(3):
            rows = slice(128 * b, 128 * b + 128)
            limit = jnp.zeros((1, 128), jnp.int32)
            for i in range(4):
                limit = jnp.where((col128 >> 5) == i, tail_lens[members[4 * b + i]], limit)
            seen = same_req & (((col128 & 31) + me * TBLOCK) < limit)
            part = jnp.where(seen, dot(q[rows], keys[b], NT), LOW)
            buf[rows, PBLOCK : PBLOCK + 128] = part
            top = jnp.max(jnp.maximum(high[rows], part), axis=1, keepdims=True)
            top = jnp.maximum(top, FLOOR).astype(BF16).astype(F32)
            tops[rows, :] = jnp.broadcast_to(top, (128, 128))

    def weigh(g, buf, tops):
        first = g * MEMBERS
        kv = prompt_v[g]
        vx = kv * upper + lower
        keys, members = tails(g)
        peaks = tops[...]
        w = jnp.concatenate(
            [
                jnp.exp(buf[:, 128 * h : 128 * h + 128] - peaks).astype(BF16)
                for h in range(PBLOCK // 128)
            ],
            axis=1,
        )
        w2 = jnp.exp(buf[:, PBLOCK : PBLOCK + 128] - peaks).astype(BF16)
        whole = dot(w, vx, NN)
        for b in range(3):
            rows = slice(128 * b, 128 * b + 128)
            peak = peaks[rows]
            o = whole[rows] + dot(w2[rows], keys[b] * upper + lower, NN)
            for i in range(4):
                values, stats = tiles_of(o[32 * i : 32 * i + 32], peak[32 * i : 32 * i + 32], lane)
                acc_s[first + 4 * b + i] = values
                stat_s[first + 4 * b + i] = stats

    for g in range(GROUPS):
        load_prompt(g).wait()
    scores(0, even_s, even_top)

    def two_groups(k, carry):
        g = 2 * k
        scores(g + 1, odd_s, odd_top)
        weigh(g, even_s, even_top)
        scores(jnp.minimum(g + 2, GROUPS - 1), even_s, even_top)
        weigh(g + 1, odd_s, odd_top)
        return carry

    lax.fori_loop(0, GROUPS // 2, two_groups, 0)

    rcv3[...] = jnp.zeros((N_SEQ, 16, 128), BF16)
    rcv6[...] = jnp.zeros((N_SEQ, 16, 128), BF16)
    pl.semaphore_wait(barrier, N_SEQ - 1 + N_HEAD - 1)

    def pack(dst, slot, o):
        total = jnp.zeros((16, 128), F32)
        for i in range(3):
            k = rank[3 * o + i]
            dst[slot, 16 * i : 16 * i + 16, :] = acc_s[k]
            piece = stat_s[k]
            total = total + (piece if i == 0 else pltpu.roll(piece, 8 * i, 1))
        dst[slot, 48:56, :] = (total[:8] + pltpu.roll(total[8:], 64, 1)).astype(BF16)

    def seq_copy(msg, rcv, send, recv, to):
        rows = 56 if msg is msg1 else 10
        return pltpu.make_async_remote_copy(
            src_ref=msg.at[to, pl.ds(0, rows)],
            dst_ref=rcv.at[me, pl.ds(0, rows)],
            send_sem=send.at[to],
            recv_sem=recv.at[me],
            device_id=(to, head),
            device_id_type=MESH,
        )

    def seq_arrival(msg, rcv, send, recv, source):
        rows = 56 if msg is msg1 else 10
        return pltpu.make_async_remote_copy(
            src_ref=msg.at[source, pl.ds(0, rows)],
            dst_ref=rcv.at[source, pl.ds(0, rows)],
            send_sem=send.at[source],
            recv_sem=recv.at[source],
            device_id=(source, head),
            device_id_type=MESH,
        )

    def head_copy(msg, slot, rcv, send, recv, to):
        return pltpu.make_async_remote_copy(
            src_ref=msg if slot is None else msg.at[slot],
            dst_ref=rcv.at[head],
            send_sem=send.at[to],
            recv_sem=recv.at[head],
            device_id=(me, to),
            device_id_type=MESH,
        )

    def head_arrival(msg, slot, rcv, send, recv, source):
        return pltpu.make_async_remote_copy(
            src_ref=msg if slot is None else msg.at[slot],
            dst_ref=rcv.at[source],
            send_sem=send.at[source],
            recv_sem=recv.at[source],
            device_id=(me, source),
            device_id_type=MESH,
        )

    def others(count, mine, body):
        if count == N_HEAD:
            for j in head_order:
                body(j)
        else:
            for dy, dz in SEQ_ORDER:
                body(lax.rem(me // 8 + dy, 4) * 8 + lax.rem(lax.rem(me, 8) + dz, 8))

    core = lax.rem(head, 2)
    chip = head // 2
    near = chip + 1 - 2 * lax.rem(chip, 2)
    sibling = 2 * chip + 1 - core
    far = [near, 3 - chip, lax.rem(chip + 2, 4)]
    head_order = []
    for c in (far[2], far[0], far[1]):
        head_order += [2 * c + core, 2 * c + 1 - core]
    head_order.append(sibling)

    def send_partials(o):
        pack(msg1, o, o)
        seq_copy(msg1, rcv1, send1, recv1, o).start()

    others(N_SEQ, me, send_partials)
    pack(rcv1, me, me)

    angle = jnp.zeros((16, 128), F32)
    for i in range(3):
        angle = jnp.where((row >> 2) == i, freq * place(me * 3 + i), angle)
        small_s[4 * i : 4 * i + 4, :] = fresh[i].astype(F32)
    base_c, base_s = cos_sin(angle)
    small_s[12:16, :] = jnp.zeros((4, 128), F32)
    kv_new = small_s[...]
    key_new = turned(kv_new, base_c * ct - base_s * st, base_s * ct + base_c * st, lane)
    kn = jnp.where(lane < 64, key_new, kv_new).astype(BF16)
    vn = jnp.where(lane < 64, 1.0, kv_new).astype(BF16)
    fresh_stats = jnp.zeros((16, 128), F32)
    srow = iota((32, 16), 0)
    scol = iota((32, 16), 1)
    for i in range(3):
        k = rank[3 * me + i]
        q = q_all[k]
        seen = ((scol >> 2) == i) & ((scol & 3) <= (srow & 3))
        s = jnp.where(seen, dot(q, kn, NT), LOW)
        peak = jnp.max(s, axis=1, keepdims=True).astype(BF16).astype(F32)
        w = jnp.exp(s - peak).astype(BF16)
        values, stats = tiles_of(dot(w, vn, NN), peak, lane)
        rcv1[N_SEQ, 16 * i : 16 * i + 16, :] = values
        fresh_stats = fresh_stats + (stats if i == 0 else pltpu.roll(stats, 8 * i, 1))
    folded = fresh_stats[:8] + pltpu.roll(fresh_stats[8:], 64, 1)
    rcv1[N_SEQ, 48:56, :] = folded.astype(BF16)

    sink = jnp.zeros((16, 128), F32)
    for j in range(8):
        here = ((row >> 2) == (j >> 1)) & ((lane >> 6) == (j & 1))
        sink = jnp.where(here, sinks[j], sink)

    wide_lane = iota((16, 512), 1)
    expert = wide_lane >> 4
    place = wide_lane & 15
    pick = (place >= 3).astype(jnp.int32) + (place >= 6).astype(jnp.int32)
    tile = place - 3 * pick
    own = (iota((REQ, 384), 0) == me * 3 + (iota((REQ, 384), 1) >> 7)).astype(F32).astype(BF16)
    flat_ids = jnp.concatenate([ids[t] for t in range(4)], axis=0).astype(F32).astype(BF16)
    own_ids = dot(flat_ids, own, NN).astype(BF16)
    xr = iota((64, 16), 0)
    xc = iota((64, 16), 1)
    names = jnp.full((64, 128), -1.0, F32) * ((iota((64, 128), 0) & 15) >= 12).astype(F32)
    for i in range(3):
        take = (xc == (xr & 3) * 4 + (xr >> 4)) & (((xr & 15) >> 2) == i)
        names = names + dot(
            take.astype(F32).astype(BF16), own_ids[:, 128 * i : 128 * i + 128], NN
        )
    names = jnp.concatenate([names] * 4, axis=1)
    route_s[...] = jnp.zeros((16, 128), F32)
    for i in range(3):
        route_s[4 * i : 4 * i + 4, 0:4] = routes[i]
    named = jnp.zeros((16, 512), F32)
    share = jnp.zeros((16, 512), F32)
    for k in range(4):
        hit = names[16 * k : 16 * k + 16] == expert.astype(F32)
        named = named + jnp.where(hit, 1.0, 0.0)
        share = share + jnp.where(hit, route_s[:, k : k + 1], 0.0)
    below = (iota((16, 16), 1) < iota((16, 16), 0)).astype(F32).astype(BF16)
    earlier = dot(below, named.astype(BF16), NN)
    chosen = (named > 0.5) & (earlier == pick.astype(F32)) & (place < 9)
    chosen_tile = [chosen & (tile == c) for c in range(3)]
    select = jnp.concatenate([jnp.where(m, 1.0, 0.0) for m in chosen_tile], axis=0)
    select = select.T.astype(BF16)
    give = jnp.concatenate([jnp.where(m, share, 0.0) for m in chosen_tile], axis=0)
    give_hi = give.astype(BF16)
    give_lo = (give - give_hi.astype(F32)).astype(BF16)

    trow = iota((288, 512), 0)
    tcol = iota((288, 512), 1)
    ttile = (trow >= 96).astype(jnp.int32) + (trow >= 192).astype(jnp.int32)
    trest = trow - 96 * ttile
    spread = (
        ((trest & 31) == (tcol >> 4)) & ((tcol & 15) == 3 * (trest >> 5) + ttile)
    ).astype(F32).astype(BF16)

    ucol = iota((512, 288), 1)
    urow = iota((512, 288), 0)
    utile = (ucol >= 96).astype(jnp.int32) + (ucol >= 192).astype(jnp.int32)
    urest = ucol - 96 * utile
    gather = (
        ((urest & 31) == (urow >> 4)) & ((urow & 15) == 3 * (urest >> 5) + utile)
    ).astype(F32).astype(BF16)
    resid_s[...] = jnp.zeros((16, 3072), F32)
    for i in range(3):
        resid_s[4 * i : 4 * i + 4, 0:D] = resid[i].astype(F32)

    load_ow.wait()
    ow_v[pl.ds(D, 3072 - D), :] = jnp.zeros((3072 - D, 512), BF16)
    load_gate.wait()
    load_up.wait()
    load_dn.wait()
    gu_v[FFL:CH, :] = jnp.zeros((CH - FFL, D), BF16)
    gu_v[CH + FFL : 2 * CH, :] = jnp.zeros((CH - FFL, D), BF16)
    dn_v[FFL:CH, :] = jnp.zeros((CH - FFL, D), BF16)
    dn_w[:, 2816:3072] = jnp.zeros((CH, 256), BF16)
    dn_w[:, 0:D] = dn_v[...]
    gu_w[:, 2816:3072] = jnp.zeros((2 * CH, 256), BF16)
    gu_w[:, 0:D] = gu_v[...]
    gain_s[:, 2816:3072] = jnp.zeros((1, 256), F32)
    gain_s[:, 0:D] = gain[...].reshape(1, D)

    others(N_SEQ, me, lambda s: seq_arrival(msg1, rcv1, send1, recv1, s).wait_recv())

    stat_rows = rcv1[:, 48:56, :].reshape((N_SEQ + 1) * 8, 128)
    er = iota((128, 384), 0)
    ec = iota((128, 384), 1)
    attended = []
    for i in range(3):
        for half in range(2):
            spot = 64 * half + 8 * i + 4 * ((ec & 127) >> 6) + (ec >> 7)
            expand = (er == spot).astype(F32).astype(BF16)
            wide = dot(stat_rows, expand, NN)
            peaks = wide[:, 0:128].reshape(N_SEQ + 1, 8, 128)
            totals = (wide[:, 128:256] + wide[:, 256:384]).reshape(N_SEQ + 1, 8, 128)
            sunk = sink[8 * half : 8 * half + 8]
            top = jnp.maximum(jnp.max(peaks, axis=0), sunk)
            factor = jnp.exp(peaks - top[None])
            start = 16 * i + 8 * half
            values = rcv1[:, start : start + 8, :].astype(F32)
            num = jnp.sum(values * factor, axis=0)
            den = jnp.sum(totals * factor, axis=0) + jnp.exp(sunk - top)
            attended.append(num / den)
    att = jnp.concatenate(attended, axis=0).astype(BF16)
    rr = iota((64, 48), 0)
    rc = iota((64, 48), 1)
    want = ((rr & 15) >> 2) * 16 + (rr >> 4) * 4 + (rr & 3)
    regroup = (rc == want).astype(F32).astype(BF16)
    mixed = dot(regroup, att, NN).astype(BF16)
    flat = jnp.concatenate([mixed[16 * p : 16 * p + 16] for p in range(4)], axis=1)

    def project(j):
        rows = ow_v[pl.ds(pl.multiple_of(j * CH, CH), CH), :]
        return dot(flat, rows, NT).astype(BF16)

    def send_projection(j):
        msg2[j] = project(j)
        head_copy(msg2, j, rcv2, send2, recv2, j).start()

    others(N_HEAD, head, send_projection)
    rcv2[head] = project(head)
    others(N_HEAD, head, lambda s: head_arrival(msg2, s, rcv2, send2, recv2, s).wait_recv())
    total = resid_s[:, pl.ds(pl.multiple_of(head * CH, CH), CH)]
    total = total + jnp.sum(rcv2[...].astype(F32), axis=0)
    hidden = total.astype(BF16)
    hidden_rows = jnp.concatenate([hidden[:, 128 * c : 128 * c + 128] for c in range(3)], axis=0)

    msg3[...] = dot(select, hidden_rows, NN).astype(BF16).reshape(N_SEQ, 16, 128)
    others(N_SEQ, me, lambda o: seq_copy(msg3, rcv3, send3, recv3, o).start())
    rcv3[me] = msg3[me]
    others(N_SEQ, me, lambda s: seq_arrival(msg3, rcv3, send3, recv3, s).wait_recv())
    got = dot(spread, rcv3[...].reshape(512, 128), NN).astype(BF16)
    mine = jnp.concatenate([got[96 * c : 96 * c + 96] for c in range(3)], axis=1)
    msg4[...] = mine
    gather_to = [2 * far[2] + core, 2 * far[0] + core, 2 * far[1] + core, sibling]
    for j in gather_to:
        head_copy(msg4, None, rcv4, send4, recv4, j).start()
    rcv4[head] = mine

    both_s[...] = jnp.zeros((ROWS, 2 * CH), F32)
    square_s[...] = jnp.zeros((ROWS, 128), F32)

    def use_chunk(j):
        cols = pl.ds(pl.multiple_of(j * CH, CH), CH)
        x = rcv4[j].astype(F32)
        square_s[...] += jnp.broadcast_to(jnp.sum(x * x, axis=1, keepdims=True), (ROWS, 128))
        both_s[...] += dot((x * gain_s[:, cols]).astype(BF16), gu_w[:, cols], NT)

    def forward(k, j):
        return pltpu.make_async_remote_copy(
            src_ref=rcv4.at[j],
            dst_ref=rcv4.at[j],
            send_sem=send_f.at[k],
            recv_sem=recv4.at[j],
            device_id=(me, sibling),
            device_id_type=MESH,
        )

    use_chunk(head)
    head_arrival(msg4, None, rcv4, send4, recv4, sibling).wait_recv()
    use_chunk(sibling)
    for k in range(3):
        j = 2 * far[k] + core
        head_arrival(msg4, None, rcv4, send4, recv4, j).wait_recv()
        forward(k, j).start()
        use_chunk(j)
    for k in range(3):
        j = 2 * far[k] + 1 - core
        forward(k, j).wait_recv()
        use_chunk(j)
    both = both_s[...]
    square = square_s[:, 0:1]
    scale = lax.rsqrt(square * (1.0 / D) + 1e-05)
    g = jnp.minimum(both[:, 0:CH] * scale, 7.0)
    u = jnp.clip(both[:, CH : 2 * CH] * scale, -7.0, 7.0)
    active = ((u + 1.0) * g * jax.nn.sigmoid(1.702 * g)).astype(BF16)

    def product(j):
        return dot(active, dn_w[:, pl.ds(pl.multiple_of(j * CH, CH), CH)], NN)

    def pair_copy(c):
        return pltpu.make_async_remote_copy(
            src_ref=msg_p.at[c],
            dst_ref=rcv_p.at[c],
            send_sem=send_p.at[c],
            recv_sem=recv_p.at[c],
            device_id=(me, sibling),
            device_id_type=MESH,
        )

    def chip_copy(c, slot):
        return pltpu.make_async_remote_copy(
            src_ref=msg5.at[c],
            dst_ref=rcv5.at[slot],
            send_sem=send5.at[c],
            recv_sem=recv5.at[slot],
            device_id=(me, 2 * c + core),
            device_id_type=MESH,
        )

    turns = [far[2], far[0], far[1], chip]
    for c in turns:
        msg_p[c] = product(2 * c + 1 - core).astype(BF16)
        pair_copy(c).start()
    for k, c in enumerate(turns):
        own = product(2 * c + core)
        pair_copy(c).wait_recv()
        both_cores = (own + rcv_p[c].astype(F32)).astype(BF16)
        if k < 3:
            msg5[c] = both_cores
            chip_copy(c, chip).start()
        else:
            rcv5[chip] = both_cores
    for c in far:
        chip_copy(c, c).wait_recv()
    summed = jnp.sum(rcv5[...].astype(F32), axis=0).astype(BF16)
    summed_rows = jnp.concatenate([summed[:, 128 * c : 128 * c + 128] for c in range(3)], axis=0)
    msg6[...] = dot(gather, summed_rows, NN).astype(BF16).reshape(N_SEQ, 16, 128)
    others(N_SEQ, me, lambda o: seq_copy(msg6, rcv6, send6, recv6, o).start())
    rcv6[me] = msg6[me]
    others(N_SEQ, me, lambda s: seq_arrival(msg6, rcv6, send6, recv6, s).wait_recv())
    back = rcv6[...].reshape(512, 128)
    added = dot(give_hi, back, NN) + dot(give_lo, back, NN)
    result = hidden_rows.astype(F32) + added
    result = jnp.concatenate([result[16 * c : 16 * c + 16] for c in range(3)], axis=1).astype(BF16)
    msg7[...] = result
    others(N_HEAD, head, lambda o: head_copy(msg7, None, rcv7, send7, recv7, o).start())
    rcv7[head] = result
    others(N_HEAD, head, lambda s: head_arrival(msg7, None, rcv7, send7, recv7, s).wait_recv())
    for i in range(3):
        for j in range(N_HEAD):
            out_ref[i, :, j * CH : j * CH + CH] = rcv7[j, 4 * i : 4 * i + 4, :]

    for msg, rcv, send, recv in (
        (msg1, rcv1, send1, recv1),
        (msg3, rcv3, send3, recv3),
        (msg6, rcv6, send6, recv6),
    ):
        others(N_SEQ, me, lambda o: seq_copy(msg, rcv, send, recv, o).wait_send())
    for j in gather_to:
        head_copy(msg4, None, rcv4, send4, recv4, j).wait_send()
    for k in range(3):
        forward(k, 2 * far[k] + core).wait_send()
    for k, c in enumerate(turns):
        pair_copy(c).wait_send()
        if k < 3:
            chip_copy(c, chip).wait_send()
    others(N_HEAD, head, lambda o: head_copy(msg2, o, rcv2, send2, recv2, o).wait_send())
    others(N_HEAD, head, lambda o: head_copy(msg7, None, rcv7, send7, recv7, o).wait_send())


def on_device(
    new_query,
    fresh_key_value,
    prompt_cache,
    decoded_tail_cache,
    sinks,
    prompt_group,
    prompt_lens,
    tail_lens,
    o_weight,
    resid,
    norm_gain,
    expert_ids,
    route_weights,
    gate_up,
    down_weight,
):
    r = jnp.arange(REQ, dtype=jnp.int32)
    mine, other = prompt_group[:, None], prompt_group[None, :]
    ahead = (other < mine) | ((other == mine) & (r[None, :] < r[:, None]))
    rank = jnp.sum(ahead.astype(jnp.int32), axis=1)
    order = jnp.sum(jnp.where(rank[None, :] == r[:, None], r[None, :], 0), axis=1)
    freq = np.exp(np.arange(32) * (-2.0 * math.log(150000.0) / 64))
    freq = np.tile(freq.astype(np.float32), 4)
    step_angle = (np.arange(16) % 4)[:, None] * freq[None, :].astype(np.float64)
    tables = np.zeros((40, 128), np.float32)
    tables[0] = freq
    tables[8:24] = np.cos(step_angle)
    tables[24:40] = np.sin(step_angle)
    fresh = fresh_key_value.transpose(0, 2, 1, 3).reshape(3, 4, 128)
    ids = expert_ids.transpose(1, 2, 0)
    q = new_query.reshape(REQ, 4, 4, 128).transpose(0, 2, 1, 3).reshape(REQ, 16, 128)
    prompt = prompt_cache.transpose(0, 2, 1, 3).reshape(GROUPS, PBLOCK, 128)
    tail = decoded_tail_cache.transpose(0, 2, 1, 3).reshape(REQ, TBLOCK, 128)
    ow = o_weight.T
    gu = gate_up.transpose(0, 2, 3, 1).reshape(2, FFL, D)
    dn = down_weight.reshape(FFL, D)

    smem = pl.BlockSpec(memory_space=pltpu.SMEM)
    vmem = pl.BlockSpec(memory_space=pltpu.VMEM)
    hbm = pl.BlockSpec(memory_space=pl.ANY)
    seq_sem = pltpu.SemaphoreType.DMA((N_SEQ,))
    head_sem = pltpu.SemaphoreType.DMA((N_HEAD,))
    chip_sem = pltpu.SemaphoreType.DMA((4,))
    out = pl.pallas_call(
        layer_kernel,
        name="layer",
        out_shape=jax.ShapeDtypeStruct((3, 4, 3072), BF16),
        in_specs=[smem] * 6 + [vmem] * 6 + [hbm] * 6,
        out_specs=vmem,
        scratch_shapes=[
            pltpu.VMEM((REQ, 16, 128), BF16),
            pltpu.VMEM((GROUPS, PBLOCK, 128), BF16),
            pltpu.VMEM((REQ, TBLOCK, 128), BF16),
            pltpu.VMEM((3072, 512), BF16),
            pltpu.VMEM((2 * CH, D), BF16),
            pltpu.VMEM((CH, D), BF16),
            pltpu.VMEM((CH, 3072), BF16),
            pltpu.VMEM((2 * CH, 3072), BF16),
            pltpu.VMEM((1, 3072), F32),
            pltpu.VMEM((REQ, 128), F32),
            pltpu.VMEM((REQ, 128), F32),
            pltpu.VMEM((16, 128), F32),
            pltpu.VMEM((16, 128), F32),
            pltpu.VMEM((16, 3072), F32),
            pltpu.VMEM((ROWS, 2 * CH), F32),
            pltpu.VMEM((ROWS, 128), F32),
            pltpu.VMEM((REQ, 32, 128), BF16),
            pltpu.VMEM((MEMBERS * 32, PBLOCK + 128), F32),
            pltpu.VMEM((MEMBERS * 32, PBLOCK + 128), F32),
            pltpu.VMEM((MEMBERS * 32, 128), F32),
            pltpu.VMEM((MEMBERS * 32, 128), F32),
            pltpu.VMEM((REQ, 16, 128), BF16),
            pltpu.VMEM((REQ, 16, 128), F32),
            pltpu.VMEM((N_SEQ, 56, 128), BF16),
            pltpu.VMEM((N_SEQ + 1, 56, 128), BF16),
            pltpu.VMEM((N_HEAD, 16, CH), BF16),
            pltpu.VMEM((N_HEAD, 16, CH), BF16),
            pltpu.VMEM((N_SEQ, 16, 128), BF16),
            pltpu.VMEM((N_SEQ, 16, 128), BF16),
            pltpu.VMEM((ROWS, CH), BF16),
            pltpu.VMEM((N_HEAD, ROWS, CH), BF16),
            pltpu.VMEM((4, ROWS, CH), BF16),
            pltpu.VMEM((4, ROWS, CH), BF16),
            pltpu.VMEM((4, ROWS, CH), BF16),
            pltpu.VMEM((4, ROWS, CH), BF16),
            pltpu.VMEM((N_SEQ, 16, 128), BF16),
            pltpu.VMEM((N_SEQ, 16, 128), BF16),
            pltpu.VMEM((16, CH), BF16),
            pltpu.VMEM((N_HEAD, 16, CH), BF16),
            pltpu.SemaphoreType.DMA((6,)),
            pltpu.SemaphoreType.DMA((GROUPS,)),
            seq_sem,
            seq_sem,
            head_sem,
            head_sem,
            seq_sem,
            seq_sem,
            head_sem,
            head_sem,
            chip_sem,
            chip_sem,
            chip_sem,
            chip_sem,
            chip_sem,
            seq_sem,
            seq_sem,
            head_sem,
            head_sem,
        ],
        compiler_params=pltpu.CompilerParams(
            collective_id=0, has_side_effects=True, vmem_limit_bytes=56 * 1024 * 1024
        ),
    )(
        order,
        rank,
        prompt_group,
        tail_lens,
        prompt_lens,
        sinks,
        jnp.asarray(tables),
        fresh,
        ids,
        route_weights,
        resid,
        norm_gain,
        q,
        prompt,
        tail,
        ow,
        gu,
        dn,
    )
    return out[:, :, :D]


def solution(mesh):
    return jax.shard_map(
        on_device,
        mesh=mesh,
        in_specs=(
            P(None, None, "head"),
            P("seq", None, "head", None),
            P(None, "seq", "head", None),
            P(None, "seq", "head", None),
            P("head"),
            P(),
            P(),
            P(),
            P("head", None),
            P("seq", None, None),
            P(),
            P(),
            P("seq", None, None),
            P("seq", None, None, "head"),
            P("seq", "head", None),
        ),
        out_specs=P("seq", None, None),
        check_vma=False,
    )
```

```python
import math

import jax
import jax.numpy as jnp
import numpy as np
from jax import lax
from jax.experimental import pallas as pl
from jax.experimental.pallas import tpu as pltpu
from jax.sharding import PartitionSpec as P

MESH = pl.DeviceIdType.MESH
LOW = -1e30
FLOOR = -1e29
F32 = jnp.float32
BF16 = jnp.bfloat16

N_SEQ = 32
N_HEAD = 8
REQ = 96
GROUPS = 8
MEMBERS = 12
PBLOCK = 1024
TBLOCK = 32
D = 2880
CH = 384
LASTC = 192
FFL = 360
ROWS = 96
HALF_PI = (1.5703125, 4.8351287841796875e-4, 3.1391647865048e-7)
NT = (((1,), (1,)), ((), ()))
NN = (((1,), (0,)), ((), ()))
TN = (((0,), (0,)), ((), ()))


SEQ_ORDER = sorted(
    ((dy, dz) for dy in range(4) for dz in range(8) if dy or dz),
    key=lambda o: (-min(o[0], 4 - o[0]) - min(o[1], 8 - o[1]), (o[0] * 3 + o[1] * 5) % 8),
)


def dot(a, b, dims):
    return lax.dot_general(a, b, dims, preferred_element_type=F32)


def iota(shape, axis):
    return lax.broadcasted_iota(jnp.int32, shape, axis)


def turned(x, cosine, sine, lane):
    ahead = pltpu.roll(x, 96, 1)
    behind = pltpu.roll(x, 32, 1)
    partner = jnp.where((lane & 63) < 32, -ahead, behind)
    return x * cosine + partner * sine


def cos_sin(angle):
    k = jnp.floor(angle * (2.0 / math.pi) + 0.5)
    r = angle - k * HALF_PI[0]
    r = r - k * HALF_PI[1]
    r = r - k * HALF_PI[2]
    r2 = r * r
    s = r + r * r2 * (-1.0 / 6 + r2 * (1.0 / 120 + r2 * (-1.0 / 5040 + r2 * (1.0 / 362880))))
    c = 1.0 + r2 * (-0.5 + r2 * (1.0 / 24 + r2 * (-1.0 / 720 + r2 * (1.0 / 40320))))
    quarter = k - 4.0 * jnp.floor(k * 0.25)
    odd = (quarter == 1.0) | (quarter == 3.0)
    cosine = jnp.where(odd, s, c)
    sine = jnp.where(odd, c, s)
    cosine = jnp.where((quarter == 1.0) | (quarter == 2.0), -cosine, cosine)
    sine = jnp.where(quarter >= 2.0, -sine, sine)
    return cosine, sine


def tiles_of(out, peak, lane):
    first, second = out[:16], out[16:]
    values = jnp.where(lane < 64, pltpu.roll(first, 64, 1), second).astype(BF16)
    hi0 = first.astype(BF16).astype(F32)
    hi1 = second.astype(BF16).astype(F32)
    lo0 = first - hi0
    lo1 = second - hi1
    stats = jnp.where(
        lane < 4,
        jnp.where(lane == 0, peak[:16], jnp.where(lane == 1, hi0, jnp.where(lane == 2, lo0, 0.0))),
        jnp.where(
            lane == 4, peak[16:], jnp.where(lane == 5, hi1, jnp.where(lane == 6, lo1, 0.0))
        ),
    )
    return values, jnp.where(lane < 8, stats, 0.0)


def layer_kernel(
    order,
    rank,
    prompt_group,
    tail_lens,
    prompt_lens,
    sinks,
    tables,
    fresh,
    ids,
    routes,
    resid,
    gain,
    q_hbm,
    prompt_hbm,
    tail_hbm,
    ow_hbm,
    gu_hbm,
    dn_hbm,
    out_ref,
    q_v,
    prompt_v,
    tail_v,
    ow_v,
    gu_v,
    dn_v,
    dn_w,
    gu_w,
    gain_s,
    cos_s,
    sin_s,
    small_s,
    route_s,
    resid_s,
    both_s,
    square_s,
    q_all,
    even_s,
    odd_s,
    even_top,
    odd_top,
    acc_s,
    stat_s,
    msg1,
    rcv1,
    msg2,
    rcv2,
    msg3,
    rcv3,
    msg4,
    rcv4,
    msg_p,
    rcv_p,
    msg5,
    rcv5,
    msg6,
    rcv6,
    msg7,
    rcv7,
    load_sem,
    prompt_sem,
    send1,
    recv1,
    send2,
    recv2,
    send3,
    recv3,
    send4,
    recv4,
    send_f,
    send_p,
    recv_p,
    send5,
    recv5,
    send6,
    recv6,
    send7,
    recv7,
):
    me = lax.axis_index("seq")
    head = lax.axis_index("head")
    barrier = pltpu.get_barrier_semaphore()

    def greet_seq(d, carry):
        pl.semaphore_signal(
            barrier, inc=1, device_id=(lax.rem(me + d, N_SEQ), head), device_id_type=MESH
        )
        return carry

    def greet_head(d, carry):
        pl.semaphore_signal(
            barrier, inc=1, device_id=(me, lax.rem(head + d, N_HEAD)), device_id_type=MESH
        )
        return carry

    load_q = pltpu.make_async_copy(q_hbm, q_v, load_sem.at[0])
    load_tail = pltpu.make_async_copy(tail_hbm, tail_v, load_sem.at[1])
    load_ow = pltpu.make_async_copy(ow_hbm, ow_v.at[pl.ds(0, D)], load_sem.at[2])
    load_gate = pltpu.make_async_copy(gu_hbm.at[0], gu_v.at[pl.ds(0, FFL)], load_sem.at[3])
    load_up = pltpu.make_async_copy(gu_hbm.at[1], gu_v.at[pl.ds(CH, FFL)], load_sem.at[5])
    load_dn = pltpu.make_async_copy(dn_hbm, dn_v.at[pl.ds(0, FFL)], load_sem.at[4])
    load_q.start()
    load_tail.start()

    def load_prompt(g):
        return pltpu.make_async_copy(prompt_hbm.at[g], prompt_v.at[g], prompt_sem.at[g])

    for g in range(GROUPS):
        load_prompt(g).start()
    load_ow.start()
    load_gate.start()
    load_up.start()
    load_dn.start()
    for d in range(1, N_SEQ):
        greet_seq(d, 0)
    for d in range(1, N_HEAD):
        greet_head(d, 0)

    lane = iota((16, 128), 1)
    row = iota((16, 128), 0)

    freq = tables[0:1, :]
    ct = tables[8:24, :]
    st = tables[24:40, :]

    def place(r):
        return (prompt_lens[prompt_group[r]] + tail_lens[r]).astype(F32)

    def put_angle(i, carry):
        cos_s[pl.ds(i, 1), :] = freq * place(order[i])
        return carry

    lax.fori_loop(0, REQ, put_angle, 0, unroll=8)
    cosine, sine = cos_sin(cos_s[...])
    cos_s[...] = cosine
    sin_s[...] = sine

    load_q.wait()

    def rotate_one(i, carry):
        r = order[i]
        x = q_v[r].astype(F32)
        c0 = cos_s[pl.ds(i, 1), :]
        s0 = sin_s[pl.ds(i, 1), :]
        y = turned(x, c0 * ct - s0 * st, s0 * ct + c0 * st, lane)
        y = y.astype(BF16).astype(F32) * 0.125
        q_all[i, 0:16, :] = jnp.where(lane < 64, y, 0.0).astype(BF16)
        q_all[i, 16:32, :] = jnp.where(
            lane < 64, pltpu.roll(y, 64, 1), 0.0
        ).astype(BF16)
        return carry

    lax.fori_loop(0, REQ, rotate_one, 0, unroll=4)
    load_tail.wait()

    key_col = iota((1, PBLOCK), 1) + me * PBLOCK
    col128 = iota((1, 128), 1)
    upper = (iota((1, 128), 1) >= 64).astype(F32).astype(BF16)
    lower = (iota((1, 128), 1) < 64).astype(F32).astype(BF16)
    same_req = (iota((128, 128), 0) >> 5) == (iota((128, 128), 1) >> 5)

    def tails(g):
        members = [order[g * MEMBERS + i] for i in range(MEMBERS)]
        return [
            jnp.concatenate([tail_v[r] for r in members[4 * b : 4 * b + 4]], axis=0)
            for b in range(3)
        ], members

    def scores(g, buf, tops):
        kv = prompt_v[g]
        bias = jnp.where(key_col < prompt_lens[g], 0.0, LOW)
        q = q_all[pl.ds(g * MEMBERS, MEMBERS)].reshape(MEMBERS * 32, 128)
        keys, members = tails(g)
        for b in range(3):
            rows = slice(128 * b, 128 * b + 128)
            high = None
            for h in range(4):
                cols = slice(256 * h, 256 * h + 256)
                part = dot(q[rows], kv[cols], NT) + bias[:, cols]
                buf[rows, cols] = part
                part = jnp.maximum(part[:, :128], part[:, 128:])
                high = part if high is None else jnp.maximum(high, part)
            limit = jnp.zeros((1, 128), jnp.int32)
            for i in range(4):
                limit = jnp.where((col128 >> 5) == i, tail_lens[members[4 * b + i]], limit)
            seen = same_req & (((col128 & 31) + me * TBLOCK) < limit)
            part = jnp.where(seen, dot(q[rows], keys[b], NT), LOW)
            buf[rows, PBLOCK : PBLOCK + 128] = part
            top = jnp.max(jnp.maximum(high, part), axis=1, keepdims=True)
            top = jnp.maximum(top, FLOOR).astype(BF16).astype(F32)
            tops[rows, :] = jnp.broadcast_to(top, (128, 128))

    def weigh(g, buf, tops):
        first = g * MEMBERS
        kv = prompt_v[g]
        vx = kv * upper + lower
        keys, members = tails(g)
        peaks = tops[...]
        w = jnp.concatenate(
            [
                jnp.exp(buf[:, 128 * h : 128 * h + 128] - peaks).astype(BF16)
                for h in range(PBLOCK // 128)
            ],
            axis=1,
        )
        w2 = jnp.exp(buf[:, PBLOCK : PBLOCK + 128] - peaks).astype(BF16)
        whole = dot(w, vx, NN)
        for b in range(3):
            rows = slice(128 * b, 128 * b + 128)
            peak = peaks[rows]
            o = whole[rows] + dot(w2[rows], keys[b] * upper + lower, NN)
            for i in range(4):
                values, stats = tiles_of(o[32 * i : 32 * i + 32], peak[32 * i : 32 * i + 32], lane)
                acc_s[first + 4 * b + i] = values
                stat_s[first + 4 * b + i] = stats

    for g in range(GROUPS):
        load_prompt(g).wait()
    scores(0, even_s, even_top)

    def two_groups(k, carry):
        g = 2 * k
        scores(g + 1, odd_s, odd_top)
        weigh(g, even_s, even_top)
        scores(jnp.minimum(g + 2, GROUPS - 1), even_s, even_top)
        weigh(g + 1, odd_s, odd_top)
        return carry

    lax.fori_loop(0, GROUPS // 2, two_groups, 0)

    rcv3[...] = jnp.zeros((N_SEQ, 16, 128), BF16)
    rcv6[...] = jnp.zeros((N_SEQ, 16, 128), BF16)
    pl.semaphore_wait(barrier, N_SEQ - 1 + N_HEAD - 1)

    def pack(dst, slot, o):
        total = jnp.zeros((16, 128), F32)
        for i in range(3):
            k = rank[3 * o + i]
            dst[slot, 16 * i : 16 * i + 16, :] = acc_s[k]
            piece = stat_s[k]
            total = total + (piece if i == 0 else pltpu.roll(piece, 8 * i, 1))
        dst[slot, 48:56, :] = (total[:8] + pltpu.roll(total[8:], 64, 1)).astype(BF16)

    def seq_copy(msg, rcv, send, recv, to):
        rows = 56 if msg is msg1 else 10
        return pltpu.make_async_remote_copy(
            src_ref=msg.at[to, pl.ds(0, rows)],
            dst_ref=rcv.at[me, pl.ds(0, rows)],
            send_sem=send.at[to],
            recv_sem=recv.at[me],
            device_id=(to, head),
            device_id_type=MESH,
        )

    def seq_arrival(msg, rcv, send, recv, source):
        rows = 56 if msg is msg1 else 10
        return pltpu.make_async_remote_copy(
            src_ref=msg.at[source, pl.ds(0, rows)],
            dst_ref=rcv.at[source, pl.ds(0, rows)],
            send_sem=send.at[source],
            recv_sem=recv.at[source],
            device_id=(source, head),
            device_id_type=MESH,
        )

    def head_copy(msg, slot, rcv, send, recv, to):
        return pltpu.make_async_remote_copy(
            src_ref=msg if slot is None else msg.at[slot],
            dst_ref=rcv.at[head],
            send_sem=send.at[to],
            recv_sem=recv.at[head],
            device_id=(me, to),
            device_id_type=MESH,
        )

    def head_arrival(msg, slot, rcv, send, recv, source):
        return pltpu.make_async_remote_copy(
            src_ref=msg if slot is None else msg.at[slot],
            dst_ref=rcv.at[source],
            send_sem=send.at[source],
            recv_sem=recv.at[source],
            device_id=(me, source),
            device_id_type=MESH,
        )

    def others(count, mine, body):
        if count == N_HEAD:
            for j in head_order:
                body(j)
        else:
            for dy, dz in SEQ_ORDER:
                body(lax.rem(me // 8 + dy, 4) * 8 + lax.rem(lax.rem(me, 8) + dz, 8))

    core = lax.rem(head, 2)
    chip = head // 2
    near = chip + 1 - 2 * lax.rem(chip, 2)
    sibling = 2 * chip + 1 - core
    far = [near, 3 - chip, lax.rem(chip + 2, 4)]
    head_order = []
    for c in (far[2], far[0], far[1]):
        head_order += [2 * c + core, 2 * c + 1 - core]
    head_order.append(sibling)

    def send_partials(o):
        pack(msg1, o, o)
        seq_copy(msg1, rcv1, send1, recv1, o).start()

    others(N_SEQ, me, send_partials)
    pack(rcv1, me, me)

    angle = jnp.zeros((16, 128), F32)
    for i in range(3):
        angle = jnp.where((row >> 2) == i, freq * place(me * 3 + i), angle)
        small_s[4 * i : 4 * i + 4, :] = fresh[i].astype(F32)
    base_c, base_s = cos_sin(angle)
    small_s[12:16, :] = jnp.zeros((4, 128), F32)
    kv_new = small_s[...]
    key_new = turned(kv_new, base_c * ct - base_s * st, base_s * ct + base_c * st, lane)
    kn = jnp.where(lane < 64, key_new, kv_new).astype(BF16)
    vn = jnp.where(lane < 64, 1.0, kv_new).astype(BF16)
    fresh_stats = jnp.zeros((16, 128), F32)
    srow = iota((32, 16), 0)
    scol = iota((32, 16), 1)
    for i in range(3):
        k = rank[3 * me + i]
        q = q_all[k]
        seen = ((scol >> 2) == i) & ((scol & 3) <= (srow & 3))
        s = jnp.where(seen, dot(q, kn, NT), LOW)
        peak = jnp.max(s, axis=1, keepdims=True).astype(BF16).astype(F32)
        w = jnp.exp(s - peak).astype(BF16)
        values, stats = tiles_of(dot(w, vn, NN), peak, lane)
        rcv1[N_SEQ, 16 * i : 16 * i + 16, :] = values
        fresh_stats = fresh_stats + (stats if i == 0 else pltpu.roll(stats, 8 * i, 1))
    folded = fresh_stats[:8] + pltpu.roll(fresh_stats[8:], 64, 1)
    rcv1[N_SEQ, 48:56, :] = folded.astype(BF16)

    sink = jnp.zeros((16, 128), F32)
    for j in range(8):
        here = ((row >> 2) == (j >> 1)) & ((lane >> 6) == (j & 1))
        sink = jnp.where(here, sinks[j], sink)

    wide_lane = iota((16, 512), 1)
    expert = wide_lane >> 4
    place = wide_lane & 15
    pick = (place >= 3).astype(jnp.int32) + (place >= 6).astype(jnp.int32)
    tile = place - 3 * pick
    own = (iota((REQ, 384), 0) == me * 3 + (iota((REQ, 384), 1) >> 7)).astype(F32).astype(BF16)
    flat_ids = jnp.concatenate([ids[t] for t in range(4)], axis=0).astype(F32).astype(BF16)
    own_ids = dot(flat_ids, own, NN).astype(BF16)
    xr = iota((64, 16), 0)
    xc = iota((64, 16), 1)
    names = jnp.full((64, 128), -1.0, F32) * ((iota((64, 128), 0) & 15) >= 12).astype(F32)
    for i in range(3):
        take = (xc == (xr & 3) * 4 + (xr >> 4)) & (((xr & 15) >> 2) == i)
        names = names + dot(
            take.astype(F32).astype(BF16), own_ids[:, 128 * i : 128 * i + 128], NN
        )
    names = jnp.concatenate([names] * 4, axis=1)
    route_s[...] = jnp.zeros((16, 128), F32)
    for i in range(3):
        route_s[4 * i : 4 * i + 4, 0:4] = routes[i]
    named = jnp.zeros((16, 512), F32)
    share = jnp.zeros((16, 512), F32)
    for k in range(4):
        hit = names[16 * k : 16 * k + 16] == expert.astype(F32)
        named = named + jnp.where(hit, 1.0, 0.0)
        share = share + jnp.where(hit, route_s[:, k : k + 1], 0.0)
    below = (iota((16, 16), 1) < iota((16, 16), 0)).astype(F32).astype(BF16)
    earlier = dot(below, named.astype(BF16), NN)
    chosen = (named > 0.5) & (earlier == pick.astype(F32)) & (place < 9)
    chosen_tile = [chosen & (tile == c) for c in range(3)]
    select = jnp.concatenate([jnp.where(m, 1.0, 0.0) for m in chosen_tile], axis=0)
    select = select.T.astype(BF16)
    give = jnp.concatenate([jnp.where(m, share, 0.0) for m in chosen_tile], axis=0)
    give_hi = give.astype(BF16)
    give_lo = (give - give_hi.astype(F32)).astype(BF16)

    trow = iota((288, 512), 0)
    tcol = iota((288, 512), 1)
    ttile = (trow >= 96).astype(jnp.int32) + (trow >= 192).astype(jnp.int32)
    trest = trow - 96 * ttile
    spread = (
        ((trest & 31) == (tcol >> 4)) & ((tcol & 15) == 3 * (trest >> 5) + ttile)
    ).astype(F32).astype(BF16)

    ucol = iota((512, 288), 1)
    urow = iota((512, 288), 0)
    utile = (ucol >= 96).astype(jnp.int32) + (ucol >= 192).astype(jnp.int32)
    urest = ucol - 96 * utile
    gather = (
        ((urest & 31) == (urow >> 4)) & ((urow & 15) == 3 * (urest >> 5) + utile)
    ).astype(F32).astype(BF16)
    resid_s[...] = jnp.zeros((16, 3072), F32)
    for i in range(3):
        resid_s[4 * i : 4 * i + 4, 0:D] = resid[i].astype(F32)

    load_ow.wait()
    ow_v[pl.ds(D, 3072 - D), :] = jnp.zeros((3072 - D, 512), BF16)
    load_gate.wait()
    load_up.wait()
    load_dn.wait()
    gu_v[FFL:CH, :] = jnp.zeros((CH - FFL, D), BF16)
    gu_v[CH + FFL : 2 * CH, :] = jnp.zeros((CH - FFL, D), BF16)
    dn_v[FFL:CH, :] = jnp.zeros((CH - FFL, D), BF16)
    dn_w[:, 2816:3072] = jnp.zeros((CH, 256), BF16)
    dn_w[:, 0:D] = dn_v[...]
    gu_w[:, 2816:3072] = jnp.zeros((2 * CH, 256), BF16)
    gu_w[:, 0:D] = gu_v[...]
    gain_s[:, 2816:3072] = jnp.zeros((1, 256), F32)
    gain_s[:, 0:D] = gain[...].reshape(1, D)

    others(N_SEQ, me, lambda s: seq_arrival(msg1, rcv1, send1, recv1, s).wait_recv())

    stat_rows = rcv1[:, 48:56, :].reshape((N_SEQ + 1) * 8, 128)
    er = iota((128, 384), 0)
    ec = iota((128, 384), 1)
    attended = []
    for i in range(3):
        for half in range(2):
            spot = 64 * half + 8 * i + 4 * ((ec & 127) >> 6) + (ec >> 7)
            expand = (er == spot).astype(F32).astype(BF16)
            wide = dot(stat_rows, expand, NN)
            peaks = wide[:, 0:128].reshape(N_SEQ + 1, 8, 128)
            totals = (wide[:, 128:256] + wide[:, 256:384]).reshape(N_SEQ + 1, 8, 128)
            sunk = sink[8 * half : 8 * half + 8]
            top = jnp.maximum(jnp.max(peaks, axis=0), sunk)
            factor = jnp.exp(peaks - top[None])
            start = 16 * i + 8 * half
            values = rcv1[:, start : start + 8, :].astype(F32)
            num = jnp.sum(values * factor, axis=0)
            den = jnp.sum(totals * factor, axis=0) + jnp.exp(sunk - top)
            attended.append(num / den)
    att = jnp.concatenate(attended, axis=0).astype(BF16)
    rr = iota((64, 48), 0)
    rc = iota((64, 48), 1)
    want = ((rr & 15) >> 2) * 16 + (rr >> 4) * 4 + (rr & 3)
    regroup = (rc == want).astype(F32).astype(BF16)
    mixed = dot(regroup, att, NN).astype(BF16)
    flat = jnp.concatenate([mixed[16 * p : 16 * p + 16] for p in range(4)], axis=1)

    def project(j):
        rows = ow_v[pl.ds(pl.multiple_of(j * CH, CH), CH), :]
        return dot(flat, rows, NT).astype(BF16)

    def send_projection(j):
        msg2[j] = project(j)
        head_copy(msg2, j, rcv2, send2, recv2, j).start()

    others(N_HEAD, head, send_projection)
    rcv2[head] = project(head)
    others(N_HEAD, head, lambda s: head_arrival(msg2, s, rcv2, send2, recv2, s).wait_recv())
    total = resid_s[:, pl.ds(pl.multiple_of(head * CH, CH), CH)]
    total = total + jnp.sum(rcv2[...].astype(F32), axis=0)
    hidden = total.astype(BF16)
    hidden_rows = jnp.concatenate([hidden[:, 128 * c : 128 * c + 128] for c in range(3)], axis=0)

    msg3[...] = dot(select, hidden_rows, NN).astype(BF16).reshape(N_SEQ, 16, 128)
    others(N_SEQ, me, lambda o: seq_copy(msg3, rcv3, send3, recv3, o).start())
    rcv3[me] = msg3[me]
    others(N_SEQ, me, lambda o: seq_copy(msg1, rcv1, send1, recv1, o).wait_send())
    others(N_HEAD, head, lambda o: head_copy(msg2, o, rcv2, send2, recv2, o).wait_send())
    others(N_SEQ, me, lambda s: seq_arrival(msg3, rcv3, send3, recv3, s).wait_recv())
    got = dot(spread, rcv3[...].reshape(512, 128), NN).astype(BF16)
    mine = jnp.concatenate([got[96 * c : 96 * c + 96] for c in range(3)], axis=1)
    msg4[...] = mine
    gather_to = [2 * far[2] + core, 2 * far[0] + core, 2 * far[1] + core, sibling]
    for j in gather_to:
        head_copy(msg4, None, rcv4, send4, recv4, j).start()
    rcv4[head] = mine

    both_s[...] = jnp.zeros((ROWS, 2 * CH), F32)
    square_s[...] = jnp.zeros((ROWS, 128), F32)

    def use_chunk(j):
        cols = pl.ds(pl.multiple_of(j * CH, CH), CH)
        x = rcv4[j].astype(F32)
        square_s[...] += jnp.broadcast_to(jnp.sum(x * x, axis=1, keepdims=True), (ROWS, 128))
        both_s[...] += dot((x * gain_s[:, cols]).astype(BF16), gu_w[:, cols], NT)

    def forward(k, j):
        return pltpu.make_async_remote_copy(
            src_ref=rcv4.at[j],
            dst_ref=rcv4.at[j],
            send_sem=send_f.at[k],
            recv_sem=recv4.at[j],
            device_id=(me, sibling),
            device_id_type=MESH,
        )

    use_chunk(head)
    head_arrival(msg4, None, rcv4, send4, recv4, sibling).wait_recv()
    use_chunk(sibling)
    for k in range(3):
        j = 2 * far[k] + core
        head_arrival(msg4, None, rcv4, send4, recv4, j).wait_recv()
        forward(k, j).start()
        use_chunk(j)
    for k in range(3):
        j = 2 * far[k] + 1 - core
        forward(k, j).wait_recv()
        use_chunk(j)
    both = both_s[...]
    square = square_s[:, 0:1]
    scale = lax.rsqrt(square * (1.0 / D) + 1e-05)
    g = jnp.minimum(both[:, 0:CH] * scale, 7.0)
    u = jnp.clip(both[:, CH : 2 * CH] * scale, -7.0, 7.0)
    active = ((u + 1.0) * g * jax.nn.sigmoid(1.702 * g)).astype(BF16)

    def product(j):
        return dot(active, dn_w[:, pl.ds(pl.multiple_of(j * CH, CH), CH)], NN)

    def pair_copy(c):
        return pltpu.make_async_remote_copy(
            src_ref=msg_p.at[c],
            dst_ref=rcv_p.at[c],
            send_sem=send_p.at[c],
            recv_sem=recv_p.at[c],
            device_id=(me, sibling),
            device_id_type=MESH,
        )

    def chip_copy(c, slot):
        return pltpu.make_async_remote_copy(
            src_ref=msg5.at[c],
            dst_ref=rcv5.at[slot],
            send_sem=send5.at[c],
            recv_sem=recv5.at[slot],
            device_id=(me, 2 * c + core),
            device_id_type=MESH,
        )

    turns = [far[2], far[0], far[1], chip]
    for c in turns:
        msg_p[c] = product(2 * c + 1 - core).astype(BF16)
        pair_copy(c).start()
    for k, c in enumerate(turns):
        own = product(2 * c + core)
        pair_copy(c).wait_recv()
        both_cores = (own + rcv_p[c].astype(F32)).astype(BF16)
        if k < 3:
            msg5[c] = both_cores
            chip_copy(c, chip).start()
        else:
            rcv5[chip] = both_cores
    for c in far:
        chip_copy(c, c).wait_recv()
    summed = jnp.sum(rcv5[...].astype(F32), axis=0).astype(BF16)
    summed_rows = jnp.concatenate([summed[:, 128 * c : 128 * c + 128] for c in range(3)], axis=0)
    msg6[...] = dot(gather, summed_rows, NN).astype(BF16).reshape(N_SEQ, 16, 128)
    others(N_SEQ, me, lambda o: seq_copy(msg6, rcv6, send6, recv6, o).start())
    rcv6[me] = msg6[me]
    others(N_SEQ, me, lambda o: seq_copy(msg3, rcv3, send3, recv3, o).wait_send())
    for j in gather_to:
        head_copy(msg4, None, rcv4, send4, recv4, j).wait_send()
    for k in range(3):
        forward(k, 2 * far[k] + core).wait_send()
    for k, c in enumerate(turns):
        pair_copy(c).wait_send()
        if k < 3:
            chip_copy(c, chip).wait_send()
    others(N_SEQ, me, lambda s: seq_arrival(msg6, rcv6, send6, recv6, s).wait_recv())
    back = rcv6[...].reshape(512, 128)
    added = dot(give_hi, back, NN) + dot(give_lo, back, NN)
    result = hidden_rows.astype(F32) + added
    result = jnp.concatenate([result[16 * c : 16 * c + 16] for c in range(3)], axis=1).astype(BF16)
    msg7[...] = result
    others(N_HEAD, head, lambda o: head_copy(msg7, None, rcv7, send7, recv7, o).start())
    rcv7[head] = result
    others(N_SEQ, me, lambda o: seq_copy(msg6, rcv6, send6, recv6, o).wait_send())
    others(N_HEAD, head, lambda s: head_arrival(msg7, None, rcv7, send7, recv7, s).wait_recv())
    for i in range(3):
        for j in range(N_HEAD):
            out_ref[i, :, j * CH : j * CH + CH] = rcv7[j, 4 * i : 4 * i + 4, :]

    others(N_HEAD, head, lambda o: head_copy(msg7, None, rcv7, send7, recv7, o).wait_send())


def on_device(
    new_query,
    fresh_key_value,
    prompt_cache,
    decoded_tail_cache,
    sinks,
    prompt_group,
    prompt_lens,
    tail_lens,
    o_weight,
    resid,
    norm_gain,
    expert_ids,
    route_weights,
    gate_up,
    down_weight,
):
    r = jnp.arange(REQ, dtype=jnp.int32)
    mine, other = prompt_group[:, None], prompt_group[None, :]
    ahead = (other < mine) | ((other == mine) & (r[None, :] < r[:, None]))
    rank = jnp.sum(ahead.astype(jnp.int32), axis=1)
    order = jnp.sum(jnp.where(rank[None, :] == r[:, None], r[None, :], 0), axis=1)
    freq = np.exp(np.arange(32) * (-2.0 * math.log(150000.0) / 64))
    freq = np.tile(freq.astype(np.float32), 4)
    step_angle = (np.arange(16) % 4)[:, None] * freq[None, :].astype(np.float64)
    tables = np.zeros((40, 128), np.float32)
    tables[0] = freq
    tables[8:24] = np.cos(step_angle)
    tables[24:40] = np.sin(step_angle)
    fresh = fresh_key_value.transpose(0, 2, 1, 3).reshape(3, 4, 128)
    ids = expert_ids.transpose(1, 2, 0)
    q = new_query.reshape(REQ, 4, 4, 128).transpose(0, 2, 1, 3).reshape(REQ, 16, 128)
    prompt = prompt_cache.transpose(0, 2, 1, 3).reshape(GROUPS, PBLOCK, 128)
    tail = decoded_tail_cache.transpose(0, 2, 1, 3).reshape(REQ, TBLOCK, 128)
    ow = o_weight.T
    gu = gate_up.transpose(0, 2, 3, 1).reshape(2, FFL, D)
    dn = down_weight.reshape(FFL, D)

    smem = pl.BlockSpec(memory_space=pltpu.SMEM)
    vmem = pl.BlockSpec(memory_space=pltpu.VMEM)
    hbm = pl.BlockSpec(memory_space=pl.ANY)
    seq_sem = pltpu.SemaphoreType.DMA((N_SEQ,))
    head_sem = pltpu.SemaphoreType.DMA((N_HEAD,))
    chip_sem = pltpu.SemaphoreType.DMA((4,))
    out = pl.pallas_call(
        layer_kernel,
        name="layer",
        out_shape=jax.ShapeDtypeStruct((3, 4, 3072), BF16),
        in_specs=[smem] * 6 + [vmem] * 6 + [hbm] * 6,
        out_specs=vmem,
        scratch_shapes=[
            pltpu.VMEM((REQ, 16, 128), BF16),
            pltpu.VMEM((GROUPS, PBLOCK, 128), BF16),
            pltpu.VMEM((REQ, TBLOCK, 128), BF16),
            pltpu.VMEM((3072, 512), BF16),
            pltpu.VMEM((2 * CH, D), BF16),
            pltpu.VMEM((CH, D), BF16),
            pltpu.VMEM((CH, 3072), BF16),
            pltpu.VMEM((2 * CH, 3072), BF16),
            pltpu.VMEM((1, 3072), F32),
            pltpu.VMEM((REQ, 128), F32),
            pltpu.VMEM((REQ, 128), F32),
            pltpu.VMEM((16, 128), F32),
            pltpu.VMEM((16, 128), F32),
            pltpu.VMEM((16, 3072), F32),
            pltpu.VMEM((ROWS, 2 * CH), F32),
            pltpu.VMEM((ROWS, 128), F32),
            pltpu.VMEM((REQ, 32, 128), BF16),
            pltpu.VMEM((MEMBERS * 32, PBLOCK + 128), F32),
            pltpu.VMEM((MEMBERS * 32, PBLOCK + 128), F32),
            pltpu.VMEM((MEMBERS * 32, 128), F32),
            pltpu.VMEM((MEMBERS * 32, 128), F32),
            pltpu.VMEM((REQ, 16, 128), BF16),
            pltpu.VMEM((REQ, 16, 128), F32),
            pltpu.VMEM((N_SEQ, 56, 128), BF16),
            pltpu.VMEM((N_SEQ + 1, 56, 128), BF16),
            pltpu.VMEM((N_HEAD, 16, CH), BF16),
            pltpu.VMEM((N_HEAD, 16, CH), BF16),
            pltpu.VMEM((N_SEQ, 16, 128), BF16),
            pltpu.VMEM((N_SEQ, 16, 128), BF16),
            pltpu.VMEM((ROWS, CH), BF16),
            pltpu.VMEM((N_HEAD, ROWS, CH), BF16),
            pltpu.VMEM((4, ROWS, CH), BF16),
            pltpu.VMEM((4, ROWS, CH), BF16),
            pltpu.VMEM((4, ROWS, CH), BF16),
            pltpu.VMEM((4, ROWS, CH), BF16),
            pltpu.VMEM((N_SEQ, 16, 128), BF16),
            pltpu.VMEM((N_SEQ, 16, 128), BF16),
            pltpu.VMEM((16, CH), BF16),
            pltpu.VMEM((N_HEAD, 16, CH), BF16),
            pltpu.SemaphoreType.DMA((6,)),
            pltpu.SemaphoreType.DMA((GROUPS,)),
            seq_sem,
            seq_sem,
            head_sem,
            head_sem,
            seq_sem,
            seq_sem,
            head_sem,
            head_sem,
            chip_sem,
            chip_sem,
            chip_sem,
            chip_sem,
            chip_sem,
            seq_sem,
            seq_sem,
            head_sem,
            head_sem,
        ],
        compiler_params=pltpu.CompilerParams(
            collective_id=0, has_side_effects=True, vmem_limit_bytes=56 * 1024 * 1024
        ),
    )(
        order,
        rank,
        prompt_group,
        tail_lens,
        prompt_lens,
        sinks,
        jnp.asarray(tables),
        fresh,
        ids,
        route_weights,
        resid,
        norm_gain,
        q,
        prompt,
        tail,
        ow,
        gu,
        dn,
    )
    return out[:, :, :D]


def solution(mesh):
    return jax.shard_map(
        on_device,
        mesh=mesh,
        in_specs=(
            P(None, None, "head"),
            P("seq", None, "head", None),
            P(None, "seq", "head", None),
            P(None, "seq", "head", None),
            P("head"),
            P(),
            P(),
            P(),
            P("head", None),
            P("seq", None, None),
            P(),
            P(),
            P("seq", None, None),
            P("seq", None, None, "head"),
            P("seq", "head", None),
        ),
        out_specs=P("seq", None, None),
        check_vma=False,
    )
```

```python
import math

import jax
import jax.numpy as jnp
import numpy as np
from jax import lax
from jax.experimental import pallas as pl
from jax.experimental.pallas import tpu as pltpu
from jax.sharding import PartitionSpec as P

MESH = pl.DeviceIdType.MESH
LOW = -1e30
FLOOR = -1e29
F32 = jnp.float32
BF16 = jnp.bfloat16

N_SEQ = 32
N_HEAD = 8
REQ = 96
GROUPS = 8
MEMBERS = 12
PBLOCK = 1024
TBLOCK = 32
D = 2880
CH = 384
LASTC = 192
FFL = 360
ROWS = 96
HALF_PI = (1.5703125, 4.8351287841796875e-4, 3.1391647865048e-7)
NT = (((1,), (1,)), ((), ()))
NN = (((1,), (0,)), ((), ()))
TN = (((0,), (0,)), ((), ()))


SEQ_ORDER = sorted(
    ((dy, dz) for dy in range(4) for dz in range(8) if dy or dz),
    key=lambda o: (-min(o[0], 4 - o[0]) - min(o[1], 8 - o[1]), (o[0] * 3 + o[1] * 5) % 8),
)


def dot(a, b, dims):
    return lax.dot_general(a, b, dims, preferred_element_type=F32)


def iota(shape, axis):
    return lax.broadcasted_iota(jnp.int32, shape, axis)


def turned(x, cosine, sine, lane):
    ahead = pltpu.roll(x, 96, 1)
    behind = pltpu.roll(x, 32, 1)
    partner = jnp.where((lane & 63) < 32, -ahead, behind)
    return x * cosine + partner * sine


def cos_sin(angle):
    k = jnp.floor(angle * (2.0 / math.pi) + 0.5)
    r = angle - k * HALF_PI[0]
    r = r - k * HALF_PI[1]
    r = r - k * HALF_PI[2]
    r2 = r * r
    s = r + r * r2 * (-1.0 / 6 + r2 * (1.0 / 120 + r2 * (-1.0 / 5040 + r2 * (1.0 / 362880))))
    c = 1.0 + r2 * (-0.5 + r2 * (1.0 / 24 + r2 * (-1.0 / 720 + r2 * (1.0 / 40320))))
    quarter = k - 4.0 * jnp.floor(k * 0.25)
    odd = (quarter == 1.0) | (quarter == 3.0)
    cosine = jnp.where(odd, s, c)
    sine = jnp.where(odd, c, s)
    cosine = jnp.where((quarter == 1.0) | (quarter == 2.0), -cosine, cosine)
    sine = jnp.where(quarter >= 2.0, -sine, sine)
    return cosine, sine


def tiles_of(out, peak, lane):
    first, second = out[:16], out[16:]
    values = jnp.where(lane < 64, pltpu.roll(first, 64, 1), second).astype(BF16)
    hi0 = first.astype(BF16).astype(F32)
    hi1 = second.astype(BF16).astype(F32)
    lo0 = first - hi0
    lo1 = second - hi1
    stats = jnp.where(
        lane < 4,
        jnp.where(lane == 0, peak[:16], jnp.where(lane == 1, hi0, jnp.where(lane == 2, lo0, 0.0))),
        jnp.where(
            lane == 4, peak[16:], jnp.where(lane == 5, hi1, jnp.where(lane == 6, lo1, 0.0))
        ),
    )
    return values, jnp.where(lane < 8, stats, 0.0)


def layer_kernel(
    order,
    rank,
    prompt_group,
    tail_lens,
    prompt_lens,
    sinks,
    tables,
    fresh,
    ids,
    routes,
    resid,
    gain,
    q_hbm,
    prompt_hbm,
    tail_hbm,
    ow_hbm,
    gu_hbm,
    dn_hbm,
    out_ref,
    q_v,
    prompt_v,
    tail_v,
    ow_v,
    gu_v,
    dn_v,
    dn_w,
    gu_w,
    gain_s,
    cos_s,
    sin_s,
    small_s,
    route_s,
    resid_s,
    both_s,
    square_s,
    q_all,
    even_s,
    odd_s,
    even_top,
    odd_top,
    acc_s,
    stat_s,
    msg1,
    rcv1,
    msg2,
    rcv2,
    msg3,
    rcv3,
    msg4,
    rcv4,
    msg_p,
    rcv_p,
    msg5,
    rcv5,
    msg6,
    rcv6,
    msg7,
    rcv7,
    load_sem,
    prompt_sem,
    send1,
    recv1,
    send2,
    recv2,
    send3,
    recv3,
    send4,
    recv4,
    send_f,
    send_p,
    recv_p,
    send5,
    recv5,
    send6,
    recv6,
    send7,
    recv7,
):
    me = lax.axis_index("seq")
    head = lax.axis_index("head")
    barrier = pltpu.get_barrier_semaphore()

    def greet_seq(d, carry):
        pl.semaphore_signal(
            barrier, inc=1, device_id=(lax.rem(me + d, N_SEQ), head), device_id_type=MESH
        )
        return carry

    def greet_head(d, carry):
        pl.semaphore_signal(
            barrier, inc=1, device_id=(me, lax.rem(head + d, N_HEAD)), device_id_type=MESH
        )
        return carry

    load_q = pltpu.make_async_copy(q_hbm, q_v, load_sem.at[0])
    load_tail = pltpu.make_async_copy(tail_hbm, tail_v, load_sem.at[1])
    load_ow = pltpu.make_async_copy(ow_hbm, ow_v.at[pl.ds(0, D)], load_sem.at[2])
    load_gate = pltpu.make_async_copy(gu_hbm.at[0], gu_v.at[pl.ds(0, FFL)], load_sem.at[3])
    load_up = pltpu.make_async_copy(gu_hbm.at[1], gu_v.at[pl.ds(CH, FFL)], load_sem.at[5])
    load_dn = pltpu.make_async_copy(dn_hbm, dn_v.at[pl.ds(0, FFL)], load_sem.at[4])
    load_q.start()
    load_tail.start()

    def load_prompt(g):
        return pltpu.make_async_copy(prompt_hbm.at[g], prompt_v.at[g], prompt_sem.at[g])

    for g in range(GROUPS):
        load_prompt(g).start()
    load_ow.start()
    load_gate.start()
    load_up.start()
    load_dn.start()
    for d in range(1, N_SEQ):
        greet_seq(d, 0)
    for d in range(1, N_HEAD):
        greet_head(d, 0)

    lane = iota((16, 128), 1)
    row = iota((16, 128), 0)

    freq = tables[0:1, :]
    ct = tables[8:24, :]
    st = tables[24:40, :]

    def place(r):
        return (prompt_lens[prompt_group[r]] + tail_lens[r]).astype(F32)

    def put_angle(i, carry):
        cos_s[pl.ds(i, 1), :] = freq * place(order[i])
        return carry

    lax.fori_loop(0, REQ, put_angle, 0, unroll=8)
    cosine, sine = cos_sin(cos_s[...])
    cos_s[...] = cosine
    sin_s[...] = sine

    load_q.wait()

    def rotate_one(i, carry):
        r = order[i]
        x = q_v[r].astype(F32)
        c0 = cos_s[pl.ds(i, 1), :]
        s0 = sin_s[pl.ds(i, 1), :]
        y = turned(x, c0 * ct - s0 * st, s0 * ct + c0 * st, lane)
        y = y.astype(BF16).astype(F32) * 0.125
        q_all[i, 0:16, :] = jnp.where(lane < 64, y, 0.0).astype(BF16)
        q_all[i, 16:32, :] = jnp.where(
            lane < 64, pltpu.roll(y, 64, 1), 0.0
        ).astype(BF16)
        return carry

    lax.fori_loop(0, REQ, rotate_one, 0, unroll=8)
    load_tail.wait()

    key_col = iota((1, PBLOCK), 1) + me * PBLOCK
    col128 = iota((1, 128), 1)
    upper = (iota((1, 128), 1) >= 64).astype(F32).astype(BF16)
    lower = (iota((1, 128), 1) < 64).astype(F32).astype(BF16)
    same_req = (iota((128, 128), 0) >> 5) == (iota((128, 128), 1) >> 5)

    def tails(g):
        members = [order[g * MEMBERS + i] for i in range(MEMBERS)]
        return [
            jnp.concatenate([tail_v[r] for r in members[4 * b : 4 * b + 4]], axis=0)
            for b in range(3)
        ], members

    def scores(g, buf, tops):
        kv = prompt_v[g]
        bias = jnp.where(key_col < prompt_lens[g], 0.0, LOW)
        q = q_all[pl.ds(g * MEMBERS, MEMBERS)].reshape(MEMBERS * 32, 128)
        keys, members = tails(g)
        for b in range(3):
            rows = slice(128 * b, 128 * b + 128)
            high = None
            for h in range(4):
                cols = slice(256 * h, 256 * h + 256)
                part = dot(q[rows], kv[cols], NT) + bias[:, cols]
                buf[rows, cols] = part
                part = jnp.maximum(part[:, :128], part[:, 128:])
                high = part if high is None else jnp.maximum(high, part)
            limit = jnp.zeros((1, 128), jnp.int32)
            for i in range(4):
                limit = jnp.where((col128 >> 5) == i, tail_lens[members[4 * b + i]], limit)
            seen = same_req & (((col128 & 31) + me * TBLOCK) < limit)
            part = jnp.where(seen, dot(q[rows], keys[b], NT), LOW)
            buf[rows, PBLOCK : PBLOCK + 128] = part
            top = jnp.max(jnp.maximum(high, part), axis=1, keepdims=True)
            top = jnp.maximum(top, FLOOR).astype(BF16).astype(F32)
            tops[rows, :] = jnp.broadcast_to(top, (128, 128))

    def weigh(g, buf, tops):
        first = g * MEMBERS
        kv = prompt_v[g]
        vx = kv * upper + lower
        keys, members = tails(g)
        peaks = tops[...]
        w = jnp.concatenate(
            [
                jnp.exp(buf[:, 128 * h : 128 * h + 128] - peaks).astype(BF16)
                for h in range(PBLOCK // 128)
            ],
            axis=1,
        )
        w2 = jnp.exp(buf[:, PBLOCK : PBLOCK + 128] - peaks).astype(BF16)
        whole = dot(w, vx, NN)
        for b in range(3):
            rows = slice(128 * b, 128 * b + 128)
            peak = peaks[rows]
            o = whole[rows] + dot(w2[rows], keys[b] * upper + lower, NN)
            for i in range(4):
                values, stats = tiles_of(o[32 * i : 32 * i + 32], peak[32 * i : 32 * i + 32], lane)
                acc_s[first + 4 * b + i] = values
                stat_s[first + 4 * b + i] = stats

    for g in range(GROUPS):
        load_prompt(g).wait()
    scores(0, even_s, even_top)

    def two_groups(k, carry):
        g = 2 * k
        scores(g + 1, odd_s, odd_top)
        weigh(g, even_s, even_top)
        scores(g + 2, even_s, even_top)
        weigh(g + 1, odd_s, odd_top)
        return carry

    lax.fori_loop(0, GROUPS // 2 - 1, two_groups, 0)
    scores(GROUPS - 1, odd_s, odd_top)
    weigh(GROUPS - 2, even_s, even_top)
    weigh(GROUPS - 1, odd_s, odd_top)

    rcv3[...] = jnp.zeros((N_SEQ, 16, 128), BF16)
    rcv6[...] = jnp.zeros((N_SEQ, 16, 128), BF16)
    pl.semaphore_wait(barrier, N_SEQ - 1 + N_HEAD - 1)

    def pack(dst, slot, o):
        total = jnp.zeros((16, 128), F32)
        for i in range(3):
            k = rank[3 * o + i]
            dst[slot, 16 * i : 16 * i + 16, :] = acc_s[k]
            piece = stat_s[k]
            total = total + (piece if i == 0 else pltpu.roll(piece, 8 * i, 1))
        dst[slot, 48:56, :] = (total[:8] + pltpu.roll(total[8:], 64, 1)).astype(BF16)

    def seq_copy(msg, rcv, send, recv, to):
        rows = 56 if msg is msg1 else 10
        return pltpu.make_async_remote_copy(
            src_ref=msg.at[to, pl.ds(0, rows)],
            dst_ref=rcv.at[me, pl.ds(0, rows)],
            send_sem=send.at[to],
            recv_sem=recv.at[me],
            device_id=(to, head),
            device_id_type=MESH,
        )

    def seq_arrival(msg, rcv, send, recv, source):
        rows = 56 if msg is msg1 else 10
        return pltpu.make_async_remote_copy(
            src_ref=msg.at[source, pl.ds(0, rows)],
            dst_ref=rcv.at[source, pl.ds(0, rows)],
            send_sem=send.at[source],
            recv_sem=recv.at[source],
            device_id=(source, head),
            device_id_type=MESH,
        )

    def head_copy(msg, slot, rcv, send, recv, to):
        return pltpu.make_async_remote_copy(
            src_ref=msg if slot is None else msg.at[slot],
            dst_ref=rcv.at[head],
            send_sem=send.at[to],
            recv_sem=recv.at[head],
            device_id=(me, to),
            device_id_type=MESH,
        )

    def head_arrival(msg, slot, rcv, send, recv, source):
        return pltpu.make_async_remote_copy(
            src_ref=msg if slot is None else msg.at[slot],
            dst_ref=rcv.at[source],
            send_sem=send.at[source],
            recv_sem=recv.at[source],
            device_id=(me, source),
            device_id_type=MESH,
        )

    def others(count, mine, body):
        if count == N_HEAD:
            for j in head_order:
                body(j)
        else:
            for dy, dz in SEQ_ORDER:
                body(lax.rem(me // 8 + dy, 4) * 8 + lax.rem(lax.rem(me, 8) + dz, 8))

    core = lax.rem(head, 2)
    chip = head // 2
    near = chip + 1 - 2 * lax.rem(chip, 2)
    sibling = 2 * chip + 1 - core
    far = [near, 3 - chip, lax.rem(chip + 2, 4)]
    head_order = []
    for c in (far[2], far[0], far[1]):
        head_order += [2 * c + core, 2 * c + 1 - core]
    head_order.append(sibling)

    def send_partials(o):
        pack(msg1, o, o)
        seq_copy(msg1, rcv1, send1, recv1, o).start()

    others(N_SEQ, me, send_partials)
    pack(rcv1, me, me)

    angle = jnp.zeros((16, 128), F32)
    for i in range(3):
        angle = jnp.where((row >> 2) == i, freq * place(me * 3 + i), angle)
        small_s[4 * i : 4 * i + 4, :] = fresh[i].astype(F32)
    base_c, base_s = cos_sin(angle)
    small_s[12:16, :] = jnp.zeros((4, 128), F32)
    kv_new = small_s[...]
    key_new = turned(kv_new, base_c * ct - base_s * st, base_s * ct + base_c * st, lane)
    kn = jnp.where(lane < 64, key_new, kv_new).astype(BF16)
    vn = jnp.where(lane < 64, 1.0, kv_new).astype(BF16)
    fresh_stats = jnp.zeros((16, 128), F32)
    srow = iota((32, 16), 0)
    scol = iota((32, 16), 1)
    for i in range(3):
        k = rank[3 * me + i]
        q = q_all[k]
        seen = ((scol >> 2) == i) & ((scol & 3) <= (srow & 3))
        s = jnp.where(seen, dot(q, kn, NT), LOW)
        peak = jnp.max(s, axis=1, keepdims=True).astype(BF16).astype(F32)
        w = jnp.exp(s - peak).astype(BF16)
        values, stats = tiles_of(dot(w, vn, NN), peak, lane)
        rcv1[N_SEQ, 16 * i : 16 * i + 16, :] = values
        fresh_stats = fresh_stats + (stats if i == 0 else pltpu.roll(stats, 8 * i, 1))
    folded = fresh_stats[:8] + pltpu.roll(fresh_stats[8:], 64, 1)
    rcv1[N_SEQ, 48:56, :] = folded.astype(BF16)

    sink = jnp.zeros((16, 128), F32)
    for j in range(8):
        here = ((row >> 2) == (j >> 1)) & ((lane >> 6) == (j & 1))
        sink = jnp.where(here, sinks[j], sink)

    wide_lane = iota((16, 512), 1)
    expert = wide_lane >> 4
    place = wide_lane & 15
    pick = (place >= 3).astype(jnp.int32) + (place >= 6).astype(jnp.int32)
    tile = place - 3 * pick
    own = (iota((REQ, 384), 0) == me * 3 + (iota((REQ, 384), 1) >> 7)).astype(F32).astype(BF16)
    flat_ids = jnp.concatenate([ids[t] for t in range(4)], axis=0).astype(F32).astype(BF16)
    own_ids = dot(flat_ids, own, NN).astype(BF16)
    xr = iota((64, 16), 0)
    xc = iota((64, 16), 1)
    names = jnp.full((64, 128), -1.0, F32) * ((iota((64, 128), 0) & 15) >= 12).astype(F32)
    for i in range(3):
        take = (xc == (xr & 3) * 4 + (xr >> 4)) & (((xr & 15) >> 2) == i)
        names = names + dot(
            take.astype(F32).astype(BF16), own_ids[:, 128 * i : 128 * i + 128], NN
        )
    names = jnp.concatenate([names] * 4, axis=1)
    route_s[...] = jnp.zeros((16, 128), F32)
    for i in range(3):
        route_s[4 * i : 4 * i + 4, 0:4] = routes[i]
    named = jnp.zeros((16, 512), F32)
    share = jnp.zeros((16, 512), F32)
    for k in range(4):
        hit = names[16 * k : 16 * k + 16] == expert.astype(F32)
        named = named + jnp.where(hit, 1.0, 0.0)
        share = share + jnp.where(hit, route_s[:, k : k + 1], 0.0)
    below = (iota((16, 16), 1) < iota((16, 16), 0)).astype(F32).astype(BF16)
    earlier = dot(below, named.astype(BF16), NN)
    chosen = (named > 0.5) & (earlier == pick.astype(F32)) & (place < 9)
    chosen_tile = [chosen & (tile == c) for c in range(3)]
    select = jnp.concatenate([jnp.where(m, 1.0, 0.0) for m in chosen_tile], axis=0)
    select = select.T.astype(BF16)
    give = jnp.concatenate([jnp.where(m, share, 0.0) for m in chosen_tile], axis=0)
    give_hi = give.astype(BF16)
    give_lo = (give - give_hi.astype(F32)).astype(BF16)

    trow = iota((288, 512), 0)
    tcol = iota((288, 512), 1)
    ttile = (trow >= 96).astype(jnp.int32) + (trow >= 192).astype(jnp.int32)
    trest = trow - 96 * ttile
    spread = (
        ((trest & 31) == (tcol >> 4)) & ((tcol & 15) == 3 * (trest >> 5) + ttile)
    ).astype(F32).astype(BF16)

    ucol = iota((512, 288), 1)
    urow = iota((512, 288), 0)
    utile = (ucol >= 96).astype(jnp.int32) + (ucol >= 192).astype(jnp.int32)
    urest = ucol - 96 * utile
    gather = (
        ((urest & 31) == (urow >> 4)) & ((urow & 15) == 3 * (urest >> 5) + utile)
    ).astype(F32).astype(BF16)
    resid_s[...] = jnp.zeros((16, 3072), F32)
    for i in range(3):
        resid_s[4 * i : 4 * i + 4, 0:D] = resid[i].astype(F32)

    load_ow.wait()
    ow_v[pl.ds(D, 3072 - D), :] = jnp.zeros((3072 - D, 512), BF16)
    load_gate.wait()
    load_up.wait()
    load_dn.wait()
    gu_v[FFL:CH, :] = jnp.zeros((CH - FFL, D), BF16)
    gu_v[CH + FFL : 2 * CH, :] = jnp.zeros((CH - FFL, D), BF16)
    dn_v[FFL:CH, :] = jnp.zeros((CH - FFL, D), BF16)
    dn_w[:, 2816:3072] = jnp.zeros((CH, 256), BF16)
    dn_w[:, 0:D] = dn_v[...]
    gu_w[:, 2816:3072] = jnp.zeros((2 * CH, 256), BF16)
    gu_w[:, 0:D] = gu_v[...]
    gain_s[:, 2816:3072] = jnp.zeros((1, 256), F32)
    gain_s[:, 0:D] = gain[...].reshape(1, D)

    others(N_SEQ, me, lambda s: seq_arrival(msg1, rcv1, send1, recv1, s).wait_recv())

    stat_rows = rcv1[:, 48:56, :].reshape((N_SEQ + 1) * 8, 128)
    er = iota((128, 384), 0)
    ec = iota((128, 384), 1)
    attended = []
    for i in range(3):
        for half in range(2):
            spot = 64 * half + 8 * i + 4 * ((ec & 127) >> 6) + (ec >> 7)
            expand = (er == spot).astype(F32).astype(BF16)
            wide = dot(stat_rows, expand, NN)
            peaks = wide[:, 0:128].reshape(N_SEQ + 1, 8, 128)
            totals = (wide[:, 128:256] + wide[:, 256:384]).reshape(N_SEQ + 1, 8, 128)
            sunk = sink[8 * half : 8 * half + 8]
            top = jnp.maximum(jnp.max(peaks, axis=0), sunk)
            factor = jnp.exp(peaks - top[None])
            start = 16 * i + 8 * half
            values = rcv1[:, start : start + 8, :].astype(F32)
            num = jnp.sum(values * factor, axis=0)
            den = jnp.sum(totals * factor, axis=0) + jnp.exp(sunk - top)
            attended.append(num / den)
    att = jnp.concatenate(attended, axis=0).astype(BF16)
    rr = iota((64, 48), 0)
    rc = iota((64, 48), 1)
    want = ((rr & 15) >> 2) * 16 + (rr >> 4) * 4 + (rr & 3)
    regroup = (rc == want).astype(F32).astype(BF16)
    mixed = dot(regroup, att, NN).astype(BF16)
    flat = jnp.concatenate([mixed[16 * p : 16 * p + 16] for p in range(4)], axis=1)

    def project(j):
        rows = ow_v[pl.ds(pl.multiple_of(j * CH, CH), CH), :]
        return dot(flat, rows, NT).astype(BF16)

    def send_projection(j):
        msg2[j] = project(j)
        head_copy(msg2, j, rcv2, send2, recv2, j).start()

    others(N_HEAD, head, send_projection)
    rcv2[head] = project(head)
    others(N_HEAD, head, lambda s: head_arrival(msg2, s, rcv2, send2, recv2, s).wait_recv())
    total = resid_s[:, pl.ds(pl.multiple_of(head * CH, CH), CH)]
    total = total + jnp.sum(rcv2[...].astype(F32), axis=0)
    hidden = total.astype(BF16)
    hidden_rows = jnp.concatenate([hidden[:, 128 * c : 128 * c + 128] for c in range(3)], axis=0)

    msg3[...] = dot(select, hidden_rows, NN).astype(BF16).reshape(N_SEQ, 16, 128)
    others(N_SEQ, me, lambda o: seq_copy(msg3, rcv3, send3, recv3, o).start())
    rcv3[me] = msg3[me]
    others(N_SEQ, me, lambda o: seq_copy(msg1, rcv1, send1, recv1, o).wait_send())
    others(N_HEAD, head, lambda o: head_copy(msg2, o, rcv2, send2, recv2, o).wait_send())
    others(N_SEQ, me, lambda s: seq_arrival(msg3, rcv3, send3, recv3, s).wait_recv())
    got = dot(spread, rcv3[...].reshape(512, 128), NN).astype(BF16)
    mine = jnp.concatenate([got[96 * c : 96 * c + 96] for c in range(3)], axis=1)
    msg4[...] = mine
    gather_to = [2 * far[2] + core, 2 * far[0] + core, 2 * far[1] + core, sibling]
    for j in gather_to:
        head_copy(msg4, None, rcv4, send4, recv4, j).start()
    rcv4[head] = mine

    both_s[...] = jnp.zeros((ROWS, 2 * CH), F32)
    square_s[...] = jnp.zeros((ROWS, 128), F32)

    def use_chunk(j):
        cols = pl.ds(pl.multiple_of(j * CH, CH), CH)
        x = rcv4[j].astype(F32)
        square_s[...] += jnp.broadcast_to(jnp.sum(x * x, axis=1, keepdims=True), (ROWS, 128))
        both_s[...] += dot((x * gain_s[:, cols]).astype(BF16), gu_w[:, cols], NT)

    def forward(k, j):
        return pltpu.make_async_remote_copy(
            src_ref=rcv4.at[j],
            dst_ref=rcv4.at[j],
            send_sem=send_f.at[k],
            recv_sem=recv4.at[j],
            device_id=(me, sibling),
            device_id_type=MESH,
        )

    use_chunk(head)
    head_arrival(msg4, None, rcv4, send4, recv4, sibling).wait_recv()
    use_chunk(sibling)
    for k in range(3):
        j = 2 * far[k] + core
        head_arrival(msg4, None, rcv4, send4, recv4, j).wait_recv()
        forward(k, j).start()
        use_chunk(j)
    for k in range(3):
        j = 2 * far[k] + 1 - core
        forward(k, j).wait_recv()
        use_chunk(j)
    both = both_s[...]
    square = square_s[:, 0:1]
    scale = lax.rsqrt(square * (1.0 / D) + 1e-05)
    g = jnp.minimum(both[:, 0:CH] * scale, 7.0)
    u = jnp.clip(both[:, CH : 2 * CH] * scale, -7.0, 7.0)
    active = ((u + 1.0) * g * jax.nn.sigmoid(1.702 * g)).astype(BF16)

    def product(j):
        return dot(active, dn_w[:, pl.ds(pl.multiple_of(j * CH, CH), CH)], NN)

    def pair_copy(c):
        return pltpu.make_async_remote_copy(
            src_ref=msg_p.at[c],
            dst_ref=rcv_p.at[c],
            send_sem=send_p.at[c],
            recv_sem=recv_p.at[c],
            device_id=(me, sibling),
            device_id_type=MESH,
        )

    def chip_copy(c, slot):
        return pltpu.make_async_remote_copy(
            src_ref=msg5.at[c],
            dst_ref=rcv5.at[slot],
            send_sem=send5.at[c],
            recv_sem=recv5.at[slot],
            device_id=(me, 2 * c + core),
            device_id_type=MESH,
        )

    turns = [far[2], far[0], far[1], chip]
    for c in turns:
        msg_p[c] = product(2 * c + 1 - core).astype(BF16)
        pair_copy(c).start()
    for k, c in enumerate(turns):
        own = product(2 * c + core)
        pair_copy(c).wait_recv()
        both_cores = (own + rcv_p[c].astype(F32)).astype(BF16)
        if k < 3:
            msg5[c] = both_cores
            chip_copy(c, chip).start()
        else:
            rcv5[chip] = both_cores
    for c in far:
        chip_copy(c, c).wait_recv()
    summed = jnp.sum(rcv5[...].astype(F32), axis=0).astype(BF16)
    summed_rows = jnp.concatenate([summed[:, 128 * c : 128 * c + 128] for c in range(3)], axis=0)
    msg6[...] = dot(gather, summed_rows, NN).astype(BF16).reshape(N_SEQ, 16, 128)
    others(N_SEQ, me, lambda o: seq_copy(msg6, rcv6, send6, recv6, o).start())
    rcv6[me] = msg6[me]
    others(N_SEQ, me, lambda o: seq_copy(msg3, rcv3, send3, recv3, o).wait_send())
    for j in gather_to:
        head_copy(msg4, None, rcv4, send4, recv4, j).wait_send()
    for k in range(3):
        forward(k, 2 * far[k] + core).wait_send()
    for k, c in enumerate(turns):
        pair_copy(c).wait_send()
        if k < 3:
            chip_copy(c, chip).wait_send()
    others(N_SEQ, me, lambda s: seq_arrival(msg6, rcv6, send6, recv6, s).wait_recv())
    back = rcv6[...].reshape(512, 128)
    added = dot(give_hi, back, NN) + dot(give_lo, back, NN)
    result = hidden_rows.astype(F32) + added
    result = jnp.concatenate([result[16 * c : 16 * c + 16] for c in range(3)], axis=1).astype(BF16)
    msg7[...] = result
    others(N_HEAD, head, lambda o: head_copy(msg7, None, rcv7, send7, recv7, o).start())
    rcv7[head] = result
    others(N_SEQ, me, lambda o: seq_copy(msg6, rcv6, send6, recv6, o).wait_send())
    others(N_HEAD, head, lambda s: head_arrival(msg7, None, rcv7, send7, recv7, s).wait_recv())
    for i in range(3):
        for j in range(N_HEAD):
            out_ref[i, :, j * CH : j * CH + CH] = rcv7[j, 4 * i : 4 * i + 4, :]

    others(N_HEAD, head, lambda o: head_copy(msg7, None, rcv7, send7, recv7, o).wait_send())


def on_device(
    new_query,
    fresh_key_value,
    prompt_cache,
    decoded_tail_cache,
    sinks,
    prompt_group,
    prompt_lens,
    tail_lens,
    o_weight,
    resid,
    norm_gain,
    expert_ids,
    route_weights,
    gate_up,
    down_weight,
):
    r = jnp.arange(REQ, dtype=jnp.int32)
    mine, other = prompt_group[:, None], prompt_group[None, :]
    ahead = (other < mine) | ((other == mine) & (r[None, :] < r[:, None]))
    rank = jnp.sum(ahead.astype(jnp.int32), axis=1)
    order = jnp.sum(jnp.where(rank[None, :] == r[:, None], r[None, :], 0), axis=1)
    freq = np.exp(np.arange(32) * (-2.0 * math.log(150000.0) / 64))
    freq = np.tile(freq.astype(np.float32), 4)
    step_angle = (np.arange(16) % 4)[:, None] * freq[None, :].astype(np.float64)
    tables = np.zeros((40, 128), np.float32)
    tables[0] = freq
    tables[8:24] = np.cos(step_angle)
    tables[24:40] = np.sin(step_angle)
    fresh = fresh_key_value.transpose(0, 2, 1, 3).reshape(3, 4, 128)
    ids = expert_ids.transpose(1, 2, 0)
    q = new_query.reshape(REQ, 4, 4, 128).transpose(0, 2, 1, 3).reshape(REQ, 16, 128)
    prompt = prompt_cache.transpose(0, 2, 1, 3).reshape(GROUPS, PBLOCK, 128)
    tail = decoded_tail_cache.transpose(0, 2, 1, 3).reshape(REQ, TBLOCK, 128)
    ow = o_weight.T
    gu = gate_up.transpose(0, 2, 3, 1).reshape(2, FFL, D)
    dn = down_weight.reshape(FFL, D)

    smem = pl.BlockSpec(memory_space=pltpu.SMEM)
    vmem = pl.BlockSpec(memory_space=pltpu.VMEM)
    hbm = pl.BlockSpec(memory_space=pl.ANY)
    seq_sem = pltpu.SemaphoreType.DMA((N_SEQ,))
    head_sem = pltpu.SemaphoreType.DMA((N_HEAD,))
    chip_sem = pltpu.SemaphoreType.DMA((4,))
    out = pl.pallas_call(
        layer_kernel,
        name="layer",
        out_shape=jax.ShapeDtypeStruct((3, 4, 3072), BF16),
        in_specs=[smem] * 6 + [vmem] * 6 + [hbm] * 6,
        out_specs=vmem,
        scratch_shapes=[
            pltpu.VMEM((REQ, 16, 128), BF16),
            pltpu.VMEM((GROUPS, PBLOCK, 128), BF16),
            pltpu.VMEM((REQ, TBLOCK, 128), BF16),
            pltpu.VMEM((3072, 512), BF16),
            pltpu.VMEM((2 * CH, D), BF16),
            pltpu.VMEM((CH, D), BF16),
            pltpu.VMEM((CH, 3072), BF16),
            pltpu.VMEM((2 * CH, 3072), BF16),
            pltpu.VMEM((1, 3072), F32),
            pltpu.VMEM((REQ, 128), F32),
            pltpu.VMEM((REQ, 128), F32),
            pltpu.VMEM((16, 128), F32),
            pltpu.VMEM((16, 128), F32),
            pltpu.VMEM((16, 3072), F32),
            pltpu.VMEM((ROWS, 2 * CH), F32),
            pltpu.VMEM((ROWS, 128), F32),
            pltpu.VMEM((REQ, 32, 128), BF16),
            pltpu.VMEM((MEMBERS * 32, PBLOCK + 128), F32),
            pltpu.VMEM((MEMBERS * 32, PBLOCK + 128), F32),
            pltpu.VMEM((MEMBERS * 32, 128), F32),
            pltpu.VMEM((MEMBERS * 32, 128), F32),
            pltpu.VMEM((REQ, 16, 128), BF16),
            pltpu.VMEM((REQ, 16, 128), F32),
            pltpu.VMEM((N_SEQ, 56, 128), BF16),
            pltpu.VMEM((N_SEQ + 1, 56, 128), BF16),
            pltpu.VMEM((N_HEAD, 16, CH), BF16),
            pltpu.VMEM((N_HEAD, 16, CH), BF16),
            pltpu.VMEM((N_SEQ, 16, 128), BF16),
            pltpu.VMEM((N_SEQ, 16, 128), BF16),
            pltpu.VMEM((ROWS, CH), BF16),
            pltpu.VMEM((N_HEAD, ROWS, CH), BF16),
            pltpu.VMEM((4, ROWS, CH), BF16),
            pltpu.VMEM((4, ROWS, CH), BF16),
            pltpu.VMEM((4, ROWS, CH), BF16),
            pltpu.VMEM((4, ROWS, CH), BF16),
            pltpu.VMEM((N_SEQ, 16, 128), BF16),
            pltpu.VMEM((N_SEQ, 16, 128), BF16),
            pltpu.VMEM((16, CH), BF16),
            pltpu.VMEM((N_HEAD, 16, CH), BF16),
            pltpu.SemaphoreType.DMA((6,)),
            pltpu.SemaphoreType.DMA((GROUPS,)),
            seq_sem,
            seq_sem,
            head_sem,
            head_sem,
            seq_sem,
            seq_sem,
            head_sem,
            head_sem,
            chip_sem,
            chip_sem,
            chip_sem,
            chip_sem,
            chip_sem,
            seq_sem,
            seq_sem,
            head_sem,
            head_sem,
        ],
        compiler_params=pltpu.CompilerParams(
            collective_id=0, has_side_effects=True, vmem_limit_bytes=56 * 1024 * 1024
        ),
    )(
        order,
        rank,
        prompt_group,
        tail_lens,
        prompt_lens,
        sinks,
        jnp.asarray(tables),
        fresh,
        ids,
        route_weights,
        resid,
        norm_gain,
        q,
        prompt,
        tail,
        ow,
        gu,
        dn,
    )
    return out[:, :, :D]


def solution(mesh):
    return jax.shard_map(
        on_device,
        mesh=mesh,
        in_specs=(
            P(None, None, "head"),
            P("seq", None, "head", None),
            P(None, "seq", "head", None),
            P(None, "seq", "head", None),
            P("head"),
            P(),
            P(),
            P(),
            P("head", None),
            P("seq", None, None),
            P(),
            P(),
            P("seq", None, None),
            P("seq", None, None, "head"),
            P("seq", "head", None),
        ),
        out_specs=P("seq", None, None),
        check_vma=False,
    )
```
